32 devices in a mesh: dp: 8 (over y, x, core), fsdp: 4 (over z).
Axes of the slice: x: 2, y: 2, z: 4, core: 2. Of those that a mesh axis runs over, the one named last changes fastest.
Arguments:
- rows_in: bfloat16 [256, 32, 1024], P(None, ('dp', 'fsdp')), may hold values from -6 to 6
- cotangent: bfloat16 [256, 32, 1024], P(None, ('dp', 'fsdp')), may hold values from -6 to 6
- lengths: int32 [64], replicated, may hold values from 65 to 191, as said below
- deal_order: int32 [64], replicated, may hold values from 0 to 63, as said below
- w_qkv: bfloat16 [1024, 3072], P(('dp', 'fsdp')), may hold values from -0.25 to 0.25
- b_query: bfloat16 [1024], P(('dp', 'fsdp')), may hold values from -3 to 3
- b_value: bfloat16 [1024], P(('dp', 'fsdp')), may hold values from -3 to 3
- w_out: bfloat16 [1024, 1024], P(('dp', 'fsdp')), may hold values from -0.5 to 0.5
- b_out: bfloat16 [1024], P(('dp', 'fsdp')), may hold values from -3 to 3
- gain_one: bfloat16 [1024], P(('dp', 'fsdp')), may hold values from 0.5 to 1.5
- shift_one: bfloat16 [1024], P(('dp', 'fsdp')), may hold values from -2 to 2
- w_up: bfloat16 [1024, 4096], P(('dp', 'fsdp')), may hold values from -0.1875 to 0.1875
- b_up: bfloat16 [4096], P(('dp', 'fsdp')), may hold values from -3 to 3
- w_down: bfloat16 [4096, 1024], P(('dp', 'fsdp')), may hold values from -0.125 to 0.125
- b_down: bfloat16 [1024], P(('dp', 'fsdp')), may hold values from -3 to 3
- gain_two: bfloat16 [1024], P(('dp', 'fsdp')), may hold values from 0.5 to 1.5
- shift_two: bfloat16 [1024], P(('dp', 'fsdp')), may hold values from -2 to 2
Outputs:
- rows_out: bfloat16 [256, 32, 1024], P(None, ('dp', 'fsdp'))
- grad_rows: bfloat16 [256, 32, 1024], P(None, ('dp', 'fsdp'))
- grad_w_qkv: float32 [1024, 3072], P(('dp', 'fsdp'))
- grad_b_query: float32 [1024], P(('dp', 'fsdp'))
- grad_b_value: float32 [1024], P(('dp', 'fsdp'))
- grad_w_out: float32 [1024, 1024], P(('dp', 'fsdp'))
- grad_b_out: float32 [1024], P(('dp', 'fsdp'))
- grad_gain_one: float32 [1024], P(('dp', 'fsdp'))
- grad_shift_one: float32 [1024], P(('dp', 'fsdp'))
- grad_w_up: float32 [1024, 4096], P(('dp', 'fsdp'))
- grad_b_up: float32 [4096], P(('dp', 'fsdp'))
- grad_w_down: float32 [4096, 1024], P(('dp', 'fsdp'))
- grad_b_down: float32 [1024], P(('dp', 'fsdp'))
- grad_gain_two: float32 [1024], P(('dp', 'fsdp'))
- grad_shift_two: float32 [1024], P(('dp', 'fsdp'))
The draws below stay inside these ranges and needn't reach their ends.
Inputs may be any that keep to these rules, and one draw needn't show every extreme that they name: `lengths`: they sum to 8192; sequences deal_order[2 i] and deal_order[2 i + 1] hold 256 tokens together for every i, so at most 9 rows of one device belong to the two sequences of another. `deal_order`: A permutation of the sequences.
All inputs are finite; a program needn't handle non-finite values.
Results may differ from the reference program's by a relative error of at most 0.014.
Values may be sent and summed in bfloat16 or wider, within the bound.
No kernel may reach another device: no remote copies, remote signals or barrier semaphores. Data moves between devices by JAX's collectives and lax.ppermute only.
A program may use at most 192 MiB of HBM per device.

```python
import jax
import jax.numpy as jnp
from jax import lax

D = 1024
HEADS = 16
HEAD_DIM = 64
FF = 4096
TOK_DEV = 256
SHORT = 65
NSEQ = 64
N_DP = 8
N_FSDP = 4


def pairing(base_key):
    groups = NSEQ // 2
    first_len = jax.random.randint(jax.random.fold_in(base_key, 101), (groups,), SHORT, TOK_DEV - SHORT + 1)
    chosen = jax.random.randint(jax.random.fold_in(base_key, 102), (), 0, groups)
    first_len = jnp.where(jnp.arange(groups) == chosen, SHORT, first_len)
    slot_lengths = jnp.stack([first_len, TOK_DEV - first_len], axis=1).reshape(NSEQ)
    dealt = jax.random.permutation(jax.random.fold_in(base_key, 103), NSEQ)
    lengths = jnp.zeros((NSEQ,), jnp.int32).at[dealt].set(slot_lengths.astype(jnp.int32))
    return (lengths, dealt.astype(jnp.int32))


def draw_lengths(key, part):
    return pairing(key)[0]


def draw_deal_order(key, part):
    return pairing(key)[1]


def shard_levels(stream_key, extent, cuts, least, largest):
    def one(dim, shards_of):
        draws = jax.random.uniform(jax.random.fold_in(jax.random.fold_in(stream_key, 6), dim), (shards_of,), jnp.float32, least / len(cuts), largest / len(cuts))
        return jnp.repeat(jnp.exp(draws), extent[dim] // shards_of).reshape((-1,) + (1,) * (len(extent) - dim - 1))

    loudness = one(*cuts[0])
    for cut in cuts[1:]:
        loudness = loudness * one(*cut)
    return loudness


def gaussian(rng, shape, scale, bound, shards=(), held_as=jnp.bfloat16):
    values = scale * jax.random.normal(rng, shape, jnp.float32)
    if shards:
        values = values * shard_levels(rng, shape, shards, -0.22, 0.18)
    return jnp.clip(values, -bound, bound).astype(held_as)


def setup_inputs(seed: int = 0) -> dict:
    key_of = jax.random.split(jax.random.key(seed), 18)
    rows_in = gaussian(key_of[0], (TOK_DEV, N_DP * N_FSDP, D), 1.0, 6.0, ((1, 32),))
    cotangent = gaussian(key_of[1], (TOK_DEV, N_DP * N_FSDP, D), 1.0, 6.0, ((1, 32),))
    lengths = draw_lengths(jax.random.fold_in(key_of[17], 71), 0)
    deal_order = draw_deal_order(jax.random.fold_in(key_of[17], 71), 0)
    w_qkv = gaussian(key_of[4], (D, 3 * D), (D // 2) ** -0.5, 0.25, ((0, 32),))
    b_query = gaussian(key_of[5], (D,), 0.5, 3.0, ((0, 32),))
    b_value = gaussian(key_of[6], (D,), 0.5, 3.0, ((0, 32),))
    w_out = gaussian(key_of[7], (D, D), (D // 8) ** -0.5, 0.5, ((0, 32),))
    b_out = gaussian(key_of[8], (D,), 0.5, 3.0, ((0, 32),))
    gain_one = jnp.clip(1.0 + 0.1 * jax.random.normal(key_of[9], (D,), jnp.float32), 0.5, 1.5).astype(jnp.bfloat16)
    shift_one = gaussian(key_of[10], (D,), 0.3, 2.0, ((0, 32),))
    w_up = gaussian(key_of[11], (D, FF), D ** -0.5, 0.1875, ((0, 32),))
    b_up = gaussian(key_of[12], (FF,), 0.5, 3.0, ((0, 32),))
    w_down = gaussian(key_of[13], (FF, D), (FF // 2) ** -0.5, 0.125, ((0, 32),))
    b_down = gaussian(key_of[14], (D,), 0.5, 3.0, ((0, 32),))
    gain_two = jnp.clip(1.0 + 0.1 * jax.random.normal(key_of[15], (D,), jnp.float32), 0.5, 1.5).astype(jnp.bfloat16)
    shift_two = gaussian(key_of[16], (D,), 0.3, 2.0, ((0, 32),))
    return dict(rows_in=rows_in, cotangent=cotangent, lengths=lengths, deal_order=deal_order, w_qkv=w_qkv, b_query=b_query, b_value=b_value, w_out=w_out, b_out=b_out, gain_one=gain_one, shift_one=shift_one, w_up=w_up, b_up=b_up, w_down=w_down, b_down=b_down, gain_two=gain_two, shift_two=shift_two)


@jax.custom_vjp
def low(v):
    return lax.optimization_barrier(v.astype(jnp.bfloat16)).astype(jnp.float32)

@jax.custom_vjp
def low_back(v):
    return v

def low_keep(v):
    return (low(v), None)

def low_pass(kept, grad):
    return (grad,)

def back_keep(v):
    return (v, None)

def back_low(kept, grad):
    return (low(grad),)
low.defvjp(low_keep, low_pass)
low_back.defvjp(back_keep, back_low)
EPSILON = 1e-05

def layer_norm(values, gain_row, shift_row):
    row_mean = lax.optimization_barrier(jnp.mean(values, axis=-1, keepdims=True))
    centered = values - row_mean
    spread = lax.optimization_barrier(jnp.mean(centered * centered, axis=-1, keepdims=True))
    return centered * lax.rsqrt(spread + EPSILON) * gain_row + shift_row

def matmul(left, right):
    return jnp.dot(left, right, precision=lax.Precision.HIGHEST)

def layer_block(parameters, group_rows, segment, position):
    w_qkv, b_query, b_value, w_out, b_out, gain_one, shift_one, w_up, b_up, w_down, b_down, gain_two, shift_two = parameters
    row_count = group_rows.shape[0]
    model_width = group_rows.shape[1]
    normed_one = low(layer_norm(group_rows, gain_one, shift_one))
    mixed = matmul(normed_one, w_qkv)
    query_rows = low_back(low(mixed[:, :model_width] + b_query)).reshape(row_count, HEADS, HEAD_DIM)
    key_rows = low_back(low(mixed[:, model_width:2 * model_width])).reshape(row_count, HEADS, HEAD_DIM)
    value_rows = low_back(low(mixed[:, 2 * model_width:] + b_value)).reshape(row_count, HEADS, HEAD_DIM)
    allowed = (segment[:, None] == segment[None, :]) & (position[None, :] <= position[:, None])
    scores = low_back(jnp.einsum('qhd,khd->hqk', query_rows, key_rows, precision=lax.Precision.HIGHEST) * HEAD_DIM ** (-0.5))
    masked = jnp.where(allowed[None, :, :], scores, -1000000000.0)
    row_max = lax.optimization_barrier(jnp.max(masked, axis=-1, keepdims=True))
    exps = jnp.exp(masked - row_max)
    softmax_w = low(exps / lax.optimization_barrier(jnp.sum(exps, axis=-1, keepdims=True)))
    attended = jnp.einsum('hqk,khd->qhd', softmax_w, value_rows, precision=lax.Precision.HIGHEST)
    attended = low_back(low(attended.reshape(row_count, model_width)))
    hidden_one = group_rows + low_back(matmul(attended, w_out) + b_out)
    normed_two = low(layer_norm(hidden_one, gain_two, shift_two))
    pre_act = low_back(matmul(normed_two, w_up) + b_up)
    activation = low(jax.nn.gelu(pre_act, approximate=False))
    return hidden_one + low_back(matmul(activation, w_down) + b_down)

def reference(rows_in, cotangent, lengths, deal_order, w_qkv, b_query, b_value, w_out, b_out, gain_one, shift_one, w_up, b_up, w_down, b_down, gain_two, shift_two):
    groups = deal_order.shape[0] // 2
    row_count = rows_in.shape[0]
    model_width = rows_in.shape[2]
    starts = (jnp.cumsum(lengths) - lengths).astype(jnp.int32)
    slot_lengths = lengths[deal_order].astype(jnp.int32)
    first_len = slot_lengths[0::2]
    local_rows = jnp.arange(row_count, dtype=jnp.int32)
    second = local_rows[None, :] >= first_len[:, None]
    sequence = jnp.where(second, deal_order[1::2][:, None], deal_order[0::2][:, None]).astype(jnp.int32)
    position = (local_rows[None, :] - jnp.where(second, first_len[:, None], 0)).astype(jnp.int32)
    token_index = (starts[sequence] + position).astype(jnp.int32)
    segment = second.astype(jnp.int32)
    flat_in = rows_in.reshape(groups * row_count, model_width).astype(jnp.float32)
    flat_cot = cotangent.reshape(groups * row_count, model_width).astype(jnp.float32)
    inputs = flat_in[token_index]
    grad_out = flat_cot[token_index]
    parameters = tuple((p.astype(jnp.float32) for p in (w_qkv, b_query, b_value, w_out, b_out, gain_one, shift_one, w_up, b_up, w_down, b_down, gain_two, shift_two)))

    def forward(params_now, rows_now):

        def one_group(group_item):
            return layer_block(params_now, group_item[0], group_item[1], group_item[2])
        return lax.map(jax.checkpoint(one_group), (rows_now, segment, position))
    outputs, pullback = jax.vjp(forward, parameters, inputs)
    gradients, d_inputs = pullback(grad_out)

    def to_order(values):
        flat_rows = jnp.zeros((groups * row_count, model_width), jnp.float32)
        flat_rows = flat_rows.at[token_index.reshape(-1)].set(values.reshape(-1, model_width))
        return flat_rows.reshape(row_count, groups, model_width).astype(jnp.bfloat16)
    return (to_order(outputs), to_order(d_inputs), gradients[0], gradients[1], gradients[2], gradients[3], gradients[4], gradients[5], gradients[6], gradients[7], gradients[8], gradients[9], gradients[10], gradients[11], gradients[12])
```

```python
import jax
import jax.numpy as jnp
from jax import lax
from jax.experimental import pallas as pl
from jax.experimental.pallas import tpu as pltpu
from jax.sharding import PartitionSpec as P

HEADS = 16
HEAD_DIM = 64
EPSILON = 1e-05
AXES = ("dp", "fsdp")
BF16 = jnp.bfloat16
F32 = jnp.float32


class Grid:
    def __init__(self, n_dp, n_z):
        self.n_dp, self.n_z = n_dp, n_z
        side = 1
        while side * side * 2 < n_dp:
            side *= 2
        self.nx, self.ny = side, n_dp // (2 * side)
        self.x_masks = [2 * k for k in range(1, self.nx)]
        self.y_masks = [2 * side * k for k in range(1, self.ny)]
        self.z_masks = list(range(1, n_z))

    def bind(self):
        dp = lax.axis_index("dp")
        self.my_z = lax.axis_index("fsdp")
        self.my_core = dp % 2
        self.my_x = (dp // 2) % self.nx
        self.my_y = dp // (2 * self.nx)
        self.me = lax.axis_index(AXES)

    def over_dp(self, value, mask):
        return lax.ppermute(value, "dp", [(i, i ^ mask) for i in range(self.n_dp)])

    def over_z(self, value, mask):
        return lax.ppermute(value, "fsdp", [(i, i ^ mask) for i in range(self.n_z)])


def after(value, *deps):
    return lax.optimization_barrier((value,) + deps)[0]


def spread(grid, blocks, first, second):
    base = jnp.concatenate(blocks, 0)
    group = jnp.concatenate([base] + [grid.over_dp(base, m) for m in first], 0)
    masks = [0] + list(first)
    found = [(group, masks)]
    for m in second:
        found.append((grid.over_dp(group, m), [m ^ f for f in masks]))
    return found


def assemble(grid, pieces, rows, col_cuts):
    block = rows // (grid.n_dp * grid.n_z)
    half = grid.n_z // 2
    spans = list(zip([0] + col_cuts[:-1], col_cuts))
    copies = sum(len(masks) * half for _, masks, _ in pieces) * len(spans)

    def kernel(me_ref, *refs):
        sources = refs[: len(pieces)]
        outs = refs[len(pieces) : len(pieces) + len(spans)]
        sems = refs[-1]
        me = me_ref[0]
        started = []
        for source, (_, masks, z_from) in zip(sources, pieces):
            at = 0
            for m in masks:
                for z in range(half):
                    owner = lax.bitwise_xor(me, jnp.int32(m * grid.n_z + z_from + z))
                    to = pl.ds(pl.multiple_of(owner * block, block), block)
                    for out, (lo, hi) in zip(outs, spans):
                        copy = pltpu.make_async_copy(
                            source.at[pl.ds(at * block, block), pl.ds(lo, hi - lo)],
                            out.at[to],
                            sems.at[len(started)],
                        )
                        copy.start()
                        started.append(copy)
                    at += 1
        for copy in started:
            copy.wait()

    return pl.pallas_call(
        kernel,
        out_shape=[jax.ShapeDtypeStruct((rows, hi - lo), BF16) for lo, hi in spans],
        grid_spec=pltpu.PrefetchScalarGridSpec(
            num_scalar_prefetch=1,
            grid=(),
            in_specs=[pl.BlockSpec(memory_space=pl.ANY)] * len(pieces),
            out_specs=[pl.BlockSpec(memory_space=pltpu.VMEM)] * len(spans),
            scratch_shapes=[pltpu.SemaphoreType.DMA((copies,))],
        ),
        compiler_params=pltpu.CompilerParams(vmem_limit_bytes=20 << 20),
        name="assemble",
    )(grid.me.reshape(1).astype(jnp.int32), *[piece for piece, _, _ in pieces])


def gather(grid, shard, col_cuts, ready=()):
    rows = shard.shape[0] * grid.n_dp * grid.n_z
    if shard.shape[0] % 16:
        full = lax.all_gather(shard, AXES, axis=0, tiled=True)
        return [full[:, lo:hi] for lo, hi in zip([0] + col_cuts[:-1], col_cuts)], ()
    if ready:
        shard = after(shard, *ready)
    line = [shard] + [grid.over_z(shard, m) for m in grid.z_masks]
    half = grid.n_z // 2
    pieces = [(v, m, 0) for v, m in spread(grid, line[:half], grid.x_masks, grid.y_masks)]
    pieces += [(v, m, half) for v, m in spread(grid, line[half:], grid.y_masks, grid.x_masks)]
    pieces += [(grid.over_dp(v, 1), [k ^ 1 for k in m], z) for v, m, z in pieces]
    return assemble(grid, pieces, rows, col_cuts), tuple(line[1:])


def outer_sum(left, right):
    return lax.dot_general(left, right, (((0,), (0,)), ((), ())), preferred_element_type=F32)


def back_dot(grad_rows, weight):
    return lax.dot_general(grad_rows, weight, (((1,), (1,)), ((), ())), preferred_element_type=F32)


def pick(array, index, axis):
    return lax.dynamic_index_in_dim(array, index, axis, keepdims=False)


def exchange_sum(grid, array, axis, mine, base):
    count = array.shape[axis]
    total = pick(array, mine, axis)
    got = []
    for k in range(1, count):
        part = pick(array, mine ^ k, axis).astype(BF16)
        if base == 0:
            got.append(grid.over_z(part, k))
        else:
            got.append(grid.over_dp(part, base * k))
    for part in got:
        total = total + part.astype(F32)
    return total


def scatter_outer(grid, left, right):
    tokens, width = left.shape
    places = grid.ny * grid.nx
    block = width // (places * 2 * grid.n_z)
    cols = right.shape[1]
    parts = left.reshape(tokens, places, 2, grid.n_z * block)
    theirs = pick(parts, 1 - grid.my_core, 2).reshape(tokens, width // 2)
    mine = pick(parts, grid.my_core, 2).reshape(tokens, width // 2)
    got = grid.over_dp(outer_sum(theirs, right).astype(BF16), 1)
    held = outer_sum(mine, right) + got.astype(F32)
    held = held.reshape(grid.ny, grid.nx, grid.n_z, block, cols)
    half = grid.n_z // 2
    one = exchange_sum(grid, held[:, :, :half], 0, grid.my_y, 2 * grid.nx)
    two = exchange_sum(grid, held[:, :, half:], 1, grid.my_x, 2)
    one = exchange_sum(grid, one, 0, grid.my_x, 2)
    two = exchange_sum(grid, two, 0, grid.my_y, 2 * grid.nx)
    return exchange_sum(grid, jnp.concatenate([one, two], 0), 0, grid.my_z, 0)


def lookup(small_table, index_rows):
    matches = index_rows[:, None] == jnp.arange(small_table.shape[0], dtype=jnp.int32)[None, :]
    return jnp.sum(jnp.where(matches, small_table[None, :], 0), axis=1)


def rank_among(group_label, order_key):
    earlier = (group_label[None, :] == group_label[:, None]) & (
        order_key[None, :] < order_key[:, None]
    )
    return jnp.sum(earlier.astype(jnp.int32), axis=1)


def routing(lengths, deal_order, devices, row_count, device):
    slot_count = deal_order.shape[0]
    slot_ids = jnp.arange(slot_count, dtype=jnp.int32)
    starts = jnp.cumsum(lengths) - lengths
    slot_of = jnp.sum(
        jnp.where(deal_order[None, :] == slot_ids[:, None], slot_ids[None, :], 0), axis=1
    )
    slot_lengths = lookup(lengths, deal_order)
    slot_rows = row_count // devices + 1
    local_rows = jnp.arange(row_count, dtype=jnp.int32)
    token_index = local_rows * devices + device
    sequence = jnp.sum((starts[None, :] <= token_index[:, None]).astype(jnp.int32), axis=1) - 1
    slot_index = lookup(slot_of, sequence)
    target = slot_index // 2
    send_at = target * slot_rows + rank_among(target, local_rows)
    first_len = lax.dynamic_index_in_dim(slot_lengths, 2 * device, 0, False)
    second = local_rows >= first_len
    first_seq = lax.dynamic_index_in_dim(deal_order, 2 * device, 0, False)
    second_seq = lax.dynamic_index_in_dim(deal_order, 2 * device + 1, 0, False)
    sequence_here = jnp.where(second, second_seq, first_seq)
    position = local_rows - jnp.where(second, first_len, 0)
    source_token = lookup(starts, sequence_here) + position
    source = source_token % devices
    take_at = source * slot_rows + rank_among(source, source_token)
    return (send_at, take_at, second.astype(jnp.int32), position, slot_rows)


def standardize(values):
    centered = values - jnp.mean(values, axis=-1, keepdims=True)
    scale = lax.rsqrt(jnp.mean(centered * centered, axis=-1, keepdims=True) + EPSILON)
    return centered * scale, scale


def standardize_back(grad, unit, scale):
    return scale * (
        grad
        - jnp.mean(grad, axis=-1, keepdims=True)
        - unit * jnp.mean(grad * unit, axis=-1, keepdims=True)
    )


def col_sum(values):
    return jnp.sum(values.astype(F32), axis=0)


def on_device(
    n_dp,
    n_z,
    rows_in,
    cotangent,
    lengths,
    deal_order,
    w_qkv,
    b_query,
    b_value,
    w_out,
    b_out,
    gain_one,
    shift_one,
    w_up,
    b_up,
    w_down,
    b_down,
    gain_two,
    shift_two,
):
    grid = Grid(n_dp, n_z)
    grid.bind()
    devices = n_dp * n_z
    row_count, _, width = rows_in.shape
    hidden = w_up.shape[1]
    share = width // devices

    (full_qkv, full_out), ready = gather(
        grid, jnp.concatenate([w_qkv, w_out], axis=1), [3 * width, 4 * width]
    )
    (full_up,), ready = gather(grid, w_up, [hidden], ready)
    (full_down,), ready = gather(grid, w_down, [width], ready)

    send_at, take_at, segment, position, slot_rows = routing(
        lengths, deal_order, devices, row_count, grid.me
    )
    slots = devices * slot_rows
    slot_ids = jnp.arange(slots, dtype=jnp.int32)
    to_slots = (slot_ids[:, None] == send_at[None, :]).astype(BF16)
    from_slots = (take_at[:, None] == slot_ids[None, :]).astype(BF16)

    def pack(selector, contract, rows):
        return lax.dot_general(
            selector, rows, (((contract,), (0,)), ((), ())), preferred_element_type=F32
        ).astype(BF16)

    def swap(*parts):
        joined = jnp.concatenate([p.reshape(devices, -1, width) for p in parts], axis=1)
        return lax.all_to_all(joined, AXES, split_axis=0, concat_axis=0, tiled=True)

    small = jnp.concatenate(
        [b_query, b_value, b_out, gain_one, shift_one, b_down, gain_two, shift_two, b_up]
    )
    small = jnp.pad(small, (0, width - small.shape[0]))
    arrived = swap(
        pack(to_slots, 1, rows_in.reshape(row_count, width)),
        pack(to_slots, 1, cotangent.reshape(row_count, width)),
        jnp.broadcast_to(small, (devices, 1, width)),
    )
    token_rows = arrived[:, :slot_rows].reshape(slots, width)
    cot_rows = arrived[:, slot_rows : 2 * slot_rows].reshape(slots, width)
    inputs = pack(from_slots, 1, token_rows).astype(F32)
    grad_m_b = pack(from_slots, 1, cot_rows)
    small_all = arrived[:, 2 * slot_rows].astype(F32)
    vectors = [small_all[:, k * share : (k + 1) * share].reshape(width) for k in range(8)]
    bq, bv, bo, g1, s1, bd, g2, s2 = vectors
    bu = small_all[:, 8 * share : 8 * share + hidden // devices].reshape(hidden)

    unit_one, scale_one = standardize(inputs)
    normed_one_b = (unit_one * g1 + s1).astype(BF16)
    mixed = jnp.dot(normed_one_b, full_qkv, preferred_element_type=F32)
    head_shape = (row_count, HEADS, HEAD_DIM)
    query_b = (mixed[:, :width] + bq).astype(BF16).reshape(head_shape)
    key_b = mixed[:, width : 2 * width].astype(BF16).reshape(head_shape)
    value_b = (mixed[:, 2 * width :] + bv).astype(BF16).reshape(head_shape)
    allowed = (segment[:, None] == segment[None, :]) & (position[None, :] <= position[:, None])
    scale_factor = HEAD_DIM ** (-0.5)
    scores = jnp.einsum("qhd,khd->hqk", query_b, key_b, preferred_element_type=F32)
    masked = jnp.where(allowed[None], scores * scale_factor, -1000000000.0)
    exps = jnp.exp(masked - jnp.max(masked, axis=-1, keepdims=True))
    softmax_f = exps / jnp.sum(exps, axis=-1, keepdims=True)
    softmax_b = softmax_f.astype(BF16)
    attended_b = jnp.einsum("hqk,khd->qhd", softmax_b, value_b, preferred_element_type=F32)
    attended_b = attended_b.reshape(row_count, width).astype(BF16)
    hidden_one = inputs + jnp.dot(attended_b, full_out, preferred_element_type=F32) + bo

    unit_two, scale_two = standardize(hidden_one)
    normed_two_b = (unit_two * g2 + s2).astype(BF16)
    pre_act = jnp.dot(normed_two_b, full_up, preferred_element_type=F32) + bu
    half_cdf = 0.5 * (1.0 + lax.erf(pre_act * (0.5**0.5)))
    activation_b = (pre_act * half_cdf).astype(BF16)
    density = jnp.exp(-0.5 * pre_act * pre_act) * ((2.0 * jnp.pi) ** -0.5)
    slope = half_cdf + pre_act * density

    grad_w_down = scatter_outer(grid, activation_b, grad_m_b)
    term_b_down = col_sum(grad_m_b)

    result_rows = hidden_one + jnp.dot(activation_b, full_down, preferred_element_type=F32) + bd

    grad_pre_b = (back_dot(grad_m_b, full_down) * slope).astype(BF16)
    grad_w_up = scatter_outer(grid, normed_two_b, grad_pre_b)
    term_b_up = col_sum(grad_pre_b)
    grad_normed_two = back_dot(grad_pre_b, full_up)
    term_g2 = col_sum(grad_normed_two * unit_two)
    term_s2 = col_sum(grad_normed_two)
    grad_hidden = grad_m_b.astype(F32) + standardize_back(grad_normed_two * g2, unit_two, scale_two)
    grad_branch_b = grad_hidden.astype(BF16)
    term_b_out = col_sum(grad_branch_b)

    grad_w_out = scatter_outer(grid, attended_b, grad_branch_b)
    grad_att_b = back_dot(grad_branch_b, full_out).astype(BF16).reshape(head_shape)
    grad_probs = jnp.einsum("qhd,khd->hqk", grad_att_b, value_b, preferred_element_type=F32)
    grad_scores_b = (
        softmax_f * (grad_probs - jnp.sum(softmax_f * grad_probs, axis=-1, keepdims=True))
    ).astype(BF16)
    grad_query = jnp.einsum("hqk,khd->qhd", grad_scores_b, key_b, preferred_element_type=F32)
    grad_key = jnp.einsum("hqk,qhd->khd", grad_scores_b, query_b, preferred_element_type=F32)
    grad_value = jnp.einsum("hqk,qhd->khd", softmax_b, grad_att_b, preferred_element_type=F32)
    grad_mixed_b = jnp.concatenate(
        [
            (grad_query * scale_factor).astype(BF16).reshape(row_count, width),
            (grad_key * scale_factor).astype(BF16).reshape(row_count, width),
            grad_value.astype(BF16).reshape(row_count, width),
        ],
        axis=1,
    )
    grad_w_qkv = scatter_outer(grid, normed_one_b, grad_mixed_b)
    term_mixed = col_sum(grad_mixed_b)
    grad_normed_one = back_dot(grad_mixed_b, full_qkv)
    term_g1 = col_sum(grad_normed_one * unit_one)
    term_s1 = col_sum(grad_normed_one)
    grad_inputs = grad_hidden + standardize_back(grad_normed_one * g1, unit_one, scale_one)

    terms = [term_mixed[:width], term_mixed[2 * width :], term_b_out, term_g1, term_s1]
    terms += [term_b_down, term_g2, term_s2, term_b_up]
    terms = jnp.concatenate([v.reshape(devices, -1) for v in terms], axis=1)
    count = terms.shape[1]
    high = lax.reduce_precision(terms, 8, 7)
    low = terms - high
    small_back = jnp.concatenate([high, low], axis=1).astype(BF16)
    small_back = jnp.pad(small_back, ((0, 0), (0, width - 2 * count)))
    returned = swap(
        pack(from_slots, 0, result_rows.astype(BF16)),
        pack(from_slots, 0, grad_inputs.astype(BF16)),
        small_back[:, None],
    )
    rows_out = pack(to_slots, 0, returned[:, :slot_rows].reshape(slots, width))
    grad_rows = pack(to_slots, 0, returned[:, slot_rows : 2 * slot_rows].reshape(slots, width))
    sums = jnp.sum(returned[:, 2 * slot_rows].astype(F32), axis=0)
    sums = sums[:count] + sums[count : 2 * count]
    cut = [sums[k * share : (k + 1) * share] for k in range(8)]
    grad_bq, grad_bv, grad_bo, grad_g1, grad_s1, grad_bd, grad_g2, grad_s2 = cut
    grad_bu = sums[8 * share :]
    return (
        rows_out.reshape(row_count, 1, width),
        grad_rows.reshape(row_count, 1, width),
        grad_w_qkv,
        grad_bq,
        grad_bv,
        grad_w_out,
        grad_bo,
        grad_g1,
        grad_s1,
        grad_w_up,
        grad_bu,
        grad_w_down,
        grad_bd,
        grad_g2,
        grad_s2,
    )


def solution(mesh):
    n_dp, n_z = mesh.shape["dp"], mesh.shape["fsdp"]
    rows, vec, mat = P(None, AXES, None), P(AXES), P(AXES, None)

    def run(*args):
        return on_device(n_dp, n_z, *args)

    return jax.shard_map(
        run,
        mesh=mesh,
        in_specs=(rows, rows, P(), P())
        + (mat, vec, vec, mat, vec, vec, vec, mat, vec, mat, vec, vec, vec),
        out_specs=(rows, rows, mat, vec, vec, mat, vec, vec, vec, mat, vec, mat, vec, vec, vec),
        check_vma=False,
    )
```

```python
import jax
import jax.numpy as jnp
from jax import lax
from jax.experimental import pallas as pl
from jax.experimental.pallas import tpu as pltpu
from jax.sharding import PartitionSpec as P

HEADS = 16
HEAD_DIM = 64
EPSILON = 1e-05
AXES = ("dp", "fsdp")
BF16 = jnp.bfloat16
F32 = jnp.float32


class Grid:
    def __init__(self, n_dp, n_z):
        self.n_dp, self.n_z = n_dp, n_z
        side = 1
        while side * side * 2 < n_dp:
            side *= 2
        self.nx, self.ny = side, n_dp // (2 * side)
        self.x_masks = [2 * k for k in range(1, self.nx)]
        self.y_masks = [2 * side * k for k in range(1, self.ny)]
        self.z_masks = list(range(1, n_z))

    def bind(self):
        self.my_dp = lax.axis_index("dp").astype(jnp.int32)
        self.my_z = lax.axis_index("fsdp").astype(jnp.int32)
        self.me = lax.axis_index(AXES).astype(jnp.int32)

    def over_dp(self, value, mask):
        return lax.ppermute(value, "dp", [(i, i ^ mask) for i in range(self.n_dp)])

    def over_z(self, value, mask):
        return lax.ppermute(value, "fsdp", [(i, i ^ mask) for i in range(self.n_z)])


class Clock:
    def __init__(self):
        self.last = ()

    def gate(self, *values):
        held = lax.optimization_barrier(tuple(values) + self.last)[: len(values)]
        return held if len(values) > 1 else held[0]

    def tick(self, *values):
        self.last = values


class Gather:
    def __init__(self, grid, clock, shard, col_cuts):
        self.grid, self.clock, self.cuts = grid, clock, col_cuts
        self.shard = shard

    def step0(self):
        shard = self.clock.gate(self.shard)
        far = [m for m in self.grid.z_masks if m % 2 == 0]
        self.near = [(shard, 0)]
        self.coming = [(self.grid.over_z(shard, m), m) for m in far]

    def step1(self):
        grid = self.grid
        got = self.clock.gate(*[v for v, _ in self.coming], self.shard)[:-1]
        got = [(v, m) for v, (_, m) in zip(got, self.coming)]
        parts = self.near + got
        low = jnp.concatenate([v for v, _ in parts], 0)
        self.clock.tick(low)
        self.low = (low, [m for _, m in parts])
        self.high = (grid.over_z(low, 1), [m ^ 1 for m in self.low[1]])
        self.low_got = [(grid.over_dp(low, m), m) for m in grid.x_masks]

    def step2(self):
        high = self.clock.gate(self.high[0], self.shard)[0]
        self.clock.tick(high)
        self.high = (high, self.high[1])
        self.high_got = [(self.grid.over_dp(high, m), m) for m in self.grid.y_masks]

    def join(self, have, coming):
        got = self.clock.gate(*[v for v, _ in coming], have[0])[:-1]
        rows = jnp.concatenate([have[0], *got], 0)
        marks = list(have[1])
        for _, m in coming:
            marks += [(d ^ m, z) for d, z in have[1]]
        self.clock.tick(rows)
        return rows, marks

    def step3(self):
        low = (self.low[0], [(0, z) for z in self.low[1]])
        self.low = self.join(low, self.low_got)
        self.low_got = [(self.grid.over_dp(self.low[0], m), m) for m in self.grid.y_masks]

    def step4(self):
        high = (self.high[0], [(0, z) for z in self.high[1]])
        self.high = self.join(high, self.high_got)
        self.high_got = [(self.grid.over_dp(self.high[0], m), m) for m in self.grid.x_masks]

    def step5(self):
        self.low = self.join(self.low, self.low_got)
        self.low_got = self.grid.over_dp(self.low[0], 1)

    def step6(self):
        self.high = self.join(self.high, self.high_got)
        self.high_got = self.grid.over_dp(self.high[0], 1)

    def step7(self):
        grid = self.grid
        block = self.shard.shape[0]
        rows = block * grid.n_dp * grid.n_z
        spans = list(zip([0] + self.cuts[:-1], self.cuts))
        pieces = []
        for (mine, marks), theirs in ((self.low, self.low_got), (self.high, self.high_got)):
            pieces.append((mine, [d * grid.n_z + z for d, z in marks]))
            pieces.append((theirs, [(d ^ 1) * grid.n_z + z for d, z in marks]))
        copies = sum(len(marks) for _, marks in pieces) * len(spans)

        def kernel(me_ref, *refs):
            sources = refs[: len(pieces)]
            outs = refs[len(pieces) : len(pieces) + len(spans)]
            sems = refs[-1]
            started = []
            for source, (_, marks) in zip(sources, pieces):
                for at, mark in enumerate(marks):
                    owner = lax.bitwise_xor(me_ref[0], jnp.int32(mark))
                    to = pl.ds(pl.multiple_of(owner * block, block), block)
                    for out, (lo, hi) in zip(outs, spans):
                        copy = pltpu.make_async_copy(
                            source.at[pl.ds(at * block, block), pl.ds(lo, hi - lo)],
                            out.at[to],
                            sems.at[len(started)],
                        )
                        copy.start()
                        started.append(copy)
            for copy in started:
                copy.wait()

        arrays = self.clock.gate(*[v for v, _ in pieces])
        full = pl.pallas_call(
            kernel,
            out_shape=[jax.ShapeDtypeStruct((rows, hi - lo), BF16) for lo, hi in spans],
            grid_spec=pltpu.PrefetchScalarGridSpec(
                num_scalar_prefetch=1,
                grid=(),
                in_specs=[pl.BlockSpec(memory_space=pl.ANY)] * len(pieces),
                out_specs=[pl.BlockSpec(memory_space=pltpu.VMEM)] * len(spans),
                scratch_shapes=[pltpu.SemaphoreType.DMA((copies,))],
            ),
            compiler_params=pltpu.CompilerParams(vmem_limit_bytes=20 << 20),
            cost_estimate=pl.CostEstimate(flops=0, bytes_accessed=0, transcendentals=0),
            name="assemble",
        )(grid.me.reshape(1), *arrays)
        self.clock.tick(*full)
        return full


class PlainGather:
    def __init__(self, grid, clock, shard, col_cuts):
        self.clock, self.shard, self.cuts = clock, shard, col_cuts

    def step0(self):
        self.full = lax.all_gather(self.shard, AXES, axis=0, tiled=True)

    def step1(self):
        pass

    step2 = step3 = step4 = step5 = step6 = step1

    def step7(self):
        return [self.full[:, lo:hi] for lo, hi in zip([0] + self.cuts[:-1], self.cuts)]


def make_gather(grid, clock, shard, col_cuts):
    kind = PlainGather if shard.shape[0] % 16 else Gather
    return kind(grid, clock, shard, col_cuts)


def contract_rows(left, right):
    return lax.dot_general(left, right, (((0,), (0,)), ((), ())), preferred_element_type=F32)


def back_dot(grad_rows, weight):
    return lax.dot_general(grad_rows, weight, (((1,), (1,)), ((), ())), preferred_element_type=F32)


def pick(array, index):
    return lax.dynamic_index_in_dim(array, index, 0, keepdims=False)


def total_of(base, parts):
    for part in parts:
        base = base + part.astype(F32)
    return base


class Scatter:
    def __init__(self, grid, clock, left, right):
        self.grid, self.clock, self.left, self.right = grid, clock, left, right
        self.places = grid.ny * grid.nx
        self.chunk = left.shape[1] // grid.n_dp
        self.cols = right.shape[1]

    def call(self, kernel, mask, ins, in_specs, out_shape, out_specs):
        tokens = self.left.shape[0]
        left, right, *ins = self.clock.gate(self.left, self.right, *ins)
        return pl.pallas_call(
            kernel,
            out_shape=out_shape,
            grid_spec=pltpu.PrefetchScalarGridSpec(
                num_scalar_prefetch=1,
                grid=(self.places,),
                in_specs=[
                    pl.BlockSpec(
                        (tokens, self.chunk),
                        lambda j, dp: (0, lax.bitwise_xor(dp[0], 2 * j + mask)),
                    ),
                    pl.BlockSpec((tokens, self.cols), lambda j, dp: (0, 0)),
                    *in_specs,
                ],
                out_specs=out_specs,
            ),
            compiler_params=pltpu.CompilerParams(vmem_limit_bytes=20 << 20),
            cost_estimate=pl.CostEstimate(
                flops=2 * tokens * self.chunk * self.places * self.cols,
                bytes_accessed=4 * self.chunk * self.places * self.cols,
                transcendentals=0,
            ),
            name="outer",
        )(self.grid.my_dp.reshape(1), left, right, *ins)

    def across(self):
        def kernel(dp_ref, left, right, out):
            out[...] = contract_rows(left[...], right[...]).astype(BF16)

        spec = pl.BlockSpec((self.chunk, self.cols), lambda j, dp: (j, 0))
        shape = jax.ShapeDtypeStruct((self.chunk * self.places, self.cols), BF16)
        send = self.call(kernel, 1, (), (), shape, spec)
        self.clock.tick(send)
        self.got = self.grid.over_dp(send, 1)

    def first(self):
        grid = self.grid
        nx, ny, cols = grid.nx, grid.ny, self.cols
        half = self.chunk // 2

        def kernel(dp_ref, left, right, got, low_keep, low_send, high_keep, high_send):
            j = pl.program_id(0)
            py, px = j // nx, j % nx
            held = contract_rows(left[...], right[...]) + got[...].astype(F32)

            @pl.when(py == 0)
            def _():
                low_keep[0] = held[:half]

            @pl.when(py != 0)
            def _():
                low_send[0] = held[:half].astype(BF16)

            @pl.when(px == 0)
            def _():
                high_keep[0] = held[half:]

            @pl.when(px != 0)
            def _():
                high_send[0] = held[half:].astype(BF16)

        def block(index):
            return pl.BlockSpec((1, half, cols), lambda j, dp: (index(j // nx, j % nx), 0, 0))

        def low_send_at(y, x):
            return jnp.where(y == 0, 0, (y - 1) * nx + x)

        def high_send_at(y, x):
            return (jnp.maximum(x, 1) - 1) * ny + y

        low_keep, low_send, high_keep, high_send = self.call(
            kernel,
            0,
            (self.got,),
            [pl.BlockSpec((self.chunk, cols), lambda j, dp: (j, 0))],
            [
                jax.ShapeDtypeStruct((nx, half, cols), F32),
                jax.ShapeDtypeStruct(((ny - 1) * nx, half, cols), BF16),
                jax.ShapeDtypeStruct((ny, half, cols), F32),
                jax.ShapeDtypeStruct(((nx - 1) * ny, half, cols), BF16),
            ],
            [
                block(lambda y, x: jnp.where(y == 0, x, nx - 1)),
                block(low_send_at),
                block(lambda y, x: y),
                block(high_send_at),
            ],
        )
        self.clock.tick(low_send, high_send)
        self.keep = (low_keep, high_keep)
        self.low_got = [
            grid.over_dp(low_send[k * nx : (k + 1) * nx], m) for k, m in enumerate(grid.y_masks)
        ]
        self.high_got = [
            grid.over_dp(high_send[k * ny : (k + 1) * ny], m) for k, m in enumerate(grid.x_masks)
        ]

    def second(self):
        grid = self.grid
        got = self.clock.gate(*self.low_got, *self.high_got)
        count = len(self.low_got)
        low_keep, high_keep = self.keep
        low_got, high_got = got[:count], got[count:]
        low_send = total_of(low_keep[1:], [g[1:] for g in low_got]).astype(BF16)
        high_send = total_of(high_keep[1:], [g[1:] for g in high_got]).astype(BF16)
        self.clock.tick(low_send, high_send)
        self.keep = (
            total_of(low_keep[0], [g[0] for g in low_got]),
            total_of(high_keep[0], [g[0] for g in high_got]),
        )
        self.low_got = [grid.over_dp(low_send[k], m) for k, m in enumerate(grid.x_masks)]
        self.high_got = [grid.over_dp(high_send[k], m) for k, m in enumerate(grid.y_masks)]

    def third(self):
        grid = self.grid
        got = self.clock.gate(*self.low_got, *self.high_got)
        count = len(self.low_got)
        low = total_of(self.keep[0], got[:count])
        high = total_of(self.keep[1], got[count:])
        lines = jnp.concatenate([low, high], 0).reshape(grid.n_z // 2, 2, -1, self.cols)
        odd = grid.my_z % 2
        send = lax.dynamic_index_in_dim(lines, 1 - odd, 1, keepdims=False).astype(BF16)
        self.keep = lax.dynamic_index_in_dim(lines, odd, 1, keepdims=False)
        self.clock.tick(send)
        self.line = grid.over_z(send, 1)

    def fourth(self):
        grid = self.grid
        held = self.keep + self.clock.gate(self.line).astype(F32)
        pair = grid.my_z // 2
        sends = [pick(held, pair ^ (m // 2)).astype(BF16) for m in grid.z_masks if m % 2 == 0]
        self.keep = pick(held, pair)
        self.clock.tick(*sends)
        far = [m for m in grid.z_masks if m % 2 == 0]
        self.line = [grid.over_z(v, m) for v, m in zip(sends, far)]

    def done(self):
        got = self.clock.gate(*self.line, self.keep)[:-1]
        out = total_of(self.keep, got)
        self.clock.tick(out)
        return out


class PlainScatter:
    def __init__(self, grid, clock, left, right):
        self.left, self.right = left, right

    def across(self):
        term = contract_rows(self.left, self.right)
        self.out = lax.psum_scatter(term, AXES, scatter_dimension=0, tiled=True)

    def first(self):
        pass

    second = third = fourth = first

    def done(self):
        return self.out


def make_scatter(grid, clock, left, right):
    kind = PlainScatter if (left.shape[1] // grid.n_dp) % 128 else Scatter
    return kind(grid, clock, left, right)


def lookup(small_table, index_rows):
    matches = index_rows[:, None] == jnp.arange(small_table.shape[0], dtype=jnp.int32)[None, :]
    return jnp.sum(jnp.where(matches, small_table[None, :], 0), axis=1)


def rank_among(group_label, order_key):
    earlier = (group_label[None, :] == group_label[:, None]) & (
        order_key[None, :] < order_key[:, None]
    )
    return jnp.sum(earlier.astype(jnp.int32), axis=1)


def routing(lengths, deal_order, devices, row_count, device):
    slot_count = deal_order.shape[0]
    slot_ids = jnp.arange(slot_count, dtype=jnp.int32)
    starts = jnp.cumsum(lengths) - lengths
    slot_of = jnp.sum(
        jnp.where(deal_order[None, :] == slot_ids[:, None], slot_ids[None, :], 0), axis=1
    )
    slot_lengths = lookup(lengths, deal_order)
    local_rows = jnp.arange(row_count, dtype=jnp.int32)
    token_index = local_rows * devices + device
    sequence = jnp.sum((starts[None, :] <= token_index[:, None]).astype(jnp.int32), axis=1) - 1
    slot_index = lookup(slot_of, sequence)
    target = slot_index // 2
    send_rank = rank_among(target, local_rows)
    first_len = lax.dynamic_index_in_dim(slot_lengths, 2 * device, 0, False)
    second = local_rows >= first_len
    first_seq = lax.dynamic_index_in_dim(deal_order, 2 * device, 0, False)
    second_seq = lax.dynamic_index_in_dim(deal_order, 2 * device + 1, 0, False)
    sequence_here = jnp.where(second, second_seq, first_seq)
    position = local_rows - jnp.where(second, first_len, 0)
    source_token = lookup(starts, sequence_here) + position
    source = source_token % devices
    take_rank = rank_among(source, source_token)
    return target, send_rank, source, take_rank, second.astype(jnp.int32), position


def standardize(values):
    centered = values - jnp.mean(values, axis=-1, keepdims=True)
    scale = lax.rsqrt(jnp.mean(centered * centered, axis=-1, keepdims=True) + EPSILON)
    return centered * scale, scale


def standardize_back(grad, unit, scale):
    return scale * (
        grad
        - jnp.mean(grad, axis=-1, keepdims=True)
        - unit * jnp.mean(grad * unit, axis=-1, keepdims=True)
    )


def col_sum(values):
    return jnp.sum(values.astype(F32), axis=0)


def on_device(
    n_dp,
    n_z,
    rows_in,
    cotangent,
    lengths,
    deal_order,
    w_qkv,
    b_query,
    b_value,
    w_out,
    b_out,
    gain_one,
    shift_one,
    w_up,
    b_up,
    w_down,
    b_down,
    gain_two,
    shift_two,
):
    grid = Grid(n_dp, n_z)
    grid.bind()
    clock = Clock()
    devices = n_dp * n_z
    row_count, _, width = rows_in.shape
    hidden = w_up.shape[1]
    share = width // devices

    attn = make_gather(
        grid, clock, jnp.concatenate([w_qkv, w_out], axis=1), [3 * width, 4 * width]
    )
    up = make_gather(grid, clock, w_up, [hidden])
    down = make_gather(grid, clock, w_down, [width])

    attn.step0()

    target, send_rank, source, take_rank, segment, position = routing(
        lengths, deal_order, devices, row_count, grid.me
    )
    slot_rows = row_count // devices + 1
    block_rows = -(-(2 * slot_rows + 1) // 8) * 8
    slots = devices * block_rows
    slot_ids = jnp.arange(slots, dtype=jnp.int32)
    send_at = target * block_rows + send_rank
    take_at = source * block_rows + take_rank
    send_both = jnp.concatenate([send_at, send_at + slot_rows])
    take_both = jnp.concatenate([take_at, take_at + slot_rows])
    to_slots = (slot_ids[:, None] == send_both[None, :]).astype(BF16)
    from_slots = (take_both[:, None] == slot_ids[None, :]).astype(BF16)
    last_row = (slot_ids % block_rows == 2 * slot_rows)[:, None]

    def all_swap(block):
        block = block.reshape(devices, block_rows, width)
        return lax.all_to_all(block, AXES, split_axis=0, concat_axis=0, tiled=True)

    small = jnp.concatenate(
        [b_query, b_value, b_out, gain_one, shift_one, b_down, gain_two, shift_two, b_up]
    )
    small = jnp.pad(small, (0, width - small.shape[0]))
    block = jnp.dot(
        to_slots[:, :row_count], rows_in.reshape(row_count, width), preferred_element_type=F32
    )
    block += jnp.dot(
        to_slots[:, row_count:], cotangent.reshape(row_count, width), preferred_element_type=F32
    )
    block = block.astype(BF16)
    block = jnp.where(last_row, small[None, :], block)
    clock.tick(block)
    attn.step1()
    up.step0()
    arrived = all_swap(clock.gate(block))
    attn.step2()
    attn.step3()
    up.step1()
    attn.step4()
    down.step0()
    up.step2()
    up.step3()

    arrived = clock.gate(arrived)
    taken = jnp.dot(from_slots, arrived.reshape(slots, width), preferred_element_type=F32)
    grad_m_b = taken[row_count:].astype(BF16)
    inputs = taken[:row_count]
    small_all = arrived[:, 2 * slot_rows].astype(F32)
    vectors = [small_all[:, k * share : (k + 1) * share].reshape(width) for k in range(8)]
    bq, bv, bo, g1, s1, bd, g2, s2 = vectors
    bu = small_all[:, 8 * share : 8 * share + hidden // devices].reshape(hidden)
    unit_one, scale_one = standardize(inputs)
    normed_one_b = (unit_one * g1 + s1).astype(BF16)
    clock.tick(normed_one_b, grad_m_b)
    term_b_down = col_sum(grad_m_b)

    attn.step5()
    down.step1()
    up.step4()
    attn.step6()
    down.step2()
    down.step3()
    full_qkv, full_out = attn.step7()

    mixed = jnp.dot(clock.gate(normed_one_b), full_qkv, preferred_element_type=F32)
    head_shape = (row_count, HEADS, HEAD_DIM)
    query_b = (mixed[:, :width] + bq).astype(BF16).reshape(head_shape)
    key_b = mixed[:, width : 2 * width].astype(BF16).reshape(head_shape)
    value_b = (mixed[:, 2 * width :] + bv).astype(BF16).reshape(head_shape)
    allowed = (segment[:, None] == segment[None, :]) & (position[None, :] <= position[:, None])
    scale_factor = HEAD_DIM ** (-0.5)
    scores = jnp.einsum("qhd,khd->hqk", query_b, key_b, preferred_element_type=F32)
    masked = jnp.where(allowed[None], scores * scale_factor, -1000000000.0)
    exps = jnp.exp(masked - jnp.max(masked, axis=-1, keepdims=True))
    softmax_f = exps / jnp.sum(exps, axis=-1, keepdims=True)
    softmax_b = softmax_f.astype(BF16)
    attended_b = jnp.einsum("hqk,khd->qhd", softmax_b, value_b, preferred_element_type=F32)
    attended_b = attended_b.reshape(row_count, width).astype(BF16)
    hidden_one = inputs + jnp.dot(attended_b, full_out, preferred_element_type=F32) + bo
    unit_two, scale_two = standardize(hidden_one)
    normed_two_b = (unit_two * g2 + s2).astype(BF16)
    clock.tick(normed_two_b)

    up.step5()
    down.step4()
    up.step6()
    (full_up,) = up.step7()
    pre_act = jnp.dot(clock.gate(normed_two_b), full_up, preferred_element_type=F32) + bu
    half_cdf = 0.5 * (1.0 + lax.erf(pre_act * (0.5**0.5)))
    activation_b = (pre_act * half_cdf).astype(BF16)
    density = jnp.exp(-0.5 * pre_act * pre_act) * ((2.0 * jnp.pi) ** -0.5)
    slope = half_cdf + pre_act * density
    clock.tick(activation_b, slope)

    for_down = make_scatter(grid, clock, activation_b, grad_m_b)
    for_down.across()
    down.step5()
    down.step6()
    for_down.first()
    (full_down,) = down.step7()

    grad_pre_b = (back_dot(clock.gate(grad_m_b), full_down) * slope).astype(BF16)
    clock.tick(grad_pre_b)
    term_b_up = col_sum(grad_pre_b)
    for_up = make_scatter(grid, clock, normed_two_b, grad_pre_b)
    for_up.across()

    grad_normed_two = back_dot(clock.gate(grad_pre_b), full_up)
    term_g2 = col_sum(grad_normed_two * unit_two)
    term_s2 = col_sum(grad_normed_two)
    grad_hidden = grad_m_b.astype(F32) + standardize_back(grad_normed_two * g2, unit_two, scale_two)
    grad_branch_b = grad_hidden.astype(BF16)
    clock.tick(grad_branch_b)
    term_b_out = col_sum(grad_branch_b)
    for_down.second()
    for_up.first()

    for_out = make_scatter(grid, clock, attended_b, grad_branch_b)
    for_out.across()
    grad_att_b = back_dot(clock.gate(grad_branch_b), full_out).astype(BF16)
    clock.tick(grad_att_b)
    for_down.third()
    for_out.first()

    grad_att_b = clock.gate(grad_att_b).reshape(head_shape)
    grad_probs = jnp.einsum("qhd,khd->hqk", grad_att_b, value_b, preferred_element_type=F32)
    grad_scores_b = (
        softmax_f * (grad_probs - jnp.sum(softmax_f * grad_probs, axis=-1, keepdims=True))
    ).astype(BF16)
    grad_query = jnp.einsum("hqk,khd->qhd", grad_scores_b, key_b, preferred_element_type=F32)
    grad_key = jnp.einsum("hqk,qhd->khd", grad_scores_b, query_b, preferred_element_type=F32)
    grad_value = jnp.einsum("hqk,qhd->khd", softmax_b, grad_att_b, preferred_element_type=F32)
    grad_mixed_b = jnp.concatenate(
        [
            (grad_query * scale_factor).astype(BF16).reshape(row_count, width),
            (grad_key * scale_factor).astype(BF16).reshape(row_count, width),
            grad_value.astype(BF16).reshape(row_count, width),
        ],
        axis=1,
    )
    clock.tick(grad_mixed_b)
    term_mixed = col_sum(grad_mixed_b)
    for_up.second()
    for_qkv = make_scatter(grid, clock, normed_one_b, grad_mixed_b)
    for_qkv.across()

    grad_normed_one = back_dot(clock.gate(grad_mixed_b), full_qkv)
    term_g1 = col_sum(grad_normed_one * unit_one)
    term_s1 = col_sum(grad_normed_one)
    grad_inputs = grad_hidden + standardize_back(grad_normed_one * g1, unit_one, scale_one)
    grad_inputs_b = grad_inputs.astype(BF16)
    clock.tick(grad_inputs_b)
    for_qkv.first()
    for_out.second()
    for_up.third()
    for_down.fourth()

    result = jnp.dot(clock.gate(activation_b), full_down, preferred_element_type=F32)
    result_b = (hidden_one + result + bd).astype(BF16)
    terms = [term_mixed[:width], term_mixed[2 * width :], term_b_out, term_g1, term_s1]
    terms += [term_b_down, term_g2, term_s2, term_b_up]
    terms = jnp.concatenate([v.reshape(devices, -1) for v in terms], axis=1)
    count = terms.shape[1]
    top = lax.reduce_precision(terms, 8, 7)
    small_back = jnp.concatenate([top, terms - top], axis=1).astype(BF16)
    small_back = jnp.pad(small_back, ((0, 0), (0, width - 2 * count)))
    small_back = jnp.broadcast_to(small_back[:, None], (devices, block_rows, width))
    both = jnp.concatenate([result_b, grad_inputs_b], axis=0)
    block = contract_rows(from_slots, both).astype(BF16)
    block = jnp.where(last_row, small_back.reshape(slots, width), block)
    clock.tick(block)
    returned = all_swap(block)

    for_qkv.second()
    for_out.third()
    for_up.fourth()
    for_qkv.third()
    for_out.fourth()
    grad_w_down = for_down.done()
    for_qkv.fourth()
    grad_w_up = for_up.done()
    grad_w_out = for_out.done()
    returned = clock.gate(returned)
    placed = contract_rows(to_slots, returned.reshape(slots, width)).astype(BF16)
    sums = jnp.sum(returned[:, 2 * slot_rows].astype(F32), axis=0)
    clock.tick(placed)
    grad_w_qkv = for_qkv.done()

    sums = sums[:count] + sums[count : 2 * count]
    cut = [sums[k * share : (k + 1) * share] for k in range(8)]
    grad_bq, grad_bv, grad_bo, grad_g1, grad_s1, grad_bd, grad_g2, grad_s2 = cut
    grad_bu = sums[8 * share :]
    return (
        placed[:row_count].reshape(row_count, 1, width),
        placed[row_count:].reshape(row_count, 1, width),
        grad_w_qkv,
        grad_bq,
        grad_bv,
        grad_w_out,
        grad_bo,
        grad_g1,
        grad_s1,
        grad_w_up,
        grad_bu,
        grad_w_down,
        grad_bd,
        grad_g2,
        grad_s2,
    )


def solution(mesh):
    n_dp, n_z = mesh.shape["dp"], mesh.shape["fsdp"]
    rows, vec, mat = P(None, AXES, None), P(AXES), P(AXES, None)

    def run(*args):
        return on_device(n_dp, n_z, *args)

    return jax.shard_map(
        run,
        mesh=mesh,
        in_specs=(rows, rows, P(), P())
        + (mat, vec, vec, mat, vec, vec, vec, mat, vec, mat, vec, vec, vec),
        out_specs=(rows, rows, mat, vec, vec, mat, vec, vec, vec, mat, vec, mat, vec, vec, vec),
        check_vma=False,
    )
```

```python
import jax
import jax.numpy as jnp
from jax import lax
from jax.experimental import pallas as pl
from jax.experimental.pallas import tpu as pltpu
from jax.sharding import PartitionSpec as P

HEADS = 16
HEAD_DIM = 64
EPSILON = 1e-05
AXES = ("dp", "fsdp")
BF16 = jnp.bfloat16
F32 = jnp.float32


class Grid:
    def __init__(self, n_dp, n_z):
        self.n_dp, self.n_z = n_dp, n_z
        side = 1
        while side * side * 2 < n_dp:
            side *= 2
        self.nx, self.ny = side, n_dp // (2 * side)
        self.x_masks = [2 * k for k in range(1, self.nx)]
        self.y_masks = [2 * side * k for k in range(1, self.ny)]
        self.z_masks = list(range(1, n_z))
        self.square = self.nx == self.ny == 2 and n_z == 4

    def bind(self):
        self.my_dp = lax.axis_index("dp").astype(jnp.int32)
        self.my_z = lax.axis_index("fsdp").astype(jnp.int32)
        self.me = lax.axis_index(AXES).astype(jnp.int32)

    def over_dp(self, value, mask):
        return lax.ppermute(value, "dp", [(i, i ^ mask) for i in range(self.n_dp)])

    def crossed(self, value, even_mask, odd_mask):
        pairs = [(i, i ^ (odd_mask if i % 2 else even_mask)) for i in range(self.n_dp)]
        return lax.ppermute(value, "dp", pairs)

    def over_z(self, value, mask):
        return lax.ppermute(value, "fsdp", [(i, i ^ mask) for i in range(self.n_z)])


class Clock:
    def __init__(self):
        self.last = ()

    def gate(self, *values):
        held = lax.optimization_barrier(tuple(values) + self.last)[: len(values)]
        return held if len(values) > 1 else held[0]

    def tick(self, *values):
        self.last = values


class Lines:
    def __init__(self, grid, clock, shards):
        self.grid, self.clock = grid, clock
        self.block = shards[0].shape[0]
        self.parts, blocks = [], []
        at = 0
        for shard in shards:
            height, cols = shard.shape
            count = height // self.block
            blocks += [shard[k * self.block : (k + 1) * self.block] for k in range(count)]
            self.parts.append((at, count, cols))
            at += count * cols
        self.shard = jnp.concatenate(blocks, axis=1) if len(blocks) > 1 else blocks[0]

    def step0(self):
        self.held = self.clock.gate(self.shard)
        self.far = [m for m in self.grid.z_masks if m % 2 == 0]
        self.coming = [self.grid.over_z(self.held, m) for m in self.far]

    def step1(self):
        *got, held = self.clock.gate(*self.coming, self.held)
        self.held = jnp.concatenate([held, *got], 0)
        self.clock.tick(self.held)
        self.coming = self.grid.over_z(self.held, 1)

    def step2(self):
        got, held = self.clock.gate(self.coming, self.held)
        z_marks = [0] + self.far
        z_marks += [m ^ 1 for m in z_marks]
        joined = []
        for at, count, cols in self.parts:
            cut = slice(at, at + count * cols)
            joined.append(jnp.concatenate([held[:, cut], got[:, cut]], 0))
        self.clock.tick(*joined)
        return [
            Gather(self.grid, self.clock, rows, z_marks, self.block, count, cols)
            for rows, (_, count, cols) in zip(joined, self.parts)
        ]


class Gather:
    def __init__(self, grid, clock, rows, z_marks, block, count, cols):
        self.grid, self.clock, self.rows = grid, clock, rows
        self.z_marks, self.block, self.count, self.cols = z_marks, block, count, cols
        self.pieces = []

    def take(self, rows, even_mask, odd_mask):
        self.pieces.append((rows, even_mask, odd_mask))
        self.pieces.append((self.grid.over_dp(rows, 1), odd_mask ^ 1, even_mask ^ 1))

    def step0(self):
        grid = self.grid
        (x,), (y,) = grid.x_masks, grid.y_masks
        rows = self.clock.gate(self.rows)
        self.first = grid.crossed(rows, x, y)
        self.second = grid.crossed(rows, y, x)
        self.take(rows, 0, 0)

    def step1(self):
        grid = self.grid
        (x,), (y,) = grid.x_masks, grid.y_masks
        first = self.clock.gate(self.first)
        self.clock.tick(first)
        self.third = grid.crossed(first, y, x)
        self.take(first, x, y)

    def step2(self):
        (x,), (y,) = self.grid.x_masks, self.grid.y_masks
        second = self.clock.gate(self.second)
        self.clock.tick(second)
        self.take(second, y, x)

    def step3(self):
        (x,), (y,) = self.grid.x_masks, self.grid.y_masks
        third = self.clock.gate(self.third)
        self.clock.tick(third)
        self.take(third, x ^ y, x ^ y)

    def done(self, cuts=()):
        grid, block, count = self.grid, self.block, self.count
        pieces, z_marks = self.pieces, self.z_marks
        owners = grid.n_dp * grid.n_z
        edges = [0, *cuts, self.cols]
        spans = list(zip(edges[:-1], edges[1:]))
        copies = owners * count * len(spans)

        def kernel(me_ref, *refs):
            sources = refs[: len(pieces)]
            results = refs[len(pieces) : len(pieces) + len(spans)]
            sems = refs[-1]
            me = me_ref[0]
            odd = (me // grid.n_z) % 2 == 1
            started = []
            for source, (_, even_mask, odd_mask) in zip(sources, pieces):
                mask = jnp.where(odd, jnp.int32(odd_mask), jnp.int32(even_mask))
                for at, z in enumerate(z_marks):
                    owner = lax.bitwise_xor(me, mask * grid.n_z + z)
                    for k in range(count):
                        to = pl.multiple_of((owner * count + k) * block, block)
                        for result, (lo, hi) in zip(results, spans):
                            copy = pltpu.make_async_copy(
                                source.at[
                                    pl.ds(at * block, block), pl.ds(k * self.cols + lo, hi - lo)
                                ],
                                result.at[pl.ds(to, block)],
                                sems.at[len(started)],
                            )
                            copy.start()
                            started.append(copy)
            for copy in started:
                copy.wait()

        arrays = self.clock.gate(*[v for v, _, _ in pieces])
        rows = owners * count * block
        full = pl.pallas_call(
            kernel,
            out_shape=[jax.ShapeDtypeStruct((rows, hi - lo), BF16) for lo, hi in spans],
            grid_spec=pltpu.PrefetchScalarGridSpec(
                num_scalar_prefetch=1,
                grid=(),
                in_specs=[pl.BlockSpec(memory_space=pl.ANY)] * len(pieces),
                out_specs=[pl.BlockSpec(memory_space=pltpu.VMEM)] * len(spans),
                scratch_shapes=[pltpu.SemaphoreType.DMA((copies,))],
            ),
            compiler_params=pltpu.CompilerParams(vmem_limit_bytes=20 << 20),
            cost_estimate=pl.CostEstimate(flops=0, bytes_accessed=0, transcendentals=0),
            name="assemble",
        )(grid.me.reshape(1), *arrays)
        self.clock.tick(*full)
        return full


class PlainLines:
    def __init__(self, grid, clock, shards):
        self.shards = shards

    def step0(self):
        pass

    step1 = step0

    def step2(self):
        return [PlainGather(v) for v in self.shards]


class PlainGather:
    def __init__(self, shard):
        self.full = lax.all_gather(shard, AXES, axis=0, tiled=True)

    def step0(self):
        pass

    step1 = step2 = step3 = step0

    def done(self, cuts=()):
        edges = [0, *cuts, self.full.shape[1]]
        return [self.full[:, lo:hi] for lo, hi in zip(edges[:-1], edges[1:])]


def make_lines(grid, clock, *shards):
    plain = shards[0].shape[0] % 16 or not grid.square
    kind = PlainLines if plain else Lines
    return kind(grid, clock, shards)


def contract_rows(left, right):
    return lax.dot_general(left, right, (((0,), (0,)), ((), ())), preferred_element_type=F32)


def back_dot(grad_rows, weight):
    return lax.dot_general(grad_rows, weight, (((1,), (1,)), ((), ())), preferred_element_type=F32)


def pick(array, index):
    return lax.dynamic_index_in_dim(array, index, 0, keepdims=False)


def total_of(base, parts):
    for part in parts:
        base = base + part.astype(F32)
    return base


class Scatter:
    places = 4

    def __init__(self, grid, clock, left, right):
        self.grid, self.clock, self.left, self.right = grid, clock, left, right
        self.chunk = left.shape[1] // grid.n_dp
        self.cols = right.shape[1]
        once = pl.Buffered(1)
        self.whole = pl.BlockSpec(
            (self.chunk, self.cols), lambda j, dp: (0, 0), pipeline_mode=once
        )
        self.rows = pl.BlockSpec(right.shape, lambda j, dp: (0, 0), pipeline_mode=once)

    def shape(self, dtype):
        return jax.ShapeDtypeStruct((self.chunk, self.cols), dtype)

    def call(self, kernel, other, ins, dtypes):
        tokens = self.left.shape[0]

        def place(j, dp):
            a, b = j // 2, j % 2
            odd = (dp[0] + other) % 2
            mask = jnp.where(odd == 1, 2 * a + 4 * b, 4 * a + 2 * b)
            return 0, lax.bitwise_xor(dp[0], mask + other)

        left, right, *ins = self.clock.gate(self.left, self.right, *ins)
        return pl.pallas_call(
            kernel,
            out_shape=[self.shape(d) for d in dtypes],
            grid_spec=pltpu.PrefetchScalarGridSpec(
                num_scalar_prefetch=1,
                grid=(self.places,),
                in_specs=[
                    pl.BlockSpec((tokens, self.chunk), place),
                    self.rows,
                    *[self.whole for _ in ins],
                ],
                out_specs=[self.whole for _ in dtypes],
            ),
            compiler_params=pltpu.CompilerParams(vmem_limit_bytes=18 << 20),
            cost_estimate=pl.CostEstimate(flops=0, bytes_accessed=0, transcendentals=0),
            name="outer",
        )(self.grid.my_dp.reshape(1), left, right, *ins)

    def across(self):
        def kernel(dp_ref, left, right, *outs):
            term = contract_rows(left[...], right[...]).astype(BF16)
            for k, out in enumerate(outs):

                @pl.when(pl.program_id(0) == k)
                def _(out=out):
                    out[...] = term

        sends = self.call(kernel, 1, (), [BF16] * self.places)
        self.clock.tick(*sends)
        self.got = [self.grid.over_dp(v, 1) for v in sends]

    def first(self):
        grid, places = self.grid, self.places
        (x,), (y,) = grid.x_masks, grid.y_masks

        def kernel(dp_ref, left, right, *refs):
            term = contract_rows(left[...], right[...])
            for k, (got, out) in enumerate(zip(refs[:places], refs[places:])):

                @pl.when(pl.program_id(0) == k)
                def _(got=got, out=out):
                    out[...] = (term + got[...].astype(F32)).astype(out.dtype)

        keep, pass_on, aside, onward = self.call(kernel, 0, self.got, [F32, F32, BF16, BF16])
        self.clock.tick(aside, onward)
        self.keep, self.pass_on = keep, pass_on
        self.got = grid.crossed(onward, y, x)
        self.aside = grid.crossed(aside, y, x)

    def second(self):
        (x,), (y,) = self.grid.x_masks, self.grid.y_masks
        got, pass_on = self.clock.gate(self.got, self.pass_on)
        send = (pass_on + got.astype(F32)).astype(BF16)
        self.clock.tick(send)
        self.got = self.grid.crossed(send, x, y)

    def third(self):
        grid = self.grid
        got, aside, keep = self.clock.gate(self.got, self.aside, self.keep)
        lines = total_of(keep, [got, aside]).reshape(2, 2, -1, self.cols)
        odd = grid.my_z % 2
        send = lax.dynamic_index_in_dim(lines, 1 - odd, 1, keepdims=False).astype(BF16)
        self.keep = lax.dynamic_index_in_dim(lines, odd, 1, keepdims=False)
        self.clock.tick(send)
        self.got = grid.over_z(send, 1)

    def fourth(self):
        grid = self.grid
        got, keep = self.clock.gate(self.got, self.keep)
        held = keep + got.astype(F32)
        pair = grid.my_z // 2
        send = pick(held, 1 - pair).astype(BF16)
        self.keep = pick(held, pair)
        self.clock.tick(send)
        self.got = grid.over_z(send, 2)

    def done(self):
        got, keep = self.clock.gate(self.got, self.keep)
        out = keep + got.astype(F32)
        self.clock.tick(out)
        return out


class PlainScatter:
    def __init__(self, grid, clock, left, right):
        self.left, self.right = left, right

    def across(self):
        term = contract_rows(self.left, self.right)
        self.out = lax.psum_scatter(term, AXES, scatter_dimension=0, tiled=True)

    def first(self):
        pass

    second = third = fourth = first

    def done(self):
        return self.out


def make_scatter(grid, clock, left, right):
    plain = (left.shape[1] // grid.n_dp) % 128 or not grid.square
    kind = PlainScatter if plain else Scatter
    return kind(grid, clock, left, right)


def lookup(small_table, index_rows):
    matches = index_rows[:, None] == jnp.arange(small_table.shape[0], dtype=jnp.int32)[None, :]
    return jnp.sum(jnp.where(matches, small_table[None, :], 0), axis=1)


def rank_among(group_label, order_key):
    earlier = (group_label[None, :] == group_label[:, None]) & (
        order_key[None, :] < order_key[:, None]
    )
    return jnp.sum(earlier.astype(jnp.int32), axis=1)


def routing(lengths, deal_order, devices, row_count, device):
    slot_count = deal_order.shape[0]
    slot_ids = jnp.arange(slot_count, dtype=jnp.int32)
    starts = jnp.cumsum(lengths) - lengths
    slot_of = jnp.sum(
        jnp.where(deal_order[None, :] == slot_ids[:, None], slot_ids[None, :], 0), axis=1
    )
    slot_lengths = lookup(lengths, deal_order)
    local_rows = jnp.arange(row_count, dtype=jnp.int32)
    token_index = local_rows * devices + device
    sequence = jnp.sum((starts[None, :] <= token_index[:, None]).astype(jnp.int32), axis=1) - 1
    slot_index = lookup(slot_of, sequence)
    target = slot_index // 2
    send_rank = rank_among(target, local_rows)
    first_len = lax.dynamic_index_in_dim(slot_lengths, 2 * device, 0, False)
    second = local_rows >= first_len
    first_seq = lax.dynamic_index_in_dim(deal_order, 2 * device, 0, False)
    second_seq = lax.dynamic_index_in_dim(deal_order, 2 * device + 1, 0, False)
    sequence_here = jnp.where(second, second_seq, first_seq)
    position = local_rows - jnp.where(second, first_len, 0)
    source_token = lookup(starts, sequence_here) + position
    source = source_token % devices
    take_rank = rank_among(source, source_token)
    return target, send_rank, source, take_rank, first_len.reshape(1)


def head_probs(query, key, first_len):
    rows = query.shape[0]
    scores = back_dot(query, key) * (HEAD_DIM**-0.5)
    q_at = lax.broadcasted_iota(jnp.int32, (rows, rows), 0)
    k_at = lax.broadcasted_iota(jnp.int32, (rows, rows), 1)
    allowed = (k_at <= q_at) & ((q_at < first_len) | (k_at >= first_len))
    masked = jnp.where(allowed, scores, -1000000000.0)
    exps = jnp.exp(masked - jnp.max(masked, axis=-1, keepdims=True))
    return exps / jnp.sum(exps, axis=-1, keepdims=True)


def attend(first_len, mixed_b):
    rows, width = mixed_b.shape[0], mixed_b.shape[1] // 3
    pairs = width // (2 * HEAD_DIM)

    def kernel(first_ref, query, key, value, out):
        left = lax.broadcasted_iota(jnp.int32, (rows, 2 * HEAD_DIM), 1) < HEAD_DIM
        found = []
        for one in (left, ~left):
            q = jnp.where(one, query[...], jnp.zeros((), BF16))
            probs = head_probs(q, key[...], first_ref[0]).astype(BF16)
            found.append(jnp.dot(probs, value[...], preferred_element_type=F32))
        out[...] = jnp.where(left, *found).astype(BF16)

    def part(k):
        return pl.BlockSpec((rows, 2 * HEAD_DIM), lambda h, first: (0, k * pairs + h))

    return pl.pallas_call(
        kernel,
        out_shape=jax.ShapeDtypeStruct((rows, width), BF16),
        grid_spec=pltpu.PrefetchScalarGridSpec(
            num_scalar_prefetch=1,
            grid=(pairs,),
            in_specs=[part(0), part(1), part(2)],
            out_specs=part(0),
        ),
        compiler_params=pltpu.CompilerParams(vmem_limit_bytes=16 << 20),
        cost_estimate=pl.CostEstimate(flops=0, bytes_accessed=0, transcendentals=0),
        name="attend",
    )(first_len, mixed_b, mixed_b, mixed_b)


def attend_back(first_len, mixed_b, grad_att_b):
    rows, width = grad_att_b.shape
    pairs = width // (2 * HEAD_DIM)

    def kernel(first_ref, query, key, value, grad, out, sums):
        h = pl.program_id(0)
        scale = HEAD_DIM**-0.5
        left = lax.broadcasted_iota(jnp.int32, (rows, 2 * HEAD_DIM), 1) < HEAD_DIM
        none = jnp.zeros((), BF16)
        results = ([], [], [])
        for one in (left, ~left):
            q = jnp.where(one, query[...], none)
            g = jnp.where(one, grad[...], none)
            probs = head_probs(q, key[...], first_ref[0])
            grad_probs = back_dot(g, value[...])
            dots = jnp.sum(probs * grad_probs, axis=-1, keepdims=True)
            grad_scores = (probs * (grad_probs - dots)).astype(BF16)
            results[0].append(jnp.dot(grad_scores, key[...], preferred_element_type=F32) * scale)
            results[1].append(contract_rows(grad_scores, q) * scale)
            results[2].append(contract_rows(probs.astype(BF16), g))
        for k, both in enumerate(results):
            block = jnp.where(left, *both).astype(BF16)
            at = pl.multiple_of(k * width + h * 2 * HEAD_DIM, 2 * HEAD_DIM)
            out[:, pl.ds(at, 2 * HEAD_DIM)] = block
            total = jnp.sum(block.astype(F32), axis=0, keepdims=True)
            sums[:, pl.ds(at, 2 * HEAD_DIM)] = total

    def part(k):
        return pl.BlockSpec((rows, 2 * HEAD_DIM), lambda h, first: (0, k * pairs + h))

    return pl.pallas_call(
        kernel,
        out_shape=[
            jax.ShapeDtypeStruct((rows, 3 * width), BF16),
            jax.ShapeDtypeStruct((1, 3 * width), F32),
        ],
        grid_spec=pltpu.PrefetchScalarGridSpec(
            num_scalar_prefetch=1,
            grid=(pairs,),
            in_specs=[part(0), part(1), part(2), part(0)],
            out_specs=[
                pl.BlockSpec((rows, 3 * width), lambda h, first: (0, 0)),
                pl.BlockSpec((1, 3 * width), lambda h, first: (0, 0)),
            ],
        ),
        compiler_params=pltpu.CompilerParams(vmem_limit_bytes=16 << 20),
        cost_estimate=pl.CostEstimate(flops=0, bytes_accessed=0, transcendentals=0),
        name="attend_back",
    )(first_len, mixed_b, mixed_b, mixed_b, grad_att_b)


def standardize(values):
    centered = values - jnp.mean(values, axis=-1, keepdims=True)
    scale = lax.rsqrt(jnp.mean(centered * centered, axis=-1, keepdims=True) + EPSILON)
    return centered * scale, scale


def standardize_back(grad, unit, scale):
    return scale * (
        grad
        - jnp.mean(grad, axis=-1, keepdims=True)
        - unit * jnp.mean(grad * unit, axis=-1, keepdims=True)
    )


def col_sum(values):
    return jnp.sum(values.astype(F32), axis=0)


def on_device(
    n_dp,
    n_z,
    rows_in,
    cotangent,
    lengths,
    deal_order,
    w_qkv,
    b_query,
    b_value,
    w_out,
    b_out,
    gain_one,
    shift_one,
    w_up,
    b_up,
    w_down,
    b_down,
    gain_two,
    shift_two,
):
    grid = Grid(n_dp, n_z)
    grid.bind()
    clock = Clock()
    devices = n_dp * n_z
    row_count, _, width = rows_in.shape
    hidden = w_up.shape[1]
    share = width // devices

    early = make_lines(grid, clock, jnp.concatenate([w_qkv, w_out], axis=1))
    late = make_lines(grid, clock, w_up, w_down)
    early.step0()

    target, send_rank, source, take_rank, first_len = routing(
        lengths, deal_order, devices, row_count, grid.me
    )
    slot_rows = row_count // devices + 1
    in_rows = -(-(slot_rows + 1) // 8) * 8
    out_rows = -(-(2 * slot_rows + 1) // 8) * 8

    def selector(owner, rank, block_rows):
        at = (owner * block_rows + rank)[:, None]
        slot_ids = jnp.arange(devices * block_rows, dtype=jnp.int32)[None, :]
        return (at == slot_ids).astype(BF16)

    def is_row(block_rows, row):
        slot_ids = jnp.arange(devices * block_rows, dtype=jnp.int32)
        return (slot_ids % block_rows == row)[:, None]

    to_slots = selector(target, send_rank, in_rows)
    from_slots = selector(source, take_rank, in_rows)
    first_half = selector(source, take_rank, out_rows)
    second_half = selector(source, take_rank + slot_rows, out_rows)
    take_both = jnp.concatenate(
        [selector(target, send_rank, out_rows), selector(target, send_rank + slot_rows, out_rows)]
    )

    def swap(block):
        shape = block.shape
        block = block.reshape(devices, -1, width)
        block = lax.all_to_all(block, AXES, split_axis=0, concat_axis=0, tiled=True)
        return block.reshape(shape)

    small = jnp.concatenate(
        [b_query, b_value, b_out, gain_one, shift_one, b_down, gain_two, shift_two, b_up]
    )
    small = jnp.pad(small, (0, width - small.shape[0]))
    block = contract_rows(to_slots, rows_in.reshape(row_count, width))
    block = jnp.where(is_row(in_rows, slot_rows), small[None, :], block.astype(BF16))
    clock.tick(block)
    early.step1()
    late.step0()
    (attn,) = early.step2()
    arrived = swap(clock.gate(block))
    attn.step0()
    late.step1()
    attn.step1()
    attn.step2()
    up, down = late.step2()
    up.step0()
    attn.step3()
    arrived = clock.gate(arrived)
    inputs = jnp.dot(from_slots, arrived, preferred_element_type=F32)
    small_all = arrived.reshape(devices, in_rows, width)[:, slot_rows].astype(F32)
    vectors = [small_all[:, k * share : (k + 1) * share].reshape(width) for k in range(8)]
    bq, bv, bo, g1, s1, bd, g2, s2 = vectors
    bu = small_all[:, 8 * share : 8 * share + hidden // devices].reshape(hidden)
    unit_one, scale_one = standardize(inputs)
    normed_one_b = (unit_one * g1 + s1).astype(BF16)
    clock.tick(normed_one_b)
    full_qkv, full_out = attn.done((3 * width,))
    mixed = jnp.dot(clock.gate(normed_one_b), full_qkv, preferred_element_type=F32)
    mixed_b = (mixed + jnp.concatenate([bq, jnp.zeros_like(bq), bv])).astype(BF16)
    attended_b = attend(first_len, mixed_b)
    clock.tick(attended_b)
    up.step1()
    up.step2()
    down.step0()
    attended_b, cot_rows = clock.gate(attended_b, cotangent)
    cot_block = contract_rows(to_slots, cot_rows.reshape(row_count, width)).astype(BF16)
    clock.tick(cot_block)
    arrived_cot = swap(cot_block)
    hidden_one = inputs + jnp.dot(attended_b, full_out, preferred_element_type=F32) + bo
    unit_two, scale_two = standardize(hidden_one)
    normed_two_b = (unit_two * g2 + s2).astype(BF16)
    clock.tick(normed_two_b)

    up.step3()
    (full_up,) = up.done()
    pre_act = jnp.dot(clock.gate(normed_two_b), full_up, preferred_element_type=F32) + bu
    half_cdf = 0.5 * (1.0 + lax.erf(pre_act * (0.5**0.5)))
    activation_b = (pre_act * half_cdf).astype(BF16)
    density = jnp.exp(-0.5 * pre_act * pre_act) * ((2.0 * jnp.pi) ** -0.5)
    slope = half_cdf + pre_act * density
    clock.tick(activation_b, slope)

    arrived_cot = clock.gate(arrived_cot)
    grad_m_b = jnp.dot(from_slots, arrived_cot, preferred_element_type=F32).astype(BF16)
    clock.tick(grad_m_b)
    term_b_down = col_sum(grad_m_b)
    for_down = make_scatter(grid, clock, activation_b, grad_m_b)
    for_down.across()
    down.step1()
    down.step2()
    for_down.first()
    down.step3()
    (full_down,) = down.done()
    grad_pre_b = (back_dot(clock.gate(grad_m_b), full_down) * slope).astype(BF16)
    clock.tick(grad_pre_b)
    term_b_up = col_sum(grad_pre_b)
    for_up = make_scatter(grid, clock, normed_two_b, grad_pre_b)
    for_up.across()
    for_down.second()

    grad_normed_two = back_dot(clock.gate(grad_pre_b), full_up)
    term_g2 = col_sum(grad_normed_two * unit_two)
    term_s2 = col_sum(grad_normed_two)
    grad_hidden = grad_m_b.astype(F32) + standardize_back(grad_normed_two * g2, unit_two, scale_two)
    grad_branch_b = grad_hidden.astype(BF16)
    clock.tick(grad_branch_b)
    term_b_out = col_sum(grad_branch_b)
    for_out = make_scatter(grid, clock, attended_b, grad_branch_b)
    for_out.across()
    for_up.first()
    grad_att_b = back_dot(clock.gate(grad_branch_b), full_out).astype(BF16)
    clock.tick(grad_att_b)
    for_out.first()
    grad_mixed_b, term_mixed = attend_back(first_len, mixed_b, clock.gate(grad_att_b))
    clock.tick(grad_mixed_b)
    term_mixed = term_mixed[0]
    for_qkv = make_scatter(grid, clock, normed_one_b, grad_mixed_b)
    for_qkv.across()
    for_down.third()
    for_up.second()
    for_out.second()

    grad_normed_one = back_dot(clock.gate(grad_mixed_b), full_qkv)
    term_g1 = col_sum(grad_normed_one * unit_one)
    term_s1 = col_sum(grad_normed_one)
    grad_inputs = grad_hidden + standardize_back(grad_normed_one * g1, unit_one, scale_one)
    grad_inputs_b = grad_inputs.astype(BF16)
    clock.tick(grad_inputs_b)
    for_qkv.first()

    result = jnp.dot(clock.gate(activation_b), full_down, preferred_element_type=F32)
    result_b = (hidden_one + result + bd).astype(BF16)
    terms = [term_mixed[:width], term_mixed[2 * width :], term_b_out, term_g1, term_s1]
    terms += [term_b_down, term_g2, term_s2, term_b_up]
    terms = jnp.concatenate([v.reshape(devices, -1) for v in terms], axis=1)
    count = terms.shape[1]
    top = lax.reduce_precision(terms, 8, 7)
    small_back = jnp.concatenate([top, terms - top], axis=1).astype(BF16)
    small_back = jnp.pad(small_back, ((0, 0), (0, width - 2 * count)))
    small_back = jnp.broadcast_to(small_back[:, None], (devices, out_rows, width))
    block = contract_rows(first_half, result_b) + contract_rows(second_half, grad_inputs_b)
    last_row = is_row(out_rows, 2 * slot_rows)
    block = jnp.where(last_row, small_back.reshape(-1, width), block.astype(BF16))
    clock.tick(block)
    returned = swap(block)

    for_up.third()
    for_qkv.second()
    for_down.fourth()
    for_out.third()
    for_up.fourth()
    for_qkv.third()
    for_out.fourth()
    for_qkv.fourth()
    grad_w_down = for_down.done()
    grad_w_up = for_up.done()
    grad_w_out = for_out.done()
    returned = clock.gate(returned)
    placed = jnp.dot(take_both, returned, preferred_element_type=F32).astype(BF16)
    rows_out, grad_rows = placed[:row_count], placed[row_count:]
    sums = jnp.sum(
        returned.reshape(devices, out_rows, width)[:, 2 * slot_rows].astype(F32), axis=0
    )
    clock.tick(placed)
    grad_w_qkv = for_qkv.done()

    sums = sums[:count] + sums[count : 2 * count]
    cut = [sums[k * share : (k + 1) * share] for k in range(8)]
    grad_bq, grad_bv, grad_bo, grad_g1, grad_s1, grad_bd, grad_g2, grad_s2 = cut
    grad_bu = sums[8 * share :]
    return (
        rows_out.reshape(row_count, 1, width),
        grad_rows.reshape(row_count, 1, width),
        grad_w_qkv,
        grad_bq,
        grad_bv,
        grad_w_out,
        grad_bo,
        grad_g1,
        grad_s1,
        grad_w_up,
        grad_bu,
        grad_w_down,
        grad_bd,
        grad_g2,
        grad_s2,
    )


def solution(mesh):
    n_dp, n_z = mesh.shape["dp"], mesh.shape["fsdp"]
    rows, vec, mat = P(None, AXES, None), P(AXES), P(AXES, None)

    def run(*args):
        return on_device(n_dp, n_z, *args)

    return jax.shard_map(
        run,
        mesh=mesh,
        in_specs=(rows, rows, P(), P())
        + (mat, vec, vec, mat, vec, vec, vec, mat, vec, mat, vec, vec, vec),
        out_specs=(rows, rows, mat, vec, vec, mat, vec, vec, vec, mat, vec, mat, vec, vec, vec),
        check_vma=False,
    )
```

```python
import jax
import jax.numpy as jnp
from jax import lax
from jax.experimental import pallas as pl
from jax.experimental.pallas import tpu as pltpu
from jax.sharding import PartitionSpec as P

HEADS = 16
HEAD_DIM = 64
EPSILON = 1e-05
AXES = ("dp", "fsdp")
BF16 = jnp.bfloat16
F32 = jnp.float32


class Grid:
    def __init__(self, n_dp, n_z):
        self.n_dp, self.n_z = n_dp, n_z
        side = 1
        while side * side * 2 < n_dp:
            side *= 2
        self.nx, self.ny = side, n_dp // (2 * side)
        self.x_masks = [2 * k for k in range(1, self.nx)]
        self.y_masks = [2 * side * k for k in range(1, self.ny)]
        self.z_masks = list(range(1, n_z))
        self.square = self.nx == self.ny == 2 and n_z == 4

    def bind(self):
        self.my_dp = lax.axis_index("dp").astype(jnp.int32)
        self.my_z = lax.axis_index("fsdp").astype(jnp.int32)
        self.me = lax.axis_index(AXES).astype(jnp.int32)

    def over_dp(self, value, mask):
        return lax.ppermute(value, "dp", [(i, i ^ mask) for i in range(self.n_dp)])

    def crossed(self, value, even_mask, odd_mask):
        pairs = [(i, i ^ (odd_mask if i % 2 else even_mask)) for i in range(self.n_dp)]
        return lax.ppermute(value, "dp", pairs)

    def over_z(self, value, mask):
        return lax.ppermute(value, "fsdp", [(i, i ^ mask) for i in range(self.n_z)])


class Clock:
    def __init__(self):
        self.last = ()

    def gate(self, *values):
        held = lax.optimization_barrier(tuple(values) + self.last)[: len(values)]
        return held if len(values) > 1 else held[0]

    def tick(self, *values):
        self.last = values


class Lines:
    def __init__(self, grid, clock, shards):
        self.grid, self.clock = grid, clock
        self.block = shards[0].shape[0]
        self.parts, blocks = [], []
        at = 0
        for shard in shards:
            height, cols = shard.shape
            count = height // self.block
            blocks += [shard[k * self.block : (k + 1) * self.block] for k in range(count)]
            self.parts.append((at, count, cols))
            at += count * cols
        self.shard = jnp.concatenate(blocks, axis=1) if len(blocks) > 1 else blocks[0]

    def step0(self):
        self.held = self.clock.gate(self.shard)
        self.far = [m for m in self.grid.z_masks if m % 2 == 0]
        self.coming = [self.grid.over_z(self.held, m) for m in self.far]

    def step1(self):
        *got, held = self.clock.gate(*self.coming, self.held)
        self.held = jnp.concatenate([held, *got], 0)
        self.clock.tick(self.held)
        self.coming = self.grid.over_z(self.held, 1)

    def step2(self):
        got, held = self.clock.gate(self.coming, self.held)
        z_marks = [0] + self.far
        z_marks += [m ^ 1 for m in z_marks]
        joined = []
        for at, count, cols in self.parts:
            cut = slice(at, at + count * cols)
            joined.append(jnp.concatenate([held[:, cut], got[:, cut]], 0))
        self.clock.tick(*joined)
        return [
            Gather(self.grid, self.clock, rows, z_marks, self.block, count, cols)
            for rows, (_, count, cols) in zip(joined, self.parts)
        ]


class Gather:
    def __init__(self, grid, clock, rows, z_marks, block, count, cols):
        self.grid, self.clock, self.rows = grid, clock, rows
        self.z_marks, self.block, self.count, self.cols = z_marks, block, count, cols
        self.pieces = []

    def take(self, rows, even_mask, odd_mask):
        self.pieces.append((rows, even_mask, odd_mask))
        self.pieces.append((self.grid.over_dp(rows, 1), odd_mask ^ 1, even_mask ^ 1))

    def step0(self):
        grid = self.grid
        (x,), (y,) = grid.x_masks, grid.y_masks
        rows = self.clock.gate(self.rows)
        self.first = grid.crossed(rows, x, y)
        self.second = grid.crossed(rows, y, x)
        self.take(rows, 0, 0)

    def step1(self):
        grid = self.grid
        (x,), (y,) = grid.x_masks, grid.y_masks
        first = self.clock.gate(self.first)
        self.clock.tick(first)
        self.third = grid.crossed(first, y, x)
        self.take(first, x, y)

    def step2(self):
        (x,), (y,) = self.grid.x_masks, self.grid.y_masks
        second = self.clock.gate(self.second)
        self.clock.tick(second)
        self.take(second, y, x)

    def step3(self):
        (x,), (y,) = self.grid.x_masks, self.grid.y_masks
        third = self.clock.gate(self.third)
        self.clock.tick(third)
        self.take(third, x ^ y, x ^ y)

    def done(self, cuts=()):
        grid, block, count = self.grid, self.block, self.count
        pieces, z_marks = self.pieces, self.z_marks
        owners = grid.n_dp * grid.n_z
        edges = [0, *cuts, self.cols]
        spans = list(zip(edges[:-1], edges[1:]))
        copies = owners * count * len(spans)

        def kernel(me_ref, *refs):
            sources = refs[: len(pieces)]
            results = refs[len(pieces) : len(pieces) + len(spans)]
            sems = refs[-1]
            me = me_ref[0]
            odd = (me // grid.n_z) % 2 == 1
            started = []
            for source, (_, even_mask, odd_mask) in zip(sources, pieces):
                mask = jnp.where(odd, jnp.int32(odd_mask), jnp.int32(even_mask))
                for at, z in enumerate(z_marks):
                    owner = lax.bitwise_xor(me, mask * grid.n_z + z)
                    for k in range(count):
                        to = pl.multiple_of((owner * count + k) * block, block)
                        for result, (lo, hi) in zip(results, spans):
                            copy = pltpu.make_async_copy(
                                source.at[
                                    pl.ds(at * block, block), pl.ds(k * self.cols + lo, hi - lo)
                                ],
                                result.at[pl.ds(to, block)],
                                sems.at[len(started)],
                            )
                            copy.start()
                            started.append(copy)
            for copy in started:
                copy.wait()

        arrays = self.clock.gate(*[v for v, _, _ in pieces])
        rows = owners * count * block
        full = pl.pallas_call(
            kernel,
            out_shape=[jax.ShapeDtypeStruct((rows, hi - lo), BF16) for lo, hi in spans],
            grid_spec=pltpu.PrefetchScalarGridSpec(
                num_scalar_prefetch=1,
                grid=(),
                in_specs=[pl.BlockSpec(memory_space=pl.ANY)] * len(pieces),
                out_specs=[pl.BlockSpec(memory_space=pltpu.VMEM)] * len(spans),
                scratch_shapes=[pltpu.SemaphoreType.DMA((copies,))],
            ),
            compiler_params=pltpu.CompilerParams(vmem_limit_bytes=20 << 20),
            cost_estimate=pl.CostEstimate(flops=0, bytes_accessed=0, transcendentals=0),
            name="assemble",
        )(grid.me.reshape(1), *arrays)
        self.clock.tick(*full)
        return full


class PlainLines:
    def __init__(self, grid, clock, shards):
        self.shards = shards

    def step0(self):
        pass

    step1 = step0

    def step2(self):
        return [PlainGather(v) for v in self.shards]


class PlainGather:
    def __init__(self, shard):
        self.full = lax.all_gather(shard, AXES, axis=0, tiled=True)

    def step0(self):
        pass

    step1 = step2 = step3 = step0

    def done(self, cuts=()):
        edges = [0, *cuts, self.full.shape[1]]
        return [self.full[:, lo:hi] for lo, hi in zip(edges[:-1], edges[1:])]


def make_lines(grid, clock, *shards):
    plain = shards[0].shape[0] % 16 or not grid.square
    kind = PlainLines if plain else Lines
    return kind(grid, clock, shards)


def contract_rows(left, right):
    return lax.dot_general(left, right, (((0,), (0,)), ((), ())), preferred_element_type=F32)


def back_dot(grad_rows, weight):
    return lax.dot_general(grad_rows, weight, (((1,), (1,)), ((), ())), preferred_element_type=F32)


def pick(array, index):
    return lax.dynamic_index_in_dim(array, index, 0, keepdims=False)


def total_of(base, parts):
    for part in parts:
        base = base + part.astype(F32)
    return base


class Scatter:
    places = 4

    def __init__(self, grid, clock, left, right):
        self.grid, self.clock, self.left, self.right = grid, clock, left, right
        self.chunk = left.shape[1] // grid.n_dp
        self.cols = right.shape[1]
        once = pl.Buffered(1)
        self.whole = pl.BlockSpec(
            (self.chunk, self.cols), lambda j, dp: (0, 0), pipeline_mode=once
        )
        self.rows = pl.BlockSpec(right.shape, lambda j, dp: (0, 0), pipeline_mode=once)

    def shape(self, dtype):
        return jax.ShapeDtypeStruct((self.chunk, self.cols), dtype)

    def call(self, kernel, other, ins, dtypes):
        tokens = self.left.shape[0]

        def place(j, dp):
            a, b = j // 2, j % 2
            odd = (dp[0] + other) % 2
            mask = jnp.where(odd == 1, 2 * a + 4 * b, 4 * a + 2 * b)
            return 0, lax.bitwise_xor(dp[0], mask + other)

        left, right, *ins = self.clock.gate(self.left, self.right, *ins)
        return pl.pallas_call(
            kernel,
            out_shape=[self.shape(d) for d in dtypes],
            grid_spec=pltpu.PrefetchScalarGridSpec(
                num_scalar_prefetch=1,
                grid=(self.places,),
                in_specs=[
                    pl.BlockSpec((tokens, self.chunk), place),
                    self.rows,
                    *[self.whole for _ in ins],
                ],
                out_specs=[self.whole for _ in dtypes],
            ),
            compiler_params=pltpu.CompilerParams(vmem_limit_bytes=18 << 20),
            cost_estimate=pl.CostEstimate(flops=0, bytes_accessed=0, transcendentals=0),
            name="outer",
        )(self.grid.my_dp.reshape(1), left, right, *ins)

    def across(self):
        def kernel(dp_ref, left, right, *outs):
            term = contract_rows(left[...], right[...]).astype(BF16)
            for k, out in enumerate(outs):

                @pl.when(pl.program_id(0) == k)
                def _(out=out):
                    out[...] = term

        sends = self.call(kernel, 1, (), [BF16] * self.places)
        self.clock.tick(*sends)
        self.got = [self.grid.over_dp(v, 1) for v in sends]

    def first(self):
        grid, places = self.grid, self.places
        (x,), (y,) = grid.x_masks, grid.y_masks

        def kernel(dp_ref, left, right, *refs):
            term = contract_rows(left[...], right[...])
            for k, (got, out) in enumerate(zip(refs[:places], refs[places:])):

                @pl.when(pl.program_id(0) == k)
                def _(got=got, out=out):
                    out[...] = (term + got[...].astype(F32)).astype(out.dtype)

        keep, pass_on, aside, onward = self.call(kernel, 0, self.got, [F32, F32, BF16, BF16])
        self.clock.tick(aside, onward)
        self.keep, self.pass_on = keep, pass_on
        self.got = grid.crossed(onward, y, x)
        self.aside = grid.crossed(aside, y, x)

    def second(self):
        (x,), (y,) = self.grid.x_masks, self.grid.y_masks
        got, self.aside, pass_on = self.clock.gate(self.got, self.aside, self.pass_on)
        send = (pass_on + got.astype(F32)).astype(BF16)
        self.clock.tick(send)
        self.got = self.grid.crossed(send, x, y)

    def third(self):
        grid = self.grid
        got, keep = self.clock.gate(self.got, self.keep)
        lines = total_of(keep, [got, self.aside]).reshape(2, 2, -1, self.cols)
        odd = grid.my_z % 2
        send = lax.dynamic_index_in_dim(lines, 1 - odd, 1, keepdims=False).astype(BF16)
        self.keep = lax.dynamic_index_in_dim(lines, odd, 1, keepdims=False)
        self.clock.tick(send)
        self.got = grid.over_z(send, 1)

    def fourth(self):
        grid = self.grid
        got, keep = self.clock.gate(self.got, self.keep)
        held = keep + got.astype(F32)
        pair = grid.my_z // 2
        send = pick(held, 1 - pair).astype(BF16)
        self.keep = pick(held, pair)
        self.clock.tick(send)
        self.got = grid.over_z(send, 2)

    def done(self):
        got, keep = self.clock.gate(self.got, self.keep)
        out = keep + got.astype(F32)
        self.clock.tick(out)
        return out


class PlainScatter:
    def __init__(self, grid, clock, left, right):
        self.left, self.right = left, right

    def across(self):
        term = contract_rows(self.left, self.right)
        self.out = lax.psum_scatter(term, AXES, scatter_dimension=0, tiled=True)

    def first(self):
        pass

    second = third = fourth = first

    def done(self):
        return self.out


def make_scatter(grid, clock, left, right):
    plain = (left.shape[1] // grid.n_dp) % 128 or not grid.square
    kind = PlainScatter if plain else Scatter
    return kind(grid, clock, left, right)


def lookup(small_table, index_rows):
    matches = index_rows[:, None] == jnp.arange(small_table.shape[0], dtype=jnp.int32)[None, :]
    return jnp.sum(jnp.where(matches, small_table[None, :], 0), axis=1)


def rank_among(group_label, order_key):
    earlier = (group_label[None, :] == group_label[:, None]) & (
        order_key[None, :] < order_key[:, None]
    )
    return jnp.sum(earlier.astype(jnp.int32), axis=1)


def routing(lengths, deal_order, devices, row_count, device):
    slot_count = deal_order.shape[0]
    slot_ids = jnp.arange(slot_count, dtype=jnp.int32)
    starts = jnp.cumsum(lengths) - lengths
    slot_of = jnp.sum(
        jnp.where(deal_order[None, :] == slot_ids[:, None], slot_ids[None, :], 0), axis=1
    )
    slot_lengths = lookup(lengths, deal_order)
    local_rows = jnp.arange(row_count, dtype=jnp.int32)
    token_index = local_rows * devices + device
    sequence = jnp.sum((starts[None, :] <= token_index[:, None]).astype(jnp.int32), axis=1) - 1
    slot_index = lookup(slot_of, sequence)
    target = slot_index // 2
    send_rank = rank_among(target, local_rows)
    first_len = lax.dynamic_index_in_dim(slot_lengths, 2 * device, 0, False)
    second = local_rows >= first_len
    first_seq = lax.dynamic_index_in_dim(deal_order, 2 * device, 0, False)
    second_seq = lax.dynamic_index_in_dim(deal_order, 2 * device + 1, 0, False)
    sequence_here = jnp.where(second, second_seq, first_seq)
    position = local_rows - jnp.where(second, first_len, 0)
    source_token = lookup(starts, sequence_here) + position
    source = source_token % devices
    take_rank = rank_among(source, source_token)
    return target, send_rank, source, take_rank, first_len.reshape(1)


def head_probs(query, key, first_len):
    rows = query.shape[0]
    scores = back_dot(query, key) * (HEAD_DIM**-0.5)
    q_at = lax.broadcasted_iota(jnp.int32, (rows, rows), 0)
    k_at = lax.broadcasted_iota(jnp.int32, (rows, rows), 1)
    allowed = (k_at <= q_at) & ((q_at < first_len) | (k_at >= first_len))
    masked = jnp.where(allowed, scores, -1000000000.0)
    exps = jnp.exp(masked - jnp.max(masked, axis=-1, keepdims=True))
    return exps / jnp.sum(exps, axis=-1, keepdims=True)


def attend(first_len, mixed_b):
    rows, width = mixed_b.shape[0], mixed_b.shape[1] // 3
    pairs = width // (2 * HEAD_DIM)

    def kernel(first_ref, query, key, value, out):
        left = lax.broadcasted_iota(jnp.int32, (rows, 2 * HEAD_DIM), 1) < HEAD_DIM
        found = []
        for one in (left, ~left):
            q = jnp.where(one, query[...], jnp.zeros((), BF16))
            probs = head_probs(q, key[...], first_ref[0]).astype(BF16)
            found.append(jnp.dot(probs, value[...], preferred_element_type=F32))
        out[...] = jnp.where(left, *found).astype(BF16)

    def part(k):
        return pl.BlockSpec((rows, 2 * HEAD_DIM), lambda h, first: (0, k * pairs + h))

    return pl.pallas_call(
        kernel,
        out_shape=jax.ShapeDtypeStruct((rows, width), BF16),
        grid_spec=pltpu.PrefetchScalarGridSpec(
            num_scalar_prefetch=1,
            grid=(pairs,),
            in_specs=[part(0), part(1), part(2)],
            out_specs=part(0),
        ),
        compiler_params=pltpu.CompilerParams(vmem_limit_bytes=16 << 20),
        cost_estimate=pl.CostEstimate(flops=0, bytes_accessed=0, transcendentals=0),
        name="attend",
    )(first_len, mixed_b, mixed_b, mixed_b)


def attend_back(first_len, mixed_b, grad_att_b):
    rows, width = grad_att_b.shape
    pairs = width // (2 * HEAD_DIM)

    def kernel(first_ref, query, key, value, grad, out, sums):
        h = pl.program_id(0)
        scale = HEAD_DIM**-0.5
        left = lax.broadcasted_iota(jnp.int32, (rows, 2 * HEAD_DIM), 1) < HEAD_DIM
        none = jnp.zeros((), BF16)
        results = ([], [], [])
        for one in (left, ~left):
            q = jnp.where(one, query[...], none)
            g = jnp.where(one, grad[...], none)
            probs = head_probs(q, key[...], first_ref[0])
            grad_probs = back_dot(g, value[...])
            dots = jnp.sum(probs * grad_probs, axis=-1, keepdims=True)
            grad_scores = (probs * (grad_probs - dots)).astype(BF16)
            results[0].append(jnp.dot(grad_scores, key[...], preferred_element_type=F32) * scale)
            results[1].append(contract_rows(grad_scores, q) * scale)
            results[2].append(contract_rows(probs.astype(BF16), g))
        for k, both in enumerate(results):
            block = jnp.where(left, *both).astype(BF16)
            at = pl.multiple_of(k * width + h * 2 * HEAD_DIM, 2 * HEAD_DIM)
            out[:, pl.ds(at, 2 * HEAD_DIM)] = block
            total = jnp.sum(block.astype(F32), axis=0, keepdims=True)
            sums[:, pl.ds(at, 2 * HEAD_DIM)] = total

    def part(k):
        return pl.BlockSpec((rows, 2 * HEAD_DIM), lambda h, first: (0, k * pairs + h))

    return pl.pallas_call(
        kernel,
        out_shape=[
            jax.ShapeDtypeStruct((rows, 3 * width), BF16),
            jax.ShapeDtypeStruct((1, 3 * width), F32),
        ],
        grid_spec=pltpu.PrefetchScalarGridSpec(
            num_scalar_prefetch=1,
            grid=(pairs,),
            in_specs=[part(0), part(1), part(2), part(0)],
            out_specs=[
                pl.BlockSpec((rows, 3 * width), lambda h, first: (0, 0)),
                pl.BlockSpec((1, 3 * width), lambda h, first: (0, 0)),
            ],
        ),
        compiler_params=pltpu.CompilerParams(vmem_limit_bytes=16 << 20),
        cost_estimate=pl.CostEstimate(flops=0, bytes_accessed=0, transcendentals=0),
        name="attend_back",
    )(first_len, mixed_b, mixed_b, mixed_b, grad_att_b)


def gelu_back(grad_b, weight, slope):
    rows, width = grad_b.shape
    hidden = weight.shape[0]
    tile = min(1024, hidden)

    def kernel(grad, weight, slope, out, sums):
        block = (back_dot(grad[...], weight[...]) * slope[...]).astype(BF16)
        out[...] = block
        sums[...] = jnp.sum(block.astype(F32), axis=0, keepdims=True)

    return pl.pallas_call(
        kernel,
        out_shape=[
            jax.ShapeDtypeStruct((rows, hidden), BF16),
            jax.ShapeDtypeStruct((1, hidden), F32),
        ],
        grid=(hidden // tile,),
        in_specs=[
            pl.BlockSpec((rows, width), lambda j: (0, 0)),
            pl.BlockSpec((tile, width), lambda j: (j, 0)),
            pl.BlockSpec((rows, tile), lambda j: (0, j)),
        ],
        out_specs=[
            pl.BlockSpec((rows, tile), lambda j: (0, j)),
            pl.BlockSpec((1, tile), lambda j: (0, j)),
        ],
        compiler_params=pltpu.CompilerParams(vmem_limit_bytes=14 << 20),
        cost_estimate=pl.CostEstimate(flops=0, bytes_accessed=0, transcendentals=0),
        name="gelu_back",
    )(grad_b, weight, slope)


def norm_back(grad_b, weight, unit, gain, scale, passed, keep_wide):
    rows, depth = grad_b.shape
    width = weight.shape[0]
    tile = 1024
    steps = depth // tile

    def kernel(grad, weight, unit, gain, scale, passed, *refs):
        outs, total = refs[:-1], refs[-1]
        step = pl.program_id(0)
        part = back_dot(grad[...], weight[...])

        @pl.when(step == 0)
        def _():
            total[...] = part

        @pl.when(step > 0)
        def _():
            total[...] += part

        @pl.when(step == steps - 1)
        def _():
            whole, u = total[...], unit[...]
            normed = whole * gain[...]
            out = passed[...].astype(F32) + standardize_back(normed, u, scale[...])
            out_b = out.astype(BF16)
            outs[0][...] = out_b
            outs[1][0:1] = jnp.sum(whole * u, axis=0, keepdims=True)
            outs[1][1:2] = jnp.sum(whole, axis=0, keepdims=True)
            outs[1][2:3] = jnp.sum(out_b.astype(F32), axis=0, keepdims=True)
            if keep_wide:
                outs[2][...] = out

    def once(shape):
        return pl.BlockSpec(shape, lambda j: (0, 0), pipeline_mode=pl.Buffered(1))

    shapes = [((rows, width), BF16), ((8, width), F32)]
    shapes += [((rows, width), F32)] if keep_wide else []
    return pl.pallas_call(
        kernel,
        out_shape=[jax.ShapeDtypeStruct(*s) for s in shapes],
        grid=(steps,),
        in_specs=[
            pl.BlockSpec((rows, tile), lambda j: (0, j)),
            pl.BlockSpec((width, tile), lambda j: (0, j)),
            once((rows, width)),
            once((1, width)),
            once((rows, 1)),
            once((rows, width)),
        ],
        out_specs=[once(shape) for shape, _ in shapes],
        scratch_shapes=[pltpu.VMEM((rows, width), F32)],
        compiler_params=pltpu.CompilerParams(vmem_limit_bytes=16 << 20),
        cost_estimate=pl.CostEstimate(flops=0, bytes_accessed=0, transcendentals=0),
        name="norm_back",
    )(grad_b, weight, unit, gain[None, :], scale, passed)


def standardize(values):
    centered = values - jnp.mean(values, axis=-1, keepdims=True)
    scale = lax.rsqrt(jnp.mean(centered * centered, axis=-1, keepdims=True) + EPSILON)
    return centered * scale, scale


def standardize_back(grad, unit, scale):
    return scale * (
        grad
        - jnp.mean(grad, axis=-1, keepdims=True)
        - unit * jnp.mean(grad * unit, axis=-1, keepdims=True)
    )


def col_sum(values):
    return jnp.sum(values.astype(F32), axis=0)


def on_device(
    n_dp,
    n_z,
    rows_in,
    cotangent,
    lengths,
    deal_order,
    w_qkv,
    b_query,
    b_value,
    w_out,
    b_out,
    gain_one,
    shift_one,
    w_up,
    b_up,
    w_down,
    b_down,
    gain_two,
    shift_two,
):
    grid = Grid(n_dp, n_z)
    grid.bind()
    clock = Clock()
    devices = n_dp * n_z
    row_count, _, width = rows_in.shape
    hidden = w_up.shape[1]
    share = width // devices

    early = make_lines(grid, clock, jnp.concatenate([w_qkv, w_out], axis=1))
    late = make_lines(grid, clock, w_up, w_down)
    early.step0()

    target, send_rank, source, take_rank, first_len = routing(
        lengths, deal_order, devices, row_count, grid.me
    )
    slot_rows = row_count // devices + 1
    in_rows = slot_rows + 1
    out_rows = 2 * slot_rows + 1

    def selector(owner, rank, block_rows):
        at = (owner * block_rows + rank)[:, None]
        slot_ids = jnp.arange(devices * block_rows, dtype=jnp.int32)[None, :]
        return (at == slot_ids).astype(BF16)

    def is_row(block_rows, row):
        slot_ids = jnp.arange(devices * block_rows, dtype=jnp.int32)
        return (slot_ids % block_rows == row)[:, None]

    to_slots = selector(target, send_rank, in_rows)
    from_slots = selector(source, take_rank, in_rows)

    def both_of(owner, rank):
        at = owner * out_rows + rank
        return jnp.concatenate([at, at + slot_rows])

    out_slot_ids = jnp.arange(devices * out_rows, dtype=jnp.int32)
    take_both = (both_of(target, send_rank)[:, None] == out_slot_ids[None, :]).astype(BF16)
    send_both = (out_slot_ids[:, None] == both_of(source, take_rank)[None, :]).astype(BF16)

    def swap(block):
        shape = block.shape
        block = block.reshape(devices, -1, 128)
        block = lax.all_to_all(block, AXES, split_axis=0, concat_axis=0, tiled=True)
        return block.reshape(shape)

    small = jnp.zeros((width,), BF16)
    at = 0
    for vector in (b_query, b_value, b_out, gain_one, shift_one, b_down, gain_two, shift_two, b_up):
        small += jnp.pad(vector, (at, width - at - vector.shape[0]))
        at += vector.shape[0]
    early.step1()
    late.step0()
    to_slots, own_rows = clock.gate(to_slots, rows_in)
    block = contract_rows(to_slots, own_rows.reshape(row_count, width))
    block = jnp.where(is_row(in_rows, slot_rows), small[None, :], block.astype(BF16))
    clock.tick(block)
    (attn,) = early.step2()
    arrived = swap(clock.gate(block))
    attn.step0()
    late.step1()
    attn.step1()
    attn.step2()
    up, down = late.step2()
    up.step0()
    attn.step3()
    arrived = clock.gate(arrived)
    inputs = jnp.dot(from_slots, arrived, preferred_element_type=F32)
    small_all = arrived.reshape(devices, in_rows, width)[:, slot_rows].astype(F32)
    vectors = [small_all[:, k * share : (k + 1) * share].reshape(width) for k in range(8)]
    bq, bv, bo, g1, s1, bd, g2, s2 = vectors
    bu = small_all[:, 8 * share : 8 * share + hidden // devices].reshape(hidden)
    unit_one, scale_one = standardize(inputs)
    normed_one_b = (unit_one * g1 + s1).astype(BF16)
    clock.tick(normed_one_b)
    take_both, send_both = clock.gate(take_both, send_both)
    clock.tick(take_both, send_both)
    full_qkv, full_out = attn.done((3 * width,))
    mixed = jnp.dot(clock.gate(normed_one_b), full_qkv, preferred_element_type=F32)
    mixed_b = (mixed + jnp.concatenate([bq, jnp.zeros_like(bq), bv])).astype(BF16)
    attended_b = attend(first_len, mixed_b)
    clock.tick(attended_b)
    up.step1()
    up.step2()
    down.step0()
    attended_b, cot_rows = clock.gate(attended_b, cotangent)
    cot_block = contract_rows(to_slots, cot_rows.reshape(row_count, width)).astype(BF16)
    clock.tick(cot_block)
    arrived_cot = swap(cot_block)
    hidden_one = inputs + jnp.dot(attended_b, full_out, preferred_element_type=F32) + bo
    unit_two, scale_two = standardize(hidden_one)
    normed_two_b = (unit_two * g2 + s2).astype(BF16)
    clock.tick(normed_two_b)

    up.step3()
    (full_up,) = up.done()
    pre_act = jnp.dot(clock.gate(normed_two_b), full_up, preferred_element_type=F32) + bu
    half_cdf = 0.5 * (1.0 + lax.erf(pre_act * (0.5**0.5)))
    activation_b = (pre_act * half_cdf).astype(BF16)
    density = jnp.exp(-0.5 * pre_act * pre_act) * ((2.0 * jnp.pi) ** -0.5)
    slope = half_cdf + pre_act * density
    clock.tick(activation_b, slope)

    arrived_cot = clock.gate(arrived_cot)
    grad_m_b = jnp.dot(from_slots, arrived_cot, preferred_element_type=F32).astype(BF16)
    clock.tick(grad_m_b)
    term_b_down = col_sum(grad_m_b)
    for_down = make_scatter(grid, clock, activation_b, grad_m_b)
    for_down.across()
    down.step1()
    down.step2()
    for_down.first()
    down.step3()
    (full_down,) = down.done()
    grad_pre_b, term_b_up = gelu_back(clock.gate(grad_m_b), full_down, slope)
    clock.tick(grad_pre_b)
    for_up = make_scatter(grid, clock, normed_two_b, grad_pre_b)
    for_up.across()

    grad_branch_b, sums_two, grad_hidden = norm_back(
        clock.gate(grad_pre_b), full_up, unit_two, g2, scale_two, grad_m_b, True
    )
    term_g2, term_s2, term_b_out = sums_two[0], sums_two[1], sums_two[2]
    clock.tick(grad_branch_b)
    for_out = make_scatter(grid, clock, attended_b, grad_branch_b)
    for_out.across()
    for_up.first()
    grad_att_b = back_dot(clock.gate(grad_branch_b), full_out).astype(BF16)
    clock.tick(grad_att_b)
    for_out.first()
    for_down.second()
    grad_mixed_b, term_mixed = attend_back(first_len, mixed_b, clock.gate(grad_att_b))
    clock.tick(grad_mixed_b)
    term_mixed = term_mixed[0]
    for_qkv = make_scatter(grid, clock, normed_one_b, grad_mixed_b)
    for_qkv.across()
    for_down.third()

    grad_inputs_b, sums_one = norm_back(
        clock.gate(grad_mixed_b), full_qkv, unit_one, g1, scale_one, grad_hidden, False
    )
    term_g1, term_s1 = sums_one[0], sums_one[1]
    clock.tick(grad_inputs_b)
    for_qkv.first()
    for_up.second()
    result = jnp.dot(clock.gate(activation_b), full_down, preferred_element_type=F32)
    result_b = (hidden_one + result + bd).astype(BF16)
    terms = [term_mixed[:width], term_mixed[2 * width :], term_b_out, term_g1, term_s1]
    terms += [term_b_down, term_g2, term_s2, term_b_up]
    terms = jnp.concatenate([v.reshape(devices, -1) for v in terms], axis=1)
    count = terms.shape[1]
    top = lax.reduce_precision(terms, 8, 7)
    small_back = jnp.concatenate([top, terms - top], axis=1).astype(BF16)
    small_back = jnp.pad(small_back, ((0, 0), (0, width - 2 * count)))
    small_back = jnp.broadcast_to(small_back[:, None], (devices, out_rows, width))
    both = jnp.concatenate([result_b, grad_inputs_b], axis=0)
    block = jnp.dot(send_both, both, preferred_element_type=F32)
    last_row = is_row(out_rows, 2 * slot_rows)
    block = jnp.where(last_row, small_back.reshape(-1, width), block.astype(BF16))
    clock.tick(block)
    returned = swap(block)

    for_out.second()
    for_up.third()
    for_down.fourth()
    for_qkv.second()
    for_out.third()
    for_qkv.third()
    for_up.fourth()
    for_out.fourth()
    for_qkv.fourth()
    grad_w_down = for_down.done()
    grad_w_up = for_up.done()
    grad_w_out = for_out.done()
    returned = clock.gate(returned)
    placed = jnp.dot(take_both, returned, preferred_element_type=F32).astype(BF16)
    rows_out, grad_rows = placed[:row_count], placed[row_count:]
    sums = jnp.sum(
        returned.reshape(devices, out_rows, width)[:, 2 * slot_rows].astype(F32), axis=0
    )
    clock.tick(placed)
    grad_w_qkv = for_qkv.done()

    sums = sums[:count] + sums[count : 2 * count]
    cut = [sums[k * share : (k + 1) * share] for k in range(8)]
    grad_bq, grad_bv, grad_bo, grad_g1, grad_s1, grad_bd, grad_g2, grad_s2 = cut
    grad_bu = sums[8 * share :]
    return (
        rows_out.reshape(row_count, 1, width),
        grad_rows.reshape(row_count, 1, width),
        grad_w_qkv,
        grad_bq,
        grad_bv,
        grad_w_out,
        grad_bo,
        grad_g1,
        grad_s1,
        grad_w_up,
        grad_bu,
        grad_w_down,
        grad_bd,
        grad_g2,
        grad_s2,
    )


def solution(mesh):
    n_dp, n_z = mesh.shape["dp"], mesh.shape["fsdp"]
    rows, vec, mat = P(None, AXES, None), P(AXES), P(AXES, None)

    def run(*args):
        return on_device(n_dp, n_z, *args)

    return jax.shard_map(
        run,
        mesh=mesh,
        in_specs=(rows, rows, P(), P())
        + (mat, vec, vec, mat, vec, vec, vec, mat, vec, mat, vec, vec, vec),
        out_specs=(rows, rows, mat, vec, vec, mat, vec, vec, vec, mat, vec, mat, vec, vec, vec),
        check_vma=False,
    )
```

```python
import jax
import jax.numpy as jnp
from jax import lax
from jax.experimental import pallas as pl
from jax.experimental.pallas import tpu as pltpu
from jax.sharding import PartitionSpec as P

HEADS = 16
HEAD_DIM = 64
EPSILON = 1e-05
AXES = ("dp", "fsdp")
BF16 = jnp.bfloat16
F32 = jnp.float32


class Grid:
    def __init__(self, n_dp, n_z):
        self.n_dp, self.n_z = n_dp, n_z
        side = 1
        while side * side * 2 < n_dp:
            side *= 2
        self.nx, self.ny = side, n_dp // (2 * side)
        self.x_masks = [2 * k for k in range(1, self.nx)]
        self.y_masks = [2 * side * k for k in range(1, self.ny)]
        self.z_masks = list(range(1, n_z))
        self.square = self.nx == self.ny == 2 and n_z == 4

    def bind(self):
        self.my_dp = lax.axis_index("dp").astype(jnp.int32)
        self.my_z = lax.axis_index("fsdp").astype(jnp.int32)
        self.me = lax.axis_index(AXES).astype(jnp.int32)

    def over_dp(self, value, mask):
        return lax.ppermute(value, "dp", [(i, i ^ mask) for i in range(self.n_dp)])

    def crossed(self, value, even_mask, odd_mask):
        pairs = [(i, i ^ (odd_mask if i % 2 else even_mask)) for i in range(self.n_dp)]
        return lax.ppermute(value, "dp", pairs)

    def over_z(self, value, mask):
        return lax.ppermute(value, "fsdp", [(i, i ^ mask) for i in range(self.n_z)])


class Clock:
    def __init__(self):
        self.last = ()

    def gate(self, *values):
        held = lax.optimization_barrier(tuple(values) + self.last)[: len(values)]
        return held if len(values) > 1 else held[0]

    def tick(self, *values):
        self.last = values


class Lines:
    def __init__(self, grid, clock, shards):
        self.grid, self.clock = grid, clock
        self.block = shards[0].shape[0]
        self.parts, blocks = [], []
        at = 0
        for shard in shards:
            height, cols = shard.shape
            count = height // self.block
            blocks += [shard[k * self.block : (k + 1) * self.block] for k in range(count)]
            self.parts.append((at, count, cols))
            at += count * cols
        self.shard = jnp.concatenate(blocks, axis=1) if len(blocks) > 1 else blocks[0]

    def step0(self):
        self.held = self.clock.gate(self.shard)
        self.far = [m for m in self.grid.z_masks if m % 2 == 0]
        self.coming = [self.grid.over_z(self.held, m) for m in self.far]

    def step1(self):
        *got, held = self.clock.gate(*self.coming, self.held)
        self.held = jnp.concatenate([held, *got], 0)
        self.clock.tick(self.held)
        self.coming = self.grid.over_z(self.held, 1)

    def step2(self):
        got, held = self.clock.gate(self.coming, self.held)
        z_marks = [0] + self.far
        z_marks += [m ^ 1 for m in z_marks]
        joined = []
        for at, count, cols in self.parts:
            cut = slice(at, at + count * cols)
            joined.append(jnp.concatenate([held[:, cut], got[:, cut]], 0))
        self.clock.tick(*joined)
        return [
            Gather(self.grid, self.clock, rows, z_marks, self.block, count, cols)
            for rows, (_, count, cols) in zip(joined, self.parts)
        ]


class Gather:
    def __init__(self, grid, clock, rows, z_marks, block, count, cols):
        self.grid, self.clock, self.rows = grid, clock, rows
        self.z_marks, self.block, self.count, self.cols = z_marks, block, count, cols
        self.pieces = []

    def take(self, rows, even_mask, odd_mask):
        self.pieces.append((rows, even_mask, odd_mask))
        self.crossing = (self.grid.over_dp(rows, 1), odd_mask ^ 1, even_mask ^ 1)

    def land(self, coming):
        rows, crossed = self.clock.gate(coming, self.crossing[0])
        self.pieces.append((crossed, *self.crossing[1:]))
        self.clock.tick(rows)
        return rows

    def step0(self):
        grid = self.grid
        (x,), (y,) = grid.x_masks, grid.y_masks
        rows = self.clock.gate(self.rows)
        self.first = grid.crossed(rows, x, y)
        self.second = grid.crossed(rows, y, x)
        self.take(rows, 0, 0)

    def step1(self):
        grid = self.grid
        (x,), (y,) = grid.x_masks, grid.y_masks
        first = self.land(self.first)
        self.third = grid.crossed(first, y, x)
        self.take(first, x, y)

    def step2(self):
        (x,), (y,) = self.grid.x_masks, self.grid.y_masks
        self.take(self.land(self.second), y, x)

    def step3(self):
        (x,), (y,) = self.grid.x_masks, self.grid.y_masks
        self.take(self.land(self.third), x ^ y, x ^ y)
        self.pieces.append(self.crossing)

    def done(self, cuts=()):
        grid, block, count = self.grid, self.block, self.count
        pieces, z_marks = self.pieces, self.z_marks
        owners = grid.n_dp * grid.n_z
        edges = [0, *cuts, self.cols]
        spans = list(zip(edges[:-1], edges[1:]))
        copies = owners * count * len(spans)

        def kernel(me_ref, *refs):
            sources = refs[: len(pieces)]
            results = refs[len(pieces) : len(pieces) + len(spans)]
            sems = refs[-1]
            me = me_ref[0]
            odd = (me // grid.n_z) % 2 == 1
            started = []
            for source, (_, even_mask, odd_mask) in zip(sources, pieces):
                mask = jnp.where(odd, jnp.int32(odd_mask), jnp.int32(even_mask))
                for at, z in enumerate(z_marks):
                    owner = lax.bitwise_xor(me, mask * grid.n_z + z)
                    for k in range(count):
                        to = pl.multiple_of((owner * count + k) * block, block)
                        for result, (lo, hi) in zip(results, spans):
                            copy = pltpu.make_async_copy(
                                source.at[
                                    pl.ds(at * block, block), pl.ds(k * self.cols + lo, hi - lo)
                                ],
                                result.at[pl.ds(to, block)],
                                sems.at[len(started)],
                            )
                            copy.start()
                            started.append(copy)
            for copy in started:
                copy.wait()

        arrays = self.clock.gate(*[v for v, _, _ in pieces])
        rows = owners * count * block
        full = pl.pallas_call(
            kernel,
            out_shape=[jax.ShapeDtypeStruct((rows, hi - lo), BF16) for lo, hi in spans],
            grid_spec=pltpu.PrefetchScalarGridSpec(
                num_scalar_prefetch=1,
                grid=(),
                in_specs=[pl.BlockSpec(memory_space=pl.ANY)] * len(pieces),
                out_specs=[pl.BlockSpec(memory_space=pltpu.VMEM)] * len(spans),
                scratch_shapes=[pltpu.SemaphoreType.DMA((copies,))],
            ),
            compiler_params=pltpu.CompilerParams(vmem_limit_bytes=10 << 20),
            cost_estimate=pl.CostEstimate(flops=0, bytes_accessed=0, transcendentals=0),
            name="assemble",
        )(grid.me.reshape(1), *arrays)
        self.clock.tick(*full)
        return full


class PlainLines:
    def __init__(self, grid, clock, shards):
        self.shards = shards

    def step0(self):
        pass

    step1 = step0

    def step2(self):
        return [PlainGather(v) for v in self.shards]


class PlainGather:
    def __init__(self, shard):
        self.full = lax.all_gather(shard, AXES, axis=0, tiled=True)

    def step0(self):
        pass

    step1 = step2 = step3 = step0

    def done(self, cuts=()):
        edges = [0, *cuts, self.full.shape[1]]
        return [self.full[:, lo:hi] for lo, hi in zip(edges[:-1], edges[1:])]


def make_lines(grid, clock, *shards):
    plain = shards[0].shape[0] % 16 or not grid.square
    kind = PlainLines if plain else Lines
    return kind(grid, clock, shards)


def contract_rows(left, right):
    return lax.dot_general(left, right, (((0,), (0,)), ((), ())), preferred_element_type=F32)


def back_dot(grad_rows, weight):
    return lax.dot_general(grad_rows, weight, (((1,), (1,)), ((), ())), preferred_element_type=F32)


def pick(array, index):
    return lax.dynamic_index_in_dim(array, index, 0, keepdims=False)


def total_of(base, parts):
    for part in parts:
        base = base + part.astype(F32)
    return base


class Scatter:
    places = 4

    def __init__(self, grid, clock, lefts, rights):
        self.grid, self.clock, self.lefts, self.rights = grid, clock, lefts, rights
        self.chunk = lefts[0].shape[1] // grid.n_dp
        self.cols = sum(right.shape[1] for right in rights)
        once = pl.Buffered(1)
        self.whole = pl.BlockSpec(
            (self.chunk, self.cols), lambda j, dp: (0, 0), pipeline_mode=once
        )
        self.rows = [
            pl.BlockSpec(right.shape, lambda j, dp: (0, 0), pipeline_mode=once) for right in rights
        ]

    def shape(self, dtype):
        return jax.ShapeDtypeStruct((self.chunk, self.cols), dtype)

    def call(self, kernel, other, ins, shapes, specs):
        tokens, count = self.lefts[0].shape[0], len(self.lefts)

        def place(j, dp):
            a, b = j // 2, j % 2
            odd = (dp[0] + other) % 2
            mask = jnp.where(odd == 1, 2 * a + 4 * b, 4 * a + 2 * b)
            return 0, lax.bitwise_xor(dp[0], mask + other)

        def whole_kernel(dp_ref, *refs):
            lefts, rights, rest = refs[:count], refs[count : 2 * count], refs[2 * count :]
            terms = [contract_rows(a[...], b[...]) for a, b in zip(lefts, rights)]
            kernel(jnp.concatenate(terms, axis=1) if count > 1 else terms[0], *rest)

        ins = self.clock.gate(*self.lefts, *self.rights, *ins)
        return pl.pallas_call(
            whole_kernel,
            out_shape=shapes,
            grid_spec=pltpu.PrefetchScalarGridSpec(
                num_scalar_prefetch=1,
                grid=(self.places,),
                in_specs=[
                    *[pl.BlockSpec((tokens, self.chunk), place) for _ in self.lefts],
                    *self.rows,
                    *[self.whole for _ in ins[2 * count :]],
                ],
                out_specs=specs,
            ),
            compiler_params=pltpu.CompilerParams(vmem_limit_bytes=18 << 20),
            cost_estimate=pl.CostEstimate(flops=0, bytes_accessed=0, transcendentals=0),
            name="outer",
        )(self.grid.my_dp.reshape(1), *ins)

    def across(self):
        def kernel(term, *outs):
            term = term.astype(BF16)
            for k, out in enumerate(outs):

                @pl.when(pl.program_id(0) == k)
                def _(out=out):
                    out[...] = term

        shapes = [self.shape(BF16)] * self.places
        sends = self.call(kernel, 1, (), shapes, [self.whole] * self.places)
        self.clock.tick(*sends)
        self.got = [self.grid.over_dp(v, 1) for v in sends]

    def first(self):
        grid, places = self.grid, self.places
        (x,), (y,) = grid.x_masks, grid.y_masks

        def kernel(term, *refs):
            got, (keep, pass_on, far) = refs[:places], refs[places:]
            outs = (keep, pass_on, far.at[0], far.at[1])
            for k in range(places):

                @pl.when(pl.program_id(0) == k)
                def _(k=k):
                    outs[k][...] = (term + got[k][...].astype(F32)).astype(outs[k].dtype)

        wide = self.shape(F32)
        pair = jax.ShapeDtypeStruct((2, *wide.shape), BF16)
        pair_spec = pl.BlockSpec(
            pair.shape, lambda j, dp: (0, 0, 0), pipeline_mode=pl.Buffered(1)
        )
        keep, pass_on, far = self.call(
            kernel, 0, self.got, [wide, wide, pair], [self.whole, self.whole, pair_spec]
        )
        self.clock.tick(far)
        self.keep, self.pass_on = keep, pass_on
        self.got = grid.crossed(far, y, x)

    def second(self):
        (x,), (y,) = self.grid.x_masks, self.grid.y_masks
        got, pass_on = self.clock.gate(self.got, self.pass_on)
        send = (pass_on + got[1].astype(F32)).astype(BF16)
        self.clock.tick(send)
        self.aside = got[0]
        self.got = self.grid.crossed(send, x, y)

    def third(self):
        grid = self.grid
        got, keep = self.clock.gate(self.got, self.keep)
        lines = total_of(keep, [got, self.aside]).reshape(2, 2, -1, self.cols)
        odd = grid.my_z % 2
        send = lax.dynamic_index_in_dim(lines, 1 - odd, 1, keepdims=False).astype(BF16)
        self.keep = lax.dynamic_index_in_dim(lines, odd, 1, keepdims=False)
        self.clock.tick(send)
        self.got = grid.over_z(send, 1)

    def fourth(self):
        grid = self.grid
        got, keep = self.clock.gate(self.got, self.keep)
        held = keep + got.astype(F32)
        pair = grid.my_z // 2
        send = pick(held, 1 - pair).astype(BF16)
        self.keep = pick(held, pair)
        self.clock.tick(send)
        self.got = grid.over_z(send, 2)

    def done(self):
        got, keep = self.clock.gate(self.got, self.keep)
        outs, at = [], 0
        for right in self.rights:
            cut = slice(at, at + right.shape[1])
            outs.append(keep[:, cut] + got[:, cut].astype(F32))
            at += right.shape[1]
        self.clock.tick(*outs)
        return outs


class PlainScatter:
    def __init__(self, lefts, rights):
        self.terms = [contract_rows(a, b) for a, b in zip(lefts, rights)]

    def across(self):
        pass

    first = second = third = fourth = across

    def done(self):
        return [lax.psum_scatter(t, AXES, scatter_dimension=0, tiled=True) for t in self.terms]


def make_scatter(grid, clock, *pairs):
    lefts, rights = [a for a, _ in pairs], [b for _, b in pairs]
    if (lefts[0].shape[1] // grid.n_dp) % 128 or not grid.square:
        return PlainScatter(lefts, rights)
    return Scatter(grid, clock, lefts, rights)


def lookup(small_table, index_rows):
    matches = index_rows[:, None] == jnp.arange(small_table.shape[0], dtype=jnp.int32)[None, :]
    return jnp.sum(jnp.where(matches, small_table[None, :], 0), axis=1)


def rank_among(group_label, order_key):
    earlier = (group_label[None, :] == group_label[:, None]) & (
        order_key[None, :] < order_key[:, None]
    )
    return jnp.sum(earlier.astype(jnp.int32), axis=1)


def routing(lengths, deal_order, devices, row_count, device):
    slot_count = deal_order.shape[0]
    slot_ids = jnp.arange(slot_count, dtype=jnp.int32)
    starts = jnp.cumsum(lengths) - lengths
    slot_of = jnp.sum(
        jnp.where(deal_order[None, :] == slot_ids[:, None], slot_ids[None, :], 0), axis=1
    )
    slot_lengths = lookup(lengths, deal_order)
    local_rows = jnp.arange(row_count, dtype=jnp.int32)
    token_index = local_rows * devices + device
    sequence = jnp.sum((starts[None, :] <= token_index[:, None]).astype(jnp.int32), axis=1) - 1
    slot_index = lookup(slot_of, sequence)
    target = slot_index // 2
    send_rank = rank_among(target, local_rows)
    first_len = lax.dynamic_index_in_dim(slot_lengths, 2 * device, 0, False)
    second = local_rows >= first_len
    first_seq = lax.dynamic_index_in_dim(deal_order, 2 * device, 0, False)
    second_seq = lax.dynamic_index_in_dim(deal_order, 2 * device + 1, 0, False)
    sequence_here = jnp.where(second, second_seq, first_seq)
    position = local_rows - jnp.where(second, first_len, 0)
    source_token = lookup(starts, sequence_here) + position
    source = source_token % devices
    take_rank = rank_among(source, source_token)
    return target, send_rank, source, take_rank, first_len.reshape(1)


HEADS_AT_ONCE = 4
LANES = HEADS_AT_ONCE * HEAD_DIM


def head_probs(query, key, first_len):
    scores = back_dot(query, key)
    q_at = lax.broadcasted_iota(jnp.int32, scores.shape, 0)
    k_at = lax.broadcasted_iota(jnp.int32, scores.shape, 1)
    allowed = (k_at <= q_at) & ((q_at < first_len) | (k_at >= first_len))
    masked = jnp.where(allowed, scores, -1000000000.0)
    exps = jnp.exp(masked - jnp.max(masked, axis=-1, keepdims=True))
    return exps * (1.0 / jnp.sum(exps, axis=-1, keepdims=True))


def of_heads(rows, parts):
    head = lax.broadcasted_iota(jnp.int32, (rows, LANES), 1) // HEAD_DIM
    whole = parts[0]
    for k in range(1, len(parts)):
        whole = jnp.where(head == k, parts[k], whole)
    return whole


def one_head(values, k):
    head = lax.broadcasted_iota(jnp.int32, values.shape, 1) // HEAD_DIM
    return jnp.where(head == k, values, jnp.zeros((), BF16))


def attend(first_len, mixed_b):
    rows, width = mixed_b.shape[0], mixed_b.shape[1] // 3
    steps = width // LANES

    def kernel(first_ref, query, key, value, out):
        scaled = query[...] * jnp.asarray(HEAD_DIM**-0.5, BF16)
        probs = [
            head_probs(one_head(scaled, k), key[...], first_ref[0]).astype(BF16)
            for k in range(HEADS_AT_ONCE)
        ]
        found = [jnp.dot(p, value[...], preferred_element_type=F32) for p in probs]
        out[...] = of_heads(rows, found).astype(BF16)

    def part(k):
        return pl.BlockSpec((rows, LANES), lambda h, first: (0, k * steps + h))

    return pl.pallas_call(
        kernel,
        out_shape=jax.ShapeDtypeStruct((rows, width), BF16),
        grid_spec=pltpu.PrefetchScalarGridSpec(
            num_scalar_prefetch=1,
            grid=(steps,),
            in_specs=[part(0), part(1), part(2)],
            out_specs=part(0),
        ),
        compiler_params=pltpu.CompilerParams(vmem_limit_bytes=10 << 20),
        cost_estimate=pl.CostEstimate(flops=0, bytes_accessed=0, transcendentals=0),
        name="attend",
    )(first_len, mixed_b, mixed_b, mixed_b)


def attend_back(first_len, mixed_b, grad_att_b):
    rows, width = grad_att_b.shape
    steps = width // LANES

    def kernel(first_ref, query, key, value, grad, out, sums):
        h = pl.program_id(0)
        scaled = query[...] * jnp.asarray(HEAD_DIM**-0.5, BF16)
        to_query, to_key, to_value = [], [], []
        for k in range(HEADS_AT_ONCE):
            q, g = one_head(scaled, k), one_head(grad[...], k)
            probs = head_probs(q, key[...], first_ref[0])
            grad_probs = back_dot(g, value[...])
            dots = jnp.sum(probs * grad_probs, axis=-1, keepdims=True)
            grad_scores = (probs * (grad_probs - dots)).astype(BF16)
            to_query.append(jnp.dot(grad_scores, key[...], preferred_element_type=F32))
            to_key.append(contract_rows(grad_scores, q))
            to_value.append(contract_rows(probs.astype(BF16), g))
        results = (of_heads(rows, to_query) * HEAD_DIM**-0.5, sum(to_key), sum(to_value))
        for k, block in enumerate(results):
            block = block.astype(BF16)
            at = pl.multiple_of(k * width + h * LANES, LANES)
            out[:, pl.ds(at, LANES)] = block
            sums[:, pl.ds(at, LANES)] = jnp.sum(block.astype(F32), axis=0, keepdims=True)

    def part(k):
        return pl.BlockSpec((rows, LANES), lambda h, first: (0, k * steps + h))

    return pl.pallas_call(
        kernel,
        out_shape=[
            jax.ShapeDtypeStruct((rows, 3 * width), BF16),
            jax.ShapeDtypeStruct((1, 3 * width), F32),
        ],
        grid_spec=pltpu.PrefetchScalarGridSpec(
            num_scalar_prefetch=1,
            grid=(steps,),
            in_specs=[part(0), part(1), part(2), part(0)],
            out_specs=[
                pl.BlockSpec((rows, 3 * width), lambda h, first: (0, 0)),
                pl.BlockSpec((1, 3 * width), lambda h, first: (0, 0)),
            ],
        ),
        compiler_params=pltpu.CompilerParams(vmem_limit_bytes=16 << 20),
        cost_estimate=pl.CostEstimate(flops=0, bytes_accessed=0, transcendentals=0),
        name="attend_back",
    )(first_len, mixed_b, mixed_b, mixed_b, grad_att_b)


def gelu_back(grad_b, weight, slope):
    rows, width = grad_b.shape
    hidden = weight.shape[0]
    tile = min(1024, hidden)

    def kernel(grad, weight, slope, out, sums):
        block = (back_dot(grad[...], weight[...]) * slope[...]).astype(BF16)
        out[...] = block
        sums[...] = jnp.sum(block.astype(F32), axis=0, keepdims=True)

    return pl.pallas_call(
        kernel,
        out_shape=[
            jax.ShapeDtypeStruct((rows, hidden), BF16),
            jax.ShapeDtypeStruct((1, hidden), F32),
        ],
        grid=(hidden // tile,),
        in_specs=[
            pl.BlockSpec((rows, width), lambda j: (0, 0)),
            pl.BlockSpec((tile, width), lambda j: (j, 0)),
            pl.BlockSpec((rows, tile), lambda j: (0, j)),
        ],
        out_specs=[
            pl.BlockSpec((rows, tile), lambda j: (0, j)),
            pl.BlockSpec((1, tile), lambda j: (0, j)),
        ],
        compiler_params=pltpu.CompilerParams(vmem_limit_bytes=14 << 20),
        cost_estimate=pl.CostEstimate(flops=0, bytes_accessed=0, transcendentals=0),
        name="gelu_back",
    )(grad_b, weight, slope)


def norm_back(grad_b, weight, unit, gain, scale, passed, keep_wide):
    rows, depth = grad_b.shape
    width = weight.shape[0]
    tile = 1024
    steps = depth // tile

    def kernel(grad, weight, unit, gain, scale, passed, *refs):
        outs, total = refs[:-1], refs[-1]
        step = pl.program_id(0)
        part = back_dot(grad[...], weight[...])

        @pl.when(step == 0)
        def _():
            total[...] = part

        @pl.when(step > 0)
        def _():
            total[...] += part

        @pl.when(step == steps - 1)
        def _():
            whole, u = total[...], unit[...]
            normed = whole * gain[...]
            out = passed[...].astype(F32) + standardize_back(normed, u, scale[...])
            out_b = out.astype(BF16)
            outs[0][...] = out_b
            outs[1][0:1] = jnp.sum(whole * u, axis=0, keepdims=True)
            outs[1][1:2] = jnp.sum(whole, axis=0, keepdims=True)
            outs[1][2:3] = jnp.sum(out_b.astype(F32), axis=0, keepdims=True)
            if keep_wide:
                outs[2][...] = out

    def once(shape):
        return pl.BlockSpec(shape, lambda j: (0, 0), pipeline_mode=pl.Buffered(1))

    shapes = [((rows, width), BF16), ((8, width), F32)]
    shapes += [((rows, width), F32)] if keep_wide else []
    return pl.pallas_call(
        kernel,
        out_shape=[jax.ShapeDtypeStruct(*s) for s in shapes],
        grid=(steps,),
        in_specs=[
            pl.BlockSpec((rows, tile), lambda j: (0, j)),
            pl.BlockSpec((width, tile), lambda j: (0, j)),
            once((rows, width)),
            once((1, width)),
            once((rows, 1)),
            once((rows, width)),
        ],
        out_specs=[once(shape) for shape, _ in shapes],
        scratch_shapes=[pltpu.VMEM((rows, width), F32)],
        compiler_params=pltpu.CompilerParams(vmem_limit_bytes=16 << 20),
        cost_estimate=pl.CostEstimate(flops=0, bytes_accessed=0, transcendentals=0),
        name="norm_back",
    )(grad_b, pltpu.with_memory_space_constraint(weight, pltpu.HBM), unit, gain, scale, passed)


def standardize(values):
    centered = values - jnp.mean(values, axis=-1, keepdims=True)
    scale = lax.rsqrt(jnp.mean(centered * centered, axis=-1, keepdims=True) + EPSILON)
    return centered * scale, scale


def standardize_back(grad, unit, scale):
    return scale * (
        grad
        - jnp.mean(grad, axis=-1, keepdims=True)
        - unit * jnp.mean(grad * unit, axis=-1, keepdims=True)
    )


def col_sum(values):
    return jnp.sum(values.astype(F32), axis=0)


def on_device(
    n_dp,
    n_z,
    rows_in,
    cotangent,
    lengths,
    deal_order,
    w_qkv,
    b_query,
    b_value,
    w_out,
    b_out,
    gain_one,
    shift_one,
    w_up,
    b_up,
    w_down,
    b_down,
    gain_two,
    shift_two,
):
    grid = Grid(n_dp, n_z)
    grid.bind()
    clock = Clock()
    devices = n_dp * n_z
    row_count, _, width = rows_in.shape
    hidden = w_up.shape[1]
    share = width // devices

    early = make_lines(grid, clock, jnp.concatenate([w_qkv, w_out], axis=1))
    middle = make_lines(grid, clock, w_up)
    late = make_lines(grid, clock, w_down)
    early.step0()

    target, send_rank, source, take_rank, first_len = routing(
        lengths, deal_order, devices, row_count, grid.me
    )
    slot_rows = row_count // devices + 1
    in_rows = slot_rows
    out_rows = 2 * slot_rows

    def selector(owner, rank, block_rows):
        at = (owner * block_rows + rank)[:, None]
        slot_ids = jnp.arange(devices * block_rows, dtype=jnp.int32)[None, :]
        return (at == slot_ids).astype(BF16)

    to_slots = selector(target, send_rank, in_rows)
    from_slots = selector(source, take_rank, in_rows)

    def both_of(owner, rank):
        at = owner * out_rows + rank
        return jnp.concatenate([at, at + slot_rows])

    out_slot_ids = jnp.arange(devices * out_rows, dtype=jnp.int32)
    take_both = (both_of(target, send_rank)[:, None] == out_slot_ids[None, :]).astype(BF16)
    send_both = (out_slot_ids[:, None] == both_of(source, take_rank)[None, :]).astype(BF16)

    def swap(block, lines=None):
        block = block.reshape(devices, -1, 128)
        if lines is not None:
            block = jnp.concatenate([block, lines], axis=1)
        block = lax.all_to_all(block, AXES, split_axis=0, concat_axis=0, tiled=True)
        if lines is None:
            return block.reshape(-1, width)
        height = block.shape[1] - lines.shape[1]
        return block[:, :height].reshape(-1, width), block[:, height:]

    vectors = jnp.stack(
        [b_query, b_value, b_out, gain_one, shift_one, b_down, gain_two, shift_two]
    )
    groups = 128 // share
    spot = grid.me % groups
    at_spot = lax.broadcasted_iota(jnp.int32, (8, 128), 1) // share == spot
    vectors = jnp.where(at_spot, jnp.tile(vectors, (1, groups)), jnp.zeros((), BF16))
    bias_groups = max(1, 128 * devices // hidden)
    bias = jnp.tile(b_up[None, :], (1, bias_groups))
    at_bias = lax.broadcasted_iota(jnp.int32, (1, 128), 1) // b_up.shape[0]
    bias = jnp.where(at_bias == grid.me % bias_groups, bias, jnp.zeros((), BF16))
    bias = jnp.pad(bias, ((0, 7), (0, 0)))
    small = jnp.concatenate([vectors, bias], axis=0)
    early.step1()
    middle.step0()
    to_slots, own_rows = clock.gate(to_slots, rows_in)
    block = contract_rows(to_slots, own_rows.reshape(row_count, width))
    block = block.astype(BF16)
    clock.tick(block)
    (attn,) = early.step2()
    attn.step0()
    middle.step1()
    late.step0()
    small = jnp.broadcast_to(small[None], (devices, *small.shape))
    arrived, small_all = swap(clock.gate(block), small)
    attn.step1()
    attn.step2()
    (up,) = middle.step2()
    up.step0()
    late.step1()
    attn.step3()
    arrived, small_all = clock.gate(arrived, small_all)
    inputs = jnp.dot(from_slots, arrived, preferred_element_type=F32)
    lines = jnp.sum(small_all[:, :8].astype(F32).reshape(-1, groups, 8, 128), axis=1)
    bq, bv, bo, g1, s1, bd, g2, s2 = [
        v[None, :] for v in jnp.swapaxes(lines, 0, 1).reshape(8, width)
    ]
    lines = jnp.sum(small_all[:, 8].astype(F32).reshape(-1, bias_groups, 128), axis=1)
    bu = lines.reshape(1, hidden)
    unit_one, scale_one = standardize(inputs)
    normed_one_b = (unit_one * g1 + s1).astype(BF16)
    clock.tick(normed_one_b)
    take_both, send_both = clock.gate(take_both, send_both)
    clock.tick(take_both, send_both)
    (down,) = late.step2()
    up.step1()
    up.step2()
    down.step0()
    full_qkv, full_out = attn.done((3 * width,))
    mixed = jnp.dot(clock.gate(normed_one_b), full_qkv, preferred_element_type=F32)
    mixed_b = (mixed + jnp.concatenate([bq, jnp.zeros_like(bq), bv], axis=1)).astype(BF16)
    attended_b = attend(first_len, mixed_b)
    clock.tick(attended_b)
    up.step3()
    attended_b, cot_rows = clock.gate(attended_b, cotangent)
    cot_block = contract_rows(to_slots, cot_rows.reshape(row_count, width)).astype(BF16)
    clock.tick(cot_block)
    arrived_cot = swap(cot_block)
    hidden_one = inputs + jnp.dot(attended_b, full_out, preferred_element_type=F32) + bo
    unit_two, scale_two = standardize(hidden_one)
    normed_two_b = (unit_two * g2 + s2).astype(BF16)
    clock.tick(normed_two_b)

    (full_up,) = up.done()
    pre_act = jnp.dot(clock.gate(normed_two_b), full_up, preferred_element_type=F32) + bu
    half_cdf = 0.5 * (1.0 + lax.erf(pre_act * (0.5**0.5)))
    activation_b = (pre_act * half_cdf).astype(BF16)
    density = jnp.exp(-0.5 * pre_act * pre_act) * ((2.0 * jnp.pi) ** -0.5)
    slope = half_cdf + pre_act * density
    clock.tick(activation_b, slope)
    down.step1()
    down.step2()

    arrived_cot = clock.gate(arrived_cot)
    grad_m_b = jnp.dot(from_slots, arrived_cot, preferred_element_type=F32)
    grad_m_b = grad_m_b.astype(BF16)
    clock.tick(grad_m_b)
    term_b_down = col_sum(grad_m_b)[None, :]
    for_down = make_scatter(grid, clock, (activation_b, grad_m_b))
    for_down.across()
    for_down.first()
    down.step3()
    (full_down,) = down.done()
    grad_pre_b, term_b_up = gelu_back(clock.gate(grad_m_b), full_down, slope)
    clock.tick(grad_pre_b)
    for_up = make_scatter(grid, clock, (normed_two_b, grad_pre_b))
    for_up.across()

    grad_branch_b, sums_two, grad_hidden = norm_back(
        clock.gate(grad_pre_b), full_up, unit_two, g2, scale_two, grad_m_b, True
    )
    clock.tick(grad_branch_b)
    for_up.first()
    grad_att_b = back_dot(clock.gate(grad_branch_b), full_out).astype(BF16)
    clock.tick(grad_att_b)
    for_down.second()
    grad_mixed_b, term_mixed = attend_back(first_len, mixed_b, clock.gate(grad_att_b))
    clock.tick(grad_mixed_b)
    for_attn = make_scatter(
        grid, clock, (normed_one_b, grad_mixed_b), (attended_b, grad_branch_b)
    )
    for_attn.across()

    grad_inputs_b, sums_one = norm_back(
        clock.gate(grad_mixed_b), full_qkv, unit_one, g1, scale_one, grad_hidden, False
    )
    clock.tick(grad_inputs_b)
    for_attn.first()
    for_up.second()
    for_down.third()
    result = jnp.dot(clock.gate(activation_b), full_down, preferred_element_type=F32)
    result_b = (hidden_one + result + bd).astype(BF16)
    term_mixed, sums_one, sums_two, term_b_down, term_b_up, result_b = clock.gate(
        term_mixed, sums_one, sums_two, term_b_down, term_b_up, result_b
    )
    terms = [term_mixed[:, :width], term_mixed[:, 2 * width :], sums_two[2:3], sums_one[:2]]
    terms = jnp.concatenate([*terms, term_b_down, sums_two[:2]], axis=0).astype(BF16)
    lines = jnp.swapaxes(terms.reshape(8, -1, 128), 0, 1)
    lines = jnp.repeat(lines, groups, axis=0)
    bias = jnp.repeat(term_b_up.astype(BF16).reshape(-1, 1, 128), bias_groups, axis=0)
    lines = jnp.concatenate([lines, jnp.pad(bias, ((0, 0), (0, 7), (0, 0)))], axis=1)
    both = jnp.concatenate([result_b, grad_inputs_b], axis=0)
    block = jnp.dot(send_both, both, preferred_element_type=F32)
    block = block.astype(BF16)
    clock.tick(block)
    returned, small_back = swap(block, lines)

    for_up.third()
    for_down.fourth()
    for_attn.second()
    returned, small_back = clock.gate(returned, small_back)
    clock.tick(returned)
    for_attn.third()
    for_up.fourth()
    for_attn.fourth()
    placed = jnp.dot(take_both, returned, preferred_element_type=F32)
    placed = placed.astype(BF16)
    rows_out, grad_rows = placed[:row_count], placed[row_count:]
    sums = jnp.sum(small_back.astype(F32), axis=0)
    clock.tick(placed)
    (grad_w_down,) = for_down.done()
    (grad_w_up,) = for_up.done()
    grad_w_qkv, grad_w_out = for_attn.done()

    mine = lax.dynamic_slice_in_dim(sums[:8], spot * share, share, axis=1)
    grad_bq, grad_bv, grad_bo, grad_g1, grad_s1, grad_bd, grad_g2, grad_s2 = mine
    bias_width = hidden // devices
    grad_bu = lax.dynamic_slice_in_dim(
        sums[8], (grid.me % bias_groups) * bias_width, bias_width, axis=0
    )
    return (
        rows_out.reshape(row_count, 1, width),
        grad_rows.reshape(row_count, 1, width),
        grad_w_qkv,
        grad_bq,
        grad_bv,
        grad_w_out,
        grad_bo,
        grad_g1,
        grad_s1,
        grad_w_up,
        grad_bu,
        grad_w_down,
        grad_bd,
        grad_g2,
        grad_s2,
    )


def solution(mesh):
    n_dp, n_z = mesh.shape["dp"], mesh.shape["fsdp"]
    rows, vec, mat = P(None, AXES, None), P(AXES), P(AXES, None)

    def run(*args):
        return on_device(n_dp, n_z, *args)

    return jax.shard_map(
        run,
        mesh=mesh,
        in_specs=(rows, rows, P(), P())
        + (mat, vec, vec, mat, vec, vec, vec, mat, vec, mat, vec, vec, vec),
        out_specs=(rows, rows, mat, vec, vec, mat, vec, vec, vec, mat, vec, mat, vec, vec, vec),
        check_vma=False,
    )
```

```python
import jax
import jax.numpy as jnp
from jax import lax
from jax.experimental import pallas as pl
from jax.experimental.pallas import tpu as pltpu
from jax.sharding import PartitionSpec as P

HEADS = 16
HEAD_DIM = 64
EPSILON = 1e-05
AXES = ("dp", "fsdp")
BF16 = jnp.bfloat16
F32 = jnp.float32


class Grid:
    def __init__(self, n_dp, n_z):
        self.n_dp, self.n_z = n_dp, n_z
        side = 1
        while side * side * 2 < n_dp:
            side *= 2
        self.nx, self.ny = side, n_dp // (2 * side)
        self.x_masks = [2 * k for k in range(1, self.nx)]
        self.y_masks = [2 * side * k for k in range(1, self.ny)]
        self.z_masks = list(range(1, n_z))
        self.square = self.nx == self.ny == 2 and n_z == 4

    def bind(self):
        self.my_dp = lax.axis_index("dp").astype(jnp.int32)
        self.my_z = lax.axis_index("fsdp").astype(jnp.int32)
        self.me = lax.axis_index(AXES).astype(jnp.int32)

    def over_dp(self, value, mask):
        return lax.ppermute(value, "dp", [(i, i ^ mask) for i in range(self.n_dp)])

    def crossed(self, value, even_mask, odd_mask):
        pairs = [(i, i ^ (odd_mask if i % 2 else even_mask)) for i in range(self.n_dp)]
        return lax.ppermute(value, "dp", pairs)

    def over_z(self, value, mask):
        return lax.ppermute(value, "fsdp", [(i, i ^ mask) for i in range(self.n_z)])


class Clock:
    def __init__(self):
        self.last = ()

    def gate(self, *values):
        held = lax.optimization_barrier(tuple(values) + self.last)[: len(values)]
        return held if len(values) > 1 else held[0]

    def tick(self, *values):
        self.last = values


class Lines:
    def __init__(self, grid, clock, shards):
        self.grid, self.clock = grid, clock
        self.block = shards[0].shape[0]
        self.parts, blocks = [], []
        at = 0
        for shard in shards:
            height, cols = shard.shape
            count = height // self.block
            blocks += [shard[k * self.block : (k + 1) * self.block] for k in range(count)]
            self.parts.append((at, count, cols))
            at += count * cols
        self.shard = jnp.concatenate(blocks, axis=1) if len(blocks) > 1 else blocks[0]

    def step0(self):
        self.held = self.clock.gate(self.shard)
        self.far = [m for m in self.grid.z_masks if m % 2 == 0]
        self.coming = [self.grid.over_z(self.held, m) for m in self.far]

    def step1(self):
        *got, held = self.clock.gate(*self.coming, self.held)
        self.held = jnp.concatenate([held, *got], 0)
        self.clock.tick(self.held)
        self.coming = self.grid.over_z(self.held, 1)

    def step2(self):
        got, held = self.clock.gate(self.coming, self.held)
        z_marks = [0] + self.far
        z_marks += [m ^ 1 for m in z_marks]
        joined = []
        for at, count, cols in self.parts:
            cut = slice(at, at + count * cols)
            joined.append(jnp.concatenate([held[:, cut], got[:, cut]], 0))
        self.clock.tick(*joined)
        return [
            Gather(self.grid, self.clock, rows, z_marks, self.block, count, cols)
            for rows, (_, count, cols) in zip(joined, self.parts)
        ]


class Gather:
    def __init__(self, grid, clock, rows, z_marks, block, count, cols):
        self.grid, self.clock, self.rows = grid, clock, rows
        self.z_marks, self.block, self.count, self.cols = z_marks, block, count, cols
        self.pieces = []

    def take(self, rows, even_mask, odd_mask):
        self.pieces.append((rows, even_mask, odd_mask))
        self.crossing = (self.grid.over_dp(rows, 1), odd_mask ^ 1, even_mask ^ 1)

    def land(self, coming):
        rows, crossed = self.clock.gate(coming, self.crossing[0])
        self.pieces.append((crossed, *self.crossing[1:]))
        self.clock.tick(rows)
        return rows

    def step0(self):
        grid = self.grid
        (x,), (y,) = grid.x_masks, grid.y_masks
        rows = self.clock.gate(self.rows)
        self.first = grid.crossed(rows, x, y)
        self.second = grid.crossed(rows, y, x)
        self.take(rows, 0, 0)

    def step1(self):
        grid = self.grid
        (x,), (y,) = grid.x_masks, grid.y_masks
        first = self.land(self.first)
        self.third = grid.crossed(first, y, x)
        self.take(first, x, y)

    def step2(self):
        (x,), (y,) = self.grid.x_masks, self.grid.y_masks
        self.take(self.land(self.second), y, x)

    def step3(self):
        (x,), (y,) = self.grid.x_masks, self.grid.y_masks
        self.take(self.land(self.third), x ^ y, x ^ y)
        self.pieces.append(self.crossing)

    def done(self, cuts=()):
        grid, block, count = self.grid, self.block, self.count
        pieces, z_marks = self.pieces, self.z_marks
        owners = grid.n_dp * grid.n_z
        edges = [0, *cuts, self.cols]
        spans = list(zip(edges[:-1], edges[1:]))
        copies = owners * count * len(spans)

        def kernel(me_ref, *refs):
            sources = refs[: len(pieces)]
            results = refs[len(pieces) : len(pieces) + len(spans)]
            sems = refs[-1]
            me = me_ref[0]
            odd = (me // grid.n_z) % 2 == 1
            started = []
            for source, (_, even_mask, odd_mask) in zip(sources, pieces):
                mask = jnp.where(odd, jnp.int32(odd_mask), jnp.int32(even_mask))
                for at, z in enumerate(z_marks):
                    owner = lax.bitwise_xor(me, mask * grid.n_z + z)
                    for k in range(count):
                        to = pl.multiple_of((owner * count + k) * block, block)
                        for result, (lo, hi) in zip(results, spans):
                            copy = pltpu.make_async_copy(
                                source.at[
                                    pl.ds(at * block, block), pl.ds(k * self.cols + lo, hi - lo)
                                ],
                                result.at[pl.ds(to, block)],
                                sems.at[len(started)],
                            )
                            copy.start()
                            started.append(copy)
            for copy in started:
                copy.wait()

        arrays = self.clock.gate(*[v for v, _, _ in pieces])
        rows = owners * count * block
        full = pl.pallas_call(
            kernel,
            out_shape=[jax.ShapeDtypeStruct((rows, hi - lo), BF16) for lo, hi in spans],
            grid_spec=pltpu.PrefetchScalarGridSpec(
                num_scalar_prefetch=1,
                grid=(),
                in_specs=[pl.BlockSpec(memory_space=pl.ANY)] * len(pieces),
                out_specs=[pl.BlockSpec(memory_space=pltpu.VMEM)] * len(spans),
                scratch_shapes=[pltpu.SemaphoreType.DMA((copies,))],
            ),
            compiler_params=pltpu.CompilerParams(vmem_limit_bytes=10 << 20),
            cost_estimate=pl.CostEstimate(flops=0, bytes_accessed=0, transcendentals=0),
            name="assemble",
        )(grid.me.reshape(1), *arrays)
        self.clock.tick(*full)
        return full


class PlainLines:
    def __init__(self, grid, clock, shards):
        self.shards = shards

    def step0(self):
        pass

    step1 = step0

    def step2(self):
        return [PlainGather(v) for v in self.shards]


class PlainGather:
    def __init__(self, shard):
        self.full = lax.all_gather(shard, AXES, axis=0, tiled=True)

    def step0(self):
        pass

    step1 = step2 = step3 = step0

    def done(self, cuts=()):
        edges = [0, *cuts, self.full.shape[1]]
        return [self.full[:, lo:hi] for lo, hi in zip(edges[:-1], edges[1:])]


def make_lines(grid, clock, *shards):
    plain = shards[0].shape[0] % 16 or not grid.square
    kind = PlainLines if plain else Lines
    return kind(grid, clock, shards)


def contract_rows(left, right):
    return lax.dot_general(left, right, (((0,), (0,)), ((), ())), preferred_element_type=F32)


def back_dot(grad_rows, weight):
    return lax.dot_general(grad_rows, weight, (((1,), (1,)), ((), ())), preferred_element_type=F32)


def pick(array, index):
    return lax.dynamic_index_in_dim(array, index, 0, keepdims=False)


def total_of(base, parts):
    for part in parts:
        base = base + part.astype(F32)
    return base


class Scatter:
    places = 4

    def __init__(self, grid, clock, lefts, rights):
        self.grid, self.clock, self.lefts, self.rights = grid, clock, lefts, rights
        self.chunk = lefts[0].shape[1] // grid.n_dp
        self.cols = sum(right.shape[1] for right in rights)
        once = pl.Buffered(1)
        self.whole = pl.BlockSpec(
            (self.chunk, self.cols), lambda j, dp: (0, 0), pipeline_mode=once
        )
        self.rows = [
            pl.BlockSpec(right.shape, lambda j, dp: (0, 0), pipeline_mode=once) for right in rights
        ]

    def shape(self, dtype):
        return jax.ShapeDtypeStruct((self.chunk, self.cols), dtype)

    def call(self, kernel, other, ins, shapes, specs):
        tokens, count = self.lefts[0].shape[0], len(self.lefts)

        def place(j, dp):
            a, b = j // 2, j % 2
            odd = (dp[0] + other) % 2
            mask = jnp.where(odd == 1, 2 * a + 4 * b, 4 * a + 2 * b)
            return 0, lax.bitwise_xor(dp[0], mask + other)

        def whole_kernel(dp_ref, *refs):
            lefts, rights, rest = refs[:count], refs[count : 2 * count], refs[2 * count :]
            terms = [contract_rows(a[...], b[...]) for a, b in zip(lefts, rights)]
            kernel(jnp.concatenate(terms, axis=1) if count > 1 else terms[0], *rest)

        ins = self.clock.gate(*self.lefts, *self.rights, *ins)
        return pl.pallas_call(
            whole_kernel,
            out_shape=shapes,
            grid_spec=pltpu.PrefetchScalarGridSpec(
                num_scalar_prefetch=1,
                grid=(self.places,),
                in_specs=[
                    *[pl.BlockSpec((tokens, self.chunk), place) for _ in self.lefts],
                    *self.rows,
                    *[self.whole for _ in ins[2 * count :]],
                ],
                out_specs=specs,
            ),
            compiler_params=pltpu.CompilerParams(vmem_limit_bytes=18 << 20),
            cost_estimate=pl.CostEstimate(flops=0, bytes_accessed=0, transcendentals=0),
            name="outer",
        )(self.grid.my_dp.reshape(1), *ins)

    def across(self):
        def kernel(term, *outs):
            term = term.astype(BF16)
            for k, out in enumerate(outs):

                @pl.when(pl.program_id(0) == k)
                def _(out=out):
                    out[...] = term

        shapes = [self.shape(BF16)] * self.places
        sends = self.call(kernel, 1, (), shapes, [self.whole] * self.places)
        self.clock.tick(*sends)
        self.got = [self.grid.over_dp(v, 1) for v in sends]

    def first(self):
        grid, places = self.grid, self.places
        (x,), (y,) = grid.x_masks, grid.y_masks

        def kernel(term, *refs):
            got, (keep, pass_on, far) = refs[:places], refs[places:]
            outs = (keep, pass_on, far.at[0], far.at[1])
            for k in range(places):

                @pl.when(pl.program_id(0) == k)
                def _(k=k):
                    outs[k][...] = (term + got[k][...].astype(F32)).astype(outs[k].dtype)

        wide = self.shape(F32)
        pair = jax.ShapeDtypeStruct((2, *wide.shape), BF16)
        pair_spec = pl.BlockSpec(
            pair.shape, lambda j, dp: (0, 0, 0), pipeline_mode=pl.Buffered(1)
        )
        keep, pass_on, far = self.call(
            kernel, 0, self.got, [wide, wide, pair], [self.whole, self.whole, pair_spec]
        )
        self.clock.tick(far)
        self.keep, self.pass_on = keep, pass_on
        self.got = grid.crossed(far, y, x)

    def second(self):
        (x,), (y,) = self.grid.x_masks, self.grid.y_masks
        got, pass_on = self.clock.gate(self.got, self.pass_on)
        send = (pass_on + got[1].astype(F32)).astype(BF16)
        self.clock.tick(send)
        self.aside = got[0]
        self.got = self.grid.crossed(send, x, y)

    def land(self):
        self.got = self.clock.gate(self.got)
        self.clock.tick(self.got)

    def third(self):
        grid = self.grid
        got, keep = self.clock.gate(self.got, self.keep)
        lines = total_of(keep, [got, self.aside]).reshape(2, 2, -1, self.cols)
        odd = grid.my_z % 2
        send = lax.dynamic_index_in_dim(lines, 1 - odd, 1, keepdims=False).astype(BF16)
        self.keep = lax.dynamic_index_in_dim(lines, odd, 1, keepdims=False)
        self.clock.tick(send)
        self.got = grid.over_z(send, 1)

    def fourth(self):
        grid = self.grid
        got, keep = self.clock.gate(self.got, self.keep)
        held = keep + got.astype(F32)
        pair = grid.my_z // 2
        send = pick(held, 1 - pair).astype(BF16)
        self.keep = pick(held, pair)
        self.clock.tick(send)
        self.got = grid.over_z(send, 2)

    def done(self):
        got, keep = self.clock.gate(self.got, self.keep)
        outs, at = [], 0
        for right in self.rights:
            cut = slice(at, at + right.shape[1])
            outs.append(keep[:, cut] + got[:, cut].astype(F32))
            at += right.shape[1]
        self.clock.tick(*outs)
        return outs


class PlainScatter:
    def __init__(self, lefts, rights):
        self.terms = [contract_rows(a, b) for a, b in zip(lefts, rights)]

    def across(self):
        pass

    first = second = land = third = fourth = across

    def done(self):
        return [lax.psum_scatter(t, AXES, scatter_dimension=0, tiled=True) for t in self.terms]


def make_scatter(grid, clock, *pairs):
    lefts, rights = [a for a, _ in pairs], [b for _, b in pairs]
    if (lefts[0].shape[1] // grid.n_dp) % 128 or not grid.square:
        return PlainScatter(lefts, rights)
    return Scatter(grid, clock, lefts, rights)


def lookup(small_table, index_rows):
    matches = index_rows[:, None] == jnp.arange(small_table.shape[0], dtype=jnp.int32)[None, :]
    return jnp.sum(jnp.where(matches, small_table[None, :], 0), axis=1)


def rank_among(group_label, order_key):
    earlier = (group_label[None, :] == group_label[:, None]) & (
        order_key[None, :] < order_key[:, None]
    )
    return jnp.sum(earlier.astype(jnp.int32), axis=1)


def routing(lengths, deal_order, devices, row_count, device):
    slot_count = deal_order.shape[0]
    slot_ids = jnp.arange(slot_count, dtype=jnp.int32)
    starts = jnp.cumsum(lengths) - lengths
    slot_of = jnp.sum(
        jnp.where(deal_order[None, :] == slot_ids[:, None], slot_ids[None, :], 0), axis=1
    )
    slot_lengths = lookup(lengths, deal_order)
    local_rows = jnp.arange(row_count, dtype=jnp.int32)
    token_index = local_rows * devices + device
    sequence = jnp.sum((starts[None, :] <= token_index[:, None]).astype(jnp.int32), axis=1) - 1
    slot_index = lookup(slot_of, sequence)
    target = slot_index // 2
    send_rank = rank_among(target, local_rows)
    first_len = lax.dynamic_index_in_dim(slot_lengths, 2 * device, 0, False)
    second = local_rows >= first_len
    first_seq = lax.dynamic_index_in_dim(deal_order, 2 * device, 0, False)
    second_seq = lax.dynamic_index_in_dim(deal_order, 2 * device + 1, 0, False)
    sequence_here = jnp.where(second, second_seq, first_seq)
    position = local_rows - jnp.where(second, first_len, 0)
    source_token = lookup(starts, sequence_here) + position
    source = source_token % devices
    take_rank = rank_among(source, source_token)
    return target, send_rank, source, take_rank, first_len.reshape(1)


HEADS_AT_ONCE = 4
LANES = HEADS_AT_ONCE * HEAD_DIM


def head_probs(query, key, first_len):
    scores = back_dot(query, key)
    q_at = lax.broadcasted_iota(jnp.int32, scores.shape, 0)
    k_at = lax.broadcasted_iota(jnp.int32, scores.shape, 1)
    allowed = (k_at <= q_at) & ((q_at < first_len) | (k_at >= first_len))
    masked = jnp.where(allowed, scores, -1000000000.0)
    exps = jnp.exp(masked - jnp.max(masked, axis=-1, keepdims=True))
    return exps * (1.0 / jnp.sum(exps, axis=-1, keepdims=True))


def of_heads(rows, parts):
    head = lax.broadcasted_iota(jnp.int32, (rows, LANES), 1) // HEAD_DIM
    whole = parts[0]
    for k in range(1, len(parts)):
        whole = jnp.where(head == k, parts[k], whole)
    return whole


def one_head(values, k):
    head = lax.broadcasted_iota(jnp.int32, values.shape, 1) // HEAD_DIM
    return jnp.where(head == k, values, jnp.zeros((), BF16))


def attend(first_len, mixed_b):
    rows, width = mixed_b.shape[0], mixed_b.shape[1] // 3
    steps = width // LANES

    def kernel(first_ref, query, key, value, out):
        scaled = query[...] * jnp.asarray(HEAD_DIM**-0.5, BF16)
        probs = [
            head_probs(one_head(scaled, k), key[...], first_ref[0]).astype(BF16)
            for k in range(HEADS_AT_ONCE)
        ]
        found = [jnp.dot(p, value[...], preferred_element_type=F32) for p in probs]
        out[...] = of_heads(rows, found).astype(BF16)

    def part(k):
        return pl.BlockSpec((rows, LANES), lambda h, first: (0, k * steps + h))

    return pl.pallas_call(
        kernel,
        out_shape=jax.ShapeDtypeStruct((rows, width), BF16),
        grid_spec=pltpu.PrefetchScalarGridSpec(
            num_scalar_prefetch=1,
            grid=(steps,),
            in_specs=[part(0), part(1), part(2)],
            out_specs=part(0),
        ),
        compiler_params=pltpu.CompilerParams(vmem_limit_bytes=10 << 20),
        cost_estimate=pl.CostEstimate(flops=0, bytes_accessed=0, transcendentals=0),
        name="attend",
    )(first_len, mixed_b, mixed_b, mixed_b)


def attend_back(first_len, mixed_b, grad_att_b):
    rows, width = grad_att_b.shape
    steps = width // LANES

    def kernel(first_ref, query, key, value, grad, out, sums):
        h = pl.program_id(0)
        scaled = query[...] * jnp.asarray(HEAD_DIM**-0.5, BF16)
        to_query, to_key, to_value = [], [], []
        for k in range(HEADS_AT_ONCE):
            q, g = one_head(scaled, k), one_head(grad[...], k)
            probs = head_probs(q, key[...], first_ref[0])
            grad_probs = back_dot(g, value[...])
            dots = jnp.sum(probs * grad_probs, axis=-1, keepdims=True)
            grad_scores = (probs * (grad_probs - dots)).astype(BF16)
            to_query.append(jnp.dot(grad_scores, key[...], preferred_element_type=F32))
            to_key.append(contract_rows(grad_scores, q))
            to_value.append(contract_rows(probs.astype(BF16), g))
        results = (of_heads(rows, to_query) * HEAD_DIM**-0.5, sum(to_key), sum(to_value))
        for k, block in enumerate(results):
            block = block.astype(BF16)
            at = pl.multiple_of(k * width + h * LANES, LANES)
            out[:, pl.ds(at, LANES)] = block
            sums[:, pl.ds(at, LANES)] = jnp.sum(block.astype(F32), axis=0, keepdims=True)

    def part(k):
        return pl.BlockSpec((rows, LANES), lambda h, first: (0, k * steps + h))

    return pl.pallas_call(
        kernel,
        out_shape=[
            jax.ShapeDtypeStruct((rows, 3 * width), BF16),
            jax.ShapeDtypeStruct((1, 3 * width), F32),
        ],
        grid_spec=pltpu.PrefetchScalarGridSpec(
            num_scalar_prefetch=1,
            grid=(steps,),
            in_specs=[part(0), part(1), part(2), part(0)],
            out_specs=[
                pl.BlockSpec((rows, 3 * width), lambda h, first: (0, 0)),
                pl.BlockSpec((1, 3 * width), lambda h, first: (0, 0)),
            ],
        ),
        compiler_params=pltpu.CompilerParams(vmem_limit_bytes=16 << 20),
        cost_estimate=pl.CostEstimate(flops=0, bytes_accessed=0, transcendentals=0),
        name="attend_back",
    )(first_len, mixed_b, mixed_b, mixed_b, grad_att_b)


def gelu_back(grad_b, weight, slope):
    rows, width = grad_b.shape
    hidden = weight.shape[0]
    tile = min(1024, hidden)

    def kernel(grad, weight, slope, out, sums):
        block = (back_dot(grad[...], weight[...]) * slope[...]).astype(BF16)
        out[...] = block
        sums[...] = jnp.sum(block.astype(F32), axis=0, keepdims=True)

    return pl.pallas_call(
        kernel,
        out_shape=[
            jax.ShapeDtypeStruct((rows, hidden), BF16),
            jax.ShapeDtypeStruct((1, hidden), F32),
        ],
        grid=(hidden // tile,),
        in_specs=[
            pl.BlockSpec((rows, width), lambda j: (0, 0)),
            pl.BlockSpec((tile, width), lambda j: (j, 0)),
            pl.BlockSpec((rows, tile), lambda j: (0, j)),
        ],
        out_specs=[
            pl.BlockSpec((rows, tile), lambda j: (0, j)),
            pl.BlockSpec((1, tile), lambda j: (0, j)),
        ],
        compiler_params=pltpu.CompilerParams(vmem_limit_bytes=14 << 20),
        cost_estimate=pl.CostEstimate(flops=0, bytes_accessed=0, transcendentals=0),
        name="gelu_back",
    )(grad_b, weight, slope)


def norm_back(grad_b, weight, unit, gain, scale, passed, keep_wide):
    rows, depth = grad_b.shape
    width = weight.shape[0]
    tile = 1024
    steps = depth // tile

    def kernel(grad, weight, unit, gain, scale, passed, *refs):
        outs, total = refs[:-1], refs[-1]
        step = pl.program_id(0)
        part = back_dot(grad[...], weight[...])

        @pl.when(step == 0)
        def _():
            total[...] = part

        @pl.when(step > 0)
        def _():
            total[...] += part

        @pl.when(step == steps - 1)
        def _():
            whole, u = total[...], unit[...]
            normed = whole * gain[...]
            out = passed[...].astype(F32) + standardize_back(normed, u, scale[...])
            out_b = out.astype(BF16)
            outs[0][...] = out_b
            outs[1][0:1] = jnp.sum(whole * u, axis=0, keepdims=True)
            outs[1][1:2] = jnp.sum(whole, axis=0, keepdims=True)
            outs[1][2:3] = jnp.sum(out_b.astype(F32), axis=0, keepdims=True)
            if keep_wide:
                outs[2][...] = out

    def once(shape):
        return pl.BlockSpec(shape, lambda j: (0, 0), pipeline_mode=pl.Buffered(1))

    shapes = [((rows, width), BF16), ((8, width), F32)]
    shapes += [((rows, width), F32)] if keep_wide else []
    return pl.pallas_call(
        kernel,
        out_shape=[jax.ShapeDtypeStruct(*s) for s in shapes],
        grid=(steps,),
        in_specs=[
            pl.BlockSpec((rows, tile), lambda j: (0, j)),
            pl.BlockSpec((width, tile), lambda j: (0, j)),
            once((rows, width)),
            once((1, width)),
            once((rows, 1)),
            once((rows, width)),
        ],
        out_specs=[once(shape) for shape, _ in shapes],
        scratch_shapes=[pltpu.VMEM((rows, width), F32)],
        compiler_params=pltpu.CompilerParams(vmem_limit_bytes=16 << 20),
        cost_estimate=pl.CostEstimate(flops=0, bytes_accessed=0, transcendentals=0),
        name="norm_back",
    )(grad_b, pltpu.with_memory_space_constraint(weight, pltpu.HBM), unit, gain, scale, passed)


def standardize(values):
    centered = values - jnp.mean(values, axis=-1, keepdims=True)
    scale = lax.rsqrt(jnp.mean(centered * centered, axis=-1, keepdims=True) + EPSILON)
    return centered * scale, scale


def standardize_back(grad, unit, scale):
    return scale * (
        grad
        - jnp.mean(grad, axis=-1, keepdims=True)
        - unit * jnp.mean(grad * unit, axis=-1, keepdims=True)
    )


def col_sum(values):
    return jnp.sum(values.astype(F32), axis=0)


def on_device(
    n_dp,
    n_z,
    rows_in,
    cotangent,
    lengths,
    deal_order,
    w_qkv,
    b_query,
    b_value,
    w_out,
    b_out,
    gain_one,
    shift_one,
    w_up,
    b_up,
    w_down,
    b_down,
    gain_two,
    shift_two,
):
    grid = Grid(n_dp, n_z)
    grid.bind()
    clock = Clock()
    devices = n_dp * n_z
    row_count, _, width = rows_in.shape
    hidden = w_up.shape[1]
    share = width // devices

    early = make_lines(grid, clock, jnp.concatenate([w_qkv, w_out], axis=1))
    middle = make_lines(grid, clock, w_up)
    late = make_lines(grid, clock, w_down)
    early.step0()

    target, send_rank, source, take_rank, first_len = routing(
        lengths, deal_order, devices, row_count, grid.me
    )
    slot_rows = row_count // devices + 1
    in_rows = slot_rows
    out_rows = 2 * slot_rows

    def selector(owner, rank, block_rows):
        at = (owner * block_rows + rank)[:, None]
        slot_ids = jnp.arange(devices * block_rows, dtype=jnp.int32)[None, :]
        return (at == slot_ids).astype(BF16)

    to_slots = selector(target, send_rank, in_rows)
    from_slots = selector(source, take_rank, in_rows)

    def both_of(owner, rank):
        at = owner * out_rows + rank
        return jnp.concatenate([at, at + slot_rows])

    out_slot_ids = jnp.arange(devices * out_rows, dtype=jnp.int32)
    take_both = (both_of(target, send_rank)[:, None] == out_slot_ids[None, :]).astype(BF16)
    send_both = (out_slot_ids[:, None] == both_of(source, take_rank)[None, :]).astype(BF16)

    def swap(block, lines=None):
        block = block.reshape(devices, -1, 128)
        if lines is not None:
            block = jnp.concatenate([block, lines], axis=1)
        block = lax.all_to_all(block, AXES, split_axis=0, concat_axis=0, tiled=True)
        if lines is None:
            return block.reshape(-1, width)
        height = block.shape[1] - lines.shape[1]
        return block[:, :height].reshape(-1, width), block[:, height:]

    vectors = jnp.stack(
        [b_query, b_value, b_out, gain_one, shift_one, b_down, gain_two, shift_two]
    )
    groups = 128 // share
    spot = grid.me % groups
    at_spot = lax.broadcasted_iota(jnp.int32, (8, 128), 1) // share == spot
    vectors = jnp.where(at_spot, jnp.tile(vectors, (1, groups)), jnp.zeros((), BF16))
    bias_groups = max(1, 128 * devices // hidden)
    bias = jnp.tile(b_up[None, :], (1, bias_groups))
    at_bias = lax.broadcasted_iota(jnp.int32, (1, 128), 1) // b_up.shape[0]
    bias = jnp.where(at_bias == grid.me % bias_groups, bias, jnp.zeros((), BF16))
    bias = jnp.pad(bias, ((0, 7), (0, 0)))
    small = jnp.concatenate([vectors, bias], axis=0)
    early.step1()
    middle.step0()
    to_slots, own_rows = clock.gate(to_slots, rows_in)
    block = contract_rows(to_slots, own_rows.reshape(row_count, width))
    block = block.astype(BF16)
    clock.tick(block)
    (attn,) = early.step2()
    attn.step0()
    middle.step1()
    late.step0()
    small = jnp.broadcast_to(small[None], (devices, *small.shape))
    arrived, small_all = swap(clock.gate(block), small)
    attn.step1()
    attn.step2()
    (up,) = middle.step2()
    up.step0()
    late.step1()
    attn.step3()
    arrived, small_all = clock.gate(arrived, small_all)
    inputs = jnp.dot(from_slots, arrived, preferred_element_type=F32)
    lines = jnp.sum(small_all[:, :8].astype(F32).reshape(-1, groups, 8, 128), axis=1)
    bq, bv, bo, g1, s1, bd, g2, s2 = [
        v[None, :] for v in jnp.swapaxes(lines, 0, 1).reshape(8, width)
    ]
    lines = jnp.sum(small_all[:, 8].astype(F32).reshape(-1, bias_groups, 128), axis=1)
    bu = lines.reshape(1, hidden)
    unit_one, scale_one = standardize(inputs)
    normed_one_b = (unit_one * g1 + s1).astype(BF16)
    clock.tick(normed_one_b)
    take_both, send_both = clock.gate(take_both, send_both)
    clock.tick(take_both, send_both)
    (down,) = late.step2()
    up.step1()
    up.step2()
    down.step0()
    full_qkv, full_out = attn.done((3 * width,))
    mixed = jnp.dot(clock.gate(normed_one_b), full_qkv, preferred_element_type=F32)
    mixed_b = (mixed + jnp.concatenate([bq, jnp.zeros_like(bq), bv], axis=1)).astype(BF16)
    attended_b = attend(first_len, mixed_b)
    clock.tick(attended_b)
    up.step3()
    attended_b, cot_rows = clock.gate(attended_b, cotangent)
    cot_block = contract_rows(to_slots, cot_rows.reshape(row_count, width)).astype(BF16)
    clock.tick(cot_block)
    arrived_cot = swap(cot_block)
    hidden_one = inputs + jnp.dot(attended_b, full_out, preferred_element_type=F32) + bo
    unit_two, scale_two = standardize(hidden_one)
    normed_two_b = (unit_two * g2 + s2).astype(BF16)
    clock.tick(normed_two_b)

    (full_up,) = up.done()
    down.step1()
    down.step2()
    pre_act = jnp.dot(clock.gate(normed_two_b), full_up, preferred_element_type=F32) + bu
    half_cdf = 0.5 * (1.0 + lax.erf(pre_act * (0.5**0.5)))
    activation_b = (pre_act * half_cdf).astype(BF16)
    density = jnp.exp(-0.5 * pre_act * pre_act) * ((2.0 * jnp.pi) ** -0.5)
    slope = half_cdf + pre_act * density
    clock.tick(activation_b, slope)

    arrived_cot = clock.gate(arrived_cot)
    grad_m_b = jnp.dot(from_slots, arrived_cot, preferred_element_type=F32)
    grad_m_b = grad_m_b.astype(BF16)
    clock.tick(grad_m_b)
    term_b_down = col_sum(grad_m_b)[None, :]
    for_down = make_scatter(grid, clock, (activation_b, grad_m_b))
    for_down.across()
    down.step3()
    (full_down,) = down.done()
    grad_pre_b, term_b_up = gelu_back(clock.gate(grad_m_b), full_down, slope)
    clock.tick(grad_pre_b)
    for_down.first()
    for_up = make_scatter(grid, clock, (normed_two_b, grad_pre_b))
    for_up.across()

    grad_branch_b, sums_two, grad_hidden = norm_back(
        clock.gate(grad_pre_b), full_up, unit_two, g2, scale_two, grad_m_b, True
    )
    clock.tick(grad_branch_b)
    for_up.first()
    for_down.second()
    grad_att_b = back_dot(clock.gate(grad_branch_b), full_out).astype(BF16)
    clock.tick(grad_att_b)
    grad_mixed_b, term_mixed = attend_back(first_len, mixed_b, clock.gate(grad_att_b))
    clock.tick(grad_mixed_b)
    for_attn = make_scatter(
        grid, clock, (normed_one_b, grad_mixed_b), (attended_b, grad_branch_b)
    )
    for_attn.across()

    grad_inputs_b, sums_one = norm_back(
        clock.gate(grad_mixed_b), full_qkv, unit_one, g1, scale_one, grad_hidden, False
    )
    clock.tick(grad_inputs_b)
    for_attn.first()
    for_up.second()
    for_down.third()
    result = jnp.dot(clock.gate(activation_b), full_down, preferred_element_type=F32)
    result_b = (hidden_one + result + bd).astype(BF16)
    term_mixed, sums_one, sums_two, term_b_down, term_b_up, result_b = clock.gate(
        term_mixed, sums_one, sums_two, term_b_down, term_b_up, result_b
    )
    terms = [term_mixed[:, :width], term_mixed[:, 2 * width :], sums_two[2:3], sums_one[:2]]
    terms = jnp.concatenate([*terms, term_b_down, sums_two[:2]], axis=0).astype(BF16)
    lines = jnp.swapaxes(terms.reshape(8, -1, 128), 0, 1)
    lines = jnp.repeat(lines, groups, axis=0)
    bias = jnp.repeat(term_b_up.astype(BF16).reshape(-1, 1, 128), bias_groups, axis=0)
    lines = jnp.concatenate([lines, jnp.pad(bias, ((0, 0), (0, 7), (0, 0)))], axis=1)
    both = jnp.concatenate([result_b, grad_inputs_b], axis=0)
    block = jnp.dot(send_both, both, preferred_element_type=F32)
    block = block.astype(BF16)
    clock.tick(block)
    returned, small_back = swap(block, lines)

    for_up.third()
    for_attn.second()
    for_down.fourth()
    returned, small_back = clock.gate(returned, small_back)
    clock.tick(returned)
    for_attn.third()
    for_up.fourth()
    for_attn.fourth()
    returned = clock.gate(returned)
    placed = jnp.dot(take_both, returned, preferred_element_type=F32)
    placed = placed.astype(BF16)
    rows_out, grad_rows = placed[:row_count], placed[row_count:]
    sums = jnp.sum(small_back.astype(F32), axis=0)
    clock.tick(placed)
    (grad_w_down,) = for_down.done()
    (grad_w_up,) = for_up.done()
    grad_w_qkv, grad_w_out = for_attn.done()

    mine = lax.dynamic_slice_in_dim(sums[:8], spot * share, share, axis=1)
    grad_bq, grad_bv, grad_bo, grad_g1, grad_s1, grad_bd, grad_g2, grad_s2 = mine
    bias_width = hidden // devices
    grad_bu = lax.dynamic_slice_in_dim(
        sums[8], (grid.me % bias_groups) * bias_width, bias_width, axis=0
    )
    return (
        rows_out.reshape(row_count, 1, width),
        grad_rows.reshape(row_count, 1, width),
        grad_w_qkv,
        grad_bq,
        grad_bv,
        grad_w_out,
        grad_bo,
        grad_g1,
        grad_s1,
        grad_w_up,
        grad_bu,
        grad_w_down,
        grad_bd,
        grad_g2,
        grad_s2,
    )


def solution(mesh):
    n_dp, n_z = mesh.shape["dp"], mesh.shape["fsdp"]
    rows, vec, mat = P(None, AXES, None), P(AXES), P(AXES, None)

    def run(*args):
        return on_device(n_dp, n_z, *args)

    return jax.shard_map(
        run,
        mesh=mesh,
        in_specs=(rows, rows, P(), P())
        + (mat, vec, vec, mat, vec, vec, vec, mat, vec, mat, vec, vec, vec),
        out_specs=(rows, rows, mat, vec, vec, mat, vec, vec, vec, mat, vec, mat, vec, vec, vec),
        check_vma=False,
    )
```

```python
import jax
import jax.numpy as jnp
from jax import lax
from jax.experimental import pallas as pl
from jax.experimental.pallas import tpu as pltpu
from jax.sharding import PartitionSpec as P

HEADS = 16
HEAD_DIM = 64
EPSILON = 1e-05
AXES = ("dp", "fsdp")
BF16 = jnp.bfloat16
F32 = jnp.float32


class Grid:
    def __init__(self, n_dp, n_z):
        self.n_dp, self.n_z = n_dp, n_z
        side = 1
        while side * side * 2 < n_dp:
            side *= 2
        self.nx, self.ny = side, n_dp // (2 * side)
        self.x_masks = [2 * k for k in range(1, self.nx)]
        self.y_masks = [2 * side * k for k in range(1, self.ny)]
        self.z_masks = list(range(1, n_z))
        self.square = self.nx == self.ny == 2 and n_z == 4

    def bind(self):
        self.my_dp = lax.axis_index("dp").astype(jnp.int32)
        self.my_z = lax.axis_index("fsdp").astype(jnp.int32)
        self.me = lax.axis_index(AXES).astype(jnp.int32)

    def over_dp(self, value, mask):
        return lax.ppermute(value, "dp", [(i, i ^ mask) for i in range(self.n_dp)])

    def crossed(self, value, even_mask, odd_mask):
        pairs = [(i, i ^ (odd_mask if i % 2 else even_mask)) for i in range(self.n_dp)]
        return lax.ppermute(value, "dp", pairs)

    def over_z(self, value, mask):
        return lax.ppermute(value, "fsdp", [(i, i ^ mask) for i in range(self.n_z)])


class Clock:
    def __init__(self):
        self.last = ()

    def gate(self, *values):
        held = lax.optimization_barrier(tuple(values) + self.last)[: len(values)]
        return held if len(values) > 1 else held[0]

    def tick(self, *values):
        self.last = values


class Lines:
    def __init__(self, grid, clock, shards):
        self.grid, self.clock = grid, clock
        self.block = shards[0].shape[0]
        self.parts, blocks = [], []
        at = 0
        for shard in shards:
            height, cols = shard.shape
            count = height // self.block
            blocks += [shard[k * self.block : (k + 1) * self.block] for k in range(count)]
            self.parts.append((at, count, cols))
            at += count * cols
        self.shard = jnp.concatenate(blocks, axis=1) if len(blocks) > 1 else blocks[0]

    def step0(self):
        self.held = self.clock.gate(self.shard)
        self.far = [m for m in self.grid.z_masks if m % 2 == 0]
        self.coming = [self.grid.over_z(self.held, m) for m in self.far]

    def step1(self):
        *got, held = self.clock.gate(*self.coming, self.held)
        self.held = jnp.concatenate([held, *got], 0)
        self.clock.tick(self.held)
        self.coming = self.grid.over_z(self.held, 1)

    def step2(self):
        got, held = self.clock.gate(self.coming, self.held)
        z_marks = [0] + self.far
        z_marks += [m ^ 1 for m in z_marks]
        joined = []
        for at, count, cols in self.parts:
            cut = slice(at, at + count * cols)
            joined.append(jnp.concatenate([held[:, cut], got[:, cut]], 0))
        self.clock.tick(*joined)
        return [
            Gather(self.grid, self.clock, rows, z_marks, self.block, count, cols)
            for rows, (_, count, cols) in zip(joined, self.parts)
        ]


class Gather:
    def __init__(self, grid, clock, rows, z_marks, block, count, cols):
        self.grid, self.clock, self.rows = grid, clock, rows
        self.z_marks, self.block, self.count, self.cols = z_marks, block, count, cols
        self.pieces = []

    def take(self, rows, even_mask, odd_mask):
        self.pieces.append((rows, even_mask, odd_mask))
        self.crossing = (self.grid.over_dp(rows, 1), odd_mask ^ 1, even_mask ^ 1)

    def land(self, coming):
        rows, crossed = self.clock.gate(coming, self.crossing[0])
        self.pieces.append((crossed, *self.crossing[1:]))
        self.clock.tick(rows)
        return rows

    def step0(self):
        grid = self.grid
        (x,), (y,) = grid.x_masks, grid.y_masks
        rows = self.clock.gate(self.rows)
        self.first = grid.crossed(rows, x, y)
        self.second = grid.crossed(rows, y, x)
        self.take(rows, 0, 0)

    def step1(self):
        grid = self.grid
        (x,), (y,) = grid.x_masks, grid.y_masks
        first = self.land(self.first)
        self.third = grid.crossed(first, y, x)
        self.take(first, x, y)

    def step2(self):
        (x,), (y,) = self.grid.x_masks, self.grid.y_masks
        self.take(self.land(self.second), y, x)

    def step3(self):
        (x,), (y,) = self.grid.x_masks, self.grid.y_masks
        self.take(self.land(self.third), x ^ y, x ^ y)
        self.pieces.append(self.crossing)

    def done(self, cuts=()):
        grid, block, count = self.grid, self.block, self.count
        pieces, z_marks = self.pieces, self.z_marks
        owners = grid.n_dp * grid.n_z
        edges = [0, *cuts, self.cols]
        spans = list(zip(edges[:-1], edges[1:]))
        copies = owners * count * len(spans)

        def kernel(me_ref, *refs):
            sources = refs[: len(pieces)]
            results = refs[len(pieces) : len(pieces) + len(spans)]
            sems = refs[-1]
            me = me_ref[0]
            odd = (me // grid.n_z) % 2 == 1
            started = []
            for source, (_, even_mask, odd_mask) in zip(sources, pieces):
                mask = jnp.where(odd, jnp.int32(odd_mask), jnp.int32(even_mask))
                for at, z in enumerate(z_marks):
                    owner = lax.bitwise_xor(me, mask * grid.n_z + z)
                    for k in range(count):
                        to = pl.multiple_of((owner * count + k) * block, block)
                        for result, (lo, hi) in zip(results, spans):
                            copy = pltpu.make_async_copy(
                                source.at[
                                    pl.ds(at * block, block), pl.ds(k * self.cols + lo, hi - lo)
                                ],
                                result.at[pl.ds(to, block)],
                                sems.at[len(started)],
                            )
                            copy.start()
                            started.append(copy)
            for copy in started:
                copy.wait()

        arrays = self.clock.gate(*[v for v, _, _ in pieces])
        rows = owners * count * block
        full = pl.pallas_call(
            kernel,
            out_shape=[jax.ShapeDtypeStruct((rows, hi - lo), BF16) for lo, hi in spans],
            grid_spec=pltpu.PrefetchScalarGridSpec(
                num_scalar_prefetch=1,
                grid=(),
                in_specs=[pl.BlockSpec(memory_space=pl.ANY)] * len(pieces),
                out_specs=[pl.BlockSpec(memory_space=pltpu.VMEM)] * len(spans),
                scratch_shapes=[pltpu.SemaphoreType.DMA((copies,))],
            ),
            compiler_params=pltpu.CompilerParams(vmem_limit_bytes=10 << 20),
            cost_estimate=pl.CostEstimate(flops=0, bytes_accessed=0, transcendentals=0),
            name="assemble",
        )(grid.me.reshape(1), *arrays)
        self.clock.tick(*full)
        return full


class PlainLines:
    def __init__(self, grid, clock, shards):
        self.shards = shards

    def step0(self):
        pass

    step1 = step0

    def step2(self):
        return [PlainGather(v) for v in self.shards]


class PlainGather:
    def __init__(self, shard):
        self.full = lax.all_gather(shard, AXES, axis=0, tiled=True)

    def step0(self):
        pass

    step1 = step2 = step3 = step0

    def done(self, cuts=()):
        edges = [0, *cuts, self.full.shape[1]]
        return [self.full[:, lo:hi] for lo, hi in zip(edges[:-1], edges[1:])]


def make_lines(grid, clock, *shards):
    plain = shards[0].shape[0] % 16 or not grid.square
    kind = PlainLines if plain else Lines
    return kind(grid, clock, shards)


def contract_rows(left, right):
    return lax.dot_general(left, right, (((0,), (0,)), ((), ())), preferred_element_type=F32)


def back_dot(grad_rows, weight):
    return lax.dot_general(grad_rows, weight, (((1,), (1,)), ((), ())), preferred_element_type=F32)


def pick(array, index):
    return lax.dynamic_index_in_dim(array, index, 0, keepdims=False)


def total_of(base, parts):
    for part in parts:
        base = base + part.astype(F32)
    return base


class Scatter:
    places = 4

    def __init__(self, grid, clock, lefts, rights):
        self.grid, self.clock, self.lefts, self.rights = grid, clock, lefts, rights
        self.chunk = lefts[0].shape[1] // grid.n_dp
        self.cols = sum(right.shape[1] for right in rights)
        once = pl.Buffered(1)
        self.rows = [
            pl.BlockSpec(right.shape, lambda j, dp: (0, 0), pipeline_mode=once) for right in rights
        ]

    def call(self, other, ins, shapes, targets):
        tokens, count, places = self.lefts[0].shape[0], len(self.lefts), self.places
        added = len(ins)

        def place(j, dp):
            a, b = j // 2, j % 2
            odd = (dp[0] + other) % 2
            mask = jnp.where(odd == 1, 2 * a + 4 * b, 4 * a + 2 * b)
            return 0, lax.bitwise_xor(dp[0], mask + other)

        def kernel(dp_ref, *refs):
            lefts, rights, refs = refs[:count], refs[count : 2 * count], refs[2 * count :]
            gots, outs = refs[:added], refs[added : added + len(shapes)]
            blocks, out_sems, *fetched = refs[added + len(shapes) :]
            step = pl.program_id(0)

            def fetch(k):
                return pltpu.make_async_copy(gots[k], fetched[0].at[k], fetched[1].at[k])

            def put(k):
                return pltpu.make_async_copy(blocks.at[k], targets(outs)[k], out_sems.at[k])

            if added:

                @pl.when(step == 0)
                def _():
                    for k in range(places):
                        fetch(k).start()

            terms = [contract_rows(a[...], b[...]) for a, b in zip(lefts, rights)]
            term = jnp.concatenate(terms, axis=1) if count > 1 else terms[0]
            for k in range(places):

                @pl.when(step == k)
                def _(k=k):
                    whole = term
                    if added:
                        fetch(k).wait()
                        whole = whole + fetched[0][k].astype(F32)
                    blocks[k] = whole.astype(BF16)
                    put(k).start()

            @pl.when(step == places - 1)
            def _():
                for k in range(places):
                    put(k).wait()

        anywhere = pl.BlockSpec(memory_space=pl.ANY)
        scratch = [
            pltpu.VMEM((places, self.chunk, self.cols), BF16),
            pltpu.SemaphoreType.DMA((places,)),
        ]
        ins = self.clock.gate(*self.lefts, *self.rights, *ins)
        return pl.pallas_call(
            kernel,
            out_shape=shapes,
            grid_spec=pltpu.PrefetchScalarGridSpec(
                num_scalar_prefetch=1,
                grid=(places,),
                in_specs=[
                    *[pl.BlockSpec((tokens, self.chunk), place) for _ in self.lefts],
                    *self.rows,
                    *[anywhere] * added,
                ],
                out_specs=[anywhere] * len(shapes),
                scratch_shapes=scratch * (2 if added else 1),
            ),
            compiler_params=pltpu.CompilerParams(vmem_limit_bytes=20 << 20),
            cost_estimate=pl.CostEstimate(flops=0, bytes_accessed=0, transcendentals=0),
            name="outer",
        )(self.grid.my_dp.reshape(1), *ins)

    def across(self):
        shapes = [jax.ShapeDtypeStruct((self.chunk, self.cols), BF16)] * self.places
        sends = self.call(1, (), shapes, lambda outs: outs)
        self.clock.tick(*sends)
        self.got = [self.grid.over_dp(v, 1) for v in sends]

    def first(self):
        grid = self.grid
        (x,), (y,) = grid.x_masks, grid.y_masks
        one = jax.ShapeDtypeStruct((self.chunk, self.cols), BF16)
        pair = jax.ShapeDtypeStruct((2, self.chunk, self.cols), BF16)
        keep, pass_on, far = self.call(
            0,
            self.got,
            [one, one, pair],
            lambda outs: (outs[0], outs[1], outs[2].at[0], outs[2].at[1]),
        )
        self.clock.tick(far)
        self.keep, self.pass_on = keep, pass_on
        self.got = grid.crossed(far, y, x)

    def second(self):
        (x,), (y,) = self.grid.x_masks, self.grid.y_masks
        got, pass_on = self.clock.gate(self.got, self.pass_on)
        send = (pass_on.astype(F32) + got[1].astype(F32)).astype(BF16)
        self.clock.tick(send)
        self.aside = got[0]
        self.got = self.grid.crossed(send, x, y)

    def land(self):
        self.got = self.clock.gate(self.got)
        self.clock.tick(self.got)

    def third(self):
        grid = self.grid
        got, keep = self.clock.gate(self.got, self.keep)
        lines = total_of(keep.astype(F32), [got, self.aside]).reshape(2, 2, -1, self.cols)
        odd = grid.my_z % 2
        send = lax.dynamic_index_in_dim(lines, 1 - odd, 1, keepdims=False).astype(BF16)
        self.keep = lax.dynamic_index_in_dim(lines, odd, 1, keepdims=False)
        self.clock.tick(send)
        self.got = grid.over_z(send, 1)

    def fourth(self):
        grid = self.grid
        got, keep = self.clock.gate(self.got, self.keep)
        held = keep + got.astype(F32)
        pair = grid.my_z // 2
        send = pick(held, 1 - pair).astype(BF16)
        self.keep = pick(held, pair)
        self.clock.tick(send)
        self.got = grid.over_z(send, 2)

    def done(self):
        got, keep = self.clock.gate(self.got, self.keep)
        outs, at = [], 0
        for right in self.rights:
            cut = slice(at, at + right.shape[1])
            outs.append(keep[:, cut] + got[:, cut].astype(F32))
            at += right.shape[1]
        self.clock.tick(*outs)
        return outs


class PlainScatter:
    def __init__(self, lefts, rights):
        self.terms = [contract_rows(a, b) for a, b in zip(lefts, rights)]

    def across(self):
        pass

    first = second = land = third = fourth = across

    def done(self):
        return [lax.psum_scatter(t, AXES, scatter_dimension=0, tiled=True) for t in self.terms]


def make_scatter(grid, clock, *pairs):
    lefts, rights = [a for a, _ in pairs], [b for _, b in pairs]
    if (lefts[0].shape[1] // grid.n_dp) % 128 or not grid.square:
        return PlainScatter(lefts, rights)
    return Scatter(grid, clock, lefts, rights)


def lookup(small_table, index_rows):
    matches = index_rows[:, None] == jnp.arange(small_table.shape[0], dtype=jnp.int32)[None, :]
    return jnp.sum(jnp.where(matches, small_table[None, :], 0), axis=1)


def rank_among(group_label, order_key):
    earlier = (group_label[None, :] == group_label[:, None]) & (
        order_key[None, :] < order_key[:, None]
    )
    return jnp.sum(earlier.astype(jnp.int32), axis=1)


def routing(lengths, deal_order, devices, row_count, device):
    slot_count = deal_order.shape[0]
    slot_ids = jnp.arange(slot_count, dtype=jnp.int32)
    starts = jnp.cumsum(lengths) - lengths
    slot_of = jnp.sum(
        jnp.where(deal_order[None, :] == slot_ids[:, None], slot_ids[None, :], 0), axis=1
    )
    slot_lengths = lookup(lengths, deal_order)
    local_rows = jnp.arange(row_count, dtype=jnp.int32)
    token_index = local_rows * devices + device
    sequence = jnp.sum((starts[None, :] <= token_index[:, None]).astype(jnp.int32), axis=1) - 1
    slot_index = lookup(slot_of, sequence)
    target = slot_index // 2
    send_rank = rank_among(target, local_rows)
    first_len = lax.dynamic_index_in_dim(slot_lengths, 2 * device, 0, False)
    second = local_rows >= first_len
    first_seq = lax.dynamic_index_in_dim(deal_order, 2 * device, 0, False)
    second_seq = lax.dynamic_index_in_dim(deal_order, 2 * device + 1, 0, False)
    sequence_here = jnp.where(second, second_seq, first_seq)
    position = local_rows - jnp.where(second, first_len, 0)
    source_token = lookup(starts, sequence_here) + position
    source = source_token % devices
    take_rank = rank_among(source, source_token)
    return target, send_rank, source, take_rank, first_len.reshape(1)


HEADS_AT_ONCE = 4
LANES = HEADS_AT_ONCE * HEAD_DIM


def head_probs(query, key, first_len):
    scores = back_dot(query, key)
    q_at = lax.broadcasted_iota(jnp.int32, scores.shape, 0)
    k_at = lax.broadcasted_iota(jnp.int32, scores.shape, 1)
    allowed = (k_at <= q_at) & ((q_at < first_len) | (k_at >= first_len))
    masked = jnp.where(allowed, scores, -1000000000.0)
    exps = jnp.exp(masked - jnp.max(masked, axis=-1, keepdims=True))
    return exps * (1.0 / jnp.sum(exps, axis=-1, keepdims=True))


def of_heads(rows, parts):
    head = lax.broadcasted_iota(jnp.int32, (rows, LANES), 1) // HEAD_DIM
    whole = parts[0]
    for k in range(1, len(parts)):
        whole = jnp.where(head == k, parts[k], whole)
    return whole


def one_head(values, k):
    head = lax.broadcasted_iota(jnp.int32, values.shape, 1) // HEAD_DIM
    return jnp.where(head == k, values, jnp.zeros((), BF16))


def attend(first_len, mixed_b):
    rows, width = mixed_b.shape[0], mixed_b.shape[1] // 3
    steps = width // LANES

    def kernel(first_ref, query, key, value, out):
        scaled = query[...] * jnp.asarray(HEAD_DIM**-0.5, BF16)
        probs = [
            head_probs(one_head(scaled, k), key[...], first_ref[0]).astype(BF16)
            for k in range(HEADS_AT_ONCE)
        ]
        found = [jnp.dot(p, value[...], preferred_element_type=F32) for p in probs]
        out[...] = of_heads(rows, found).astype(BF16)

    def part(k):
        return pl.BlockSpec((rows, LANES), lambda h, first: (0, k * steps + h))

    return pl.pallas_call(
        kernel,
        out_shape=jax.ShapeDtypeStruct((rows, width), BF16),
        grid_spec=pltpu.PrefetchScalarGridSpec(
            num_scalar_prefetch=1,
            grid=(steps,),
            in_specs=[part(0), part(1), part(2)],
            out_specs=part(0),
        ),
        compiler_params=pltpu.CompilerParams(vmem_limit_bytes=10 << 20),
        cost_estimate=pl.CostEstimate(flops=0, bytes_accessed=0, transcendentals=0),
        name="attend",
    )(first_len, mixed_b, mixed_b, mixed_b)


def attend_back(first_len, mixed_b, grad_att_b):
    rows, width = grad_att_b.shape
    steps = width // LANES

    def kernel(first_ref, query, key, value, grad, out, sums):
        h = pl.program_id(0)
        scaled = query[...] * jnp.asarray(HEAD_DIM**-0.5, BF16)
        to_query, to_key, to_value = [], [], []
        for k in range(HEADS_AT_ONCE):
            q, g = one_head(scaled, k), one_head(grad[...], k)
            probs = head_probs(q, key[...], first_ref[0])
            grad_probs = back_dot(g, value[...])
            dots = jnp.sum(probs * grad_probs, axis=-1, keepdims=True)
            grad_scores = (probs * (grad_probs - dots)).astype(BF16)
            to_query.append(jnp.dot(grad_scores, key[...], preferred_element_type=F32))
            to_key.append(contract_rows(grad_scores, q))
            to_value.append(contract_rows(probs.astype(BF16), g))
        results = (of_heads(rows, to_query) * HEAD_DIM**-0.5, sum(to_key), sum(to_value))
        for k, block in enumerate(results):
            block = block.astype(BF16)
            at = pl.multiple_of(k * width + h * LANES, LANES)
            out[:, pl.ds(at, LANES)] = block
            sums[:, pl.ds(at, LANES)] = jnp.sum(block.astype(F32), axis=0, keepdims=True)

    def part(k):
        return pl.BlockSpec((rows, LANES), lambda h, first: (0, k * steps + h))

    return pl.pallas_call(
        kernel,
        out_shape=[
            jax.ShapeDtypeStruct((rows, 3 * width), BF16),
            jax.ShapeDtypeStruct((1, 3 * width), F32),
        ],
        grid_spec=pltpu.PrefetchScalarGridSpec(
            num_scalar_prefetch=1,
            grid=(steps,),
            in_specs=[part(0), part(1), part(2), part(0)],
            out_specs=[
                pl.BlockSpec((rows, 3 * width), lambda h, first: (0, 0)),
                pl.BlockSpec((1, 3 * width), lambda h, first: (0, 0)),
            ],
        ),
        compiler_params=pltpu.CompilerParams(vmem_limit_bytes=16 << 20),
        cost_estimate=pl.CostEstimate(flops=0, bytes_accessed=0, transcendentals=0),
        name="attend_back",
    )(first_len, mixed_b, mixed_b, mixed_b, grad_att_b)


def gelu_back(grad_b, weight, slope):
    rows, width = grad_b.shape
    hidden = weight.shape[0]
    tile = min(1024, hidden)

    def kernel(grad, weight, slope, out, sums):
        block = (back_dot(grad[...], weight[...]) * slope[...]).astype(BF16)
        out[...] = block
        sums[...] = jnp.sum(block.astype(F32), axis=0, keepdims=True)

    return pl.pallas_call(
        kernel,
        out_shape=[
            jax.ShapeDtypeStruct((rows, hidden), BF16),
            jax.ShapeDtypeStruct((1, hidden), F32),
        ],
        grid=(hidden // tile,),
        in_specs=[
            pl.BlockSpec((rows, width), lambda j: (0, 0)),
            pl.BlockSpec((tile, width), lambda j: (j, 0)),
            pl.BlockSpec((rows, tile), lambda j: (0, j)),
        ],
        out_specs=[
            pl.BlockSpec((rows, tile), lambda j: (0, j)),
            pl.BlockSpec((1, tile), lambda j: (0, j)),
        ],
        compiler_params=pltpu.CompilerParams(vmem_limit_bytes=14 << 20),
        cost_estimate=pl.CostEstimate(flops=0, bytes_accessed=0, transcendentals=0),
        name="gelu_back",
    )(grad_b, weight, slope)


def norm_back(grad_b, weight, unit, gain, scale, passed, keep_wide):
    rows, depth = grad_b.shape
    width = weight.shape[0]
    tile = 1024
    steps = depth // tile

    def kernel(grad, weight, unit, gain, scale, passed, *refs):
        outs, total = refs[:-1], refs[-1]
        step = pl.program_id(0)
        part = back_dot(grad[...], weight[...])

        @pl.when(step == 0)
        def _():
            total[...] = part

        @pl.when(step > 0)
        def _():
            total[...] += part

        @pl.when(step == steps - 1)
        def _():
            whole, u = total[...], unit[...]
            normed = whole * gain[...]
            out = passed[...].astype(F32) + standardize_back(normed, u, scale[...])
            out_b = out.astype(BF16)
            outs[0][...] = out_b
            outs[1][0:1] = jnp.sum(whole * u, axis=0, keepdims=True)
            outs[1][1:2] = jnp.sum(whole, axis=0, keepdims=True)
            outs[1][2:3] = jnp.sum(out_b.astype(F32), axis=0, keepdims=True)
            if keep_wide:
                outs[2][...] = out

    def once(shape):
        return pl.BlockSpec(shape, lambda j: (0, 0), pipeline_mode=pl.Buffered(1))

    shapes = [((rows, width), BF16), ((8, width), F32)]
    shapes += [((rows, width), F32)] if keep_wide else []
    return pl.pallas_call(
        kernel,
        out_shape=[jax.ShapeDtypeStruct(*s) for s in shapes],
        grid=(steps,),
        in_specs=[
            pl.BlockSpec((rows, tile), lambda j: (0, j)),
            pl.BlockSpec((width, tile), lambda j: (0, j)),
            once((rows, width)),
            once((1, width)),
            once((rows, 1)),
            once((rows, width)),
        ],
        out_specs=[once(shape) for shape, _ in shapes],
        scratch_shapes=[pltpu.VMEM((rows, width), F32)],
        compiler_params=pltpu.CompilerParams(vmem_limit_bytes=16 << 20),
        cost_estimate=pl.CostEstimate(flops=0, bytes_accessed=0, transcendentals=0),
        name="norm_back",
    )(grad_b, pltpu.with_memory_space_constraint(weight, pltpu.HBM), unit, gain, scale, passed)


def standardize(values):
    centered = values - jnp.mean(values, axis=-1, keepdims=True)
    scale = lax.rsqrt(jnp.mean(centered * centered, axis=-1, keepdims=True) + EPSILON)
    return centered * scale, scale


def standardize_back(grad, unit, scale):
    return scale * (
        grad
        - jnp.mean(grad, axis=-1, keepdims=True)
        - unit * jnp.mean(grad * unit, axis=-1, keepdims=True)
    )


def col_sum(values):
    return jnp.sum(values.astype(F32), axis=0)


def on_device(
    n_dp,
    n_z,
    rows_in,
    cotangent,
    lengths,
    deal_order,
    w_qkv,
    b_query,
    b_value,
    w_out,
    b_out,
    gain_one,
    shift_one,
    w_up,
    b_up,
    w_down,
    b_down,
    gain_two,
    shift_two,
):
    grid = Grid(n_dp, n_z)
    grid.bind()
    clock = Clock()
    devices = n_dp * n_z
    row_count, _, width = rows_in.shape
    hidden = w_up.shape[1]
    share = width // devices

    early = make_lines(grid, clock, jnp.concatenate([w_qkv, w_out], axis=1))
    middle = make_lines(grid, clock, w_up)
    late = make_lines(grid, clock, w_down)
    early.step0()

    target, send_rank, source, take_rank, first_len = routing(
        lengths, deal_order, devices, row_count, grid.me
    )
    slot_rows = row_count // devices + 1
    in_rows = slot_rows
    out_rows = 2 * slot_rows

    def selector(owner, rank, block_rows):
        at = (owner * block_rows + rank)[:, None]
        slot_ids = jnp.arange(devices * block_rows, dtype=jnp.int32)[None, :]
        return (at == slot_ids).astype(BF16)

    to_slots = selector(target, send_rank, in_rows)
    from_slots = selector(source, take_rank, in_rows)

    def both_of(owner, rank):
        at = owner * out_rows + rank
        return jnp.concatenate([at, at + slot_rows])

    out_slot_ids = jnp.arange(devices * out_rows, dtype=jnp.int32)
    take_both = (both_of(target, send_rank)[:, None] == out_slot_ids[None, :]).astype(BF16)
    send_both = (out_slot_ids[:, None] == both_of(source, take_rank)[None, :]).astype(BF16)

    def swap(block, lines=None):
        block = block.reshape(devices, -1, 128)
        if lines is not None:
            block = jnp.concatenate([block, lines], axis=1)
        block = lax.all_to_all(block, AXES, split_axis=0, concat_axis=0, tiled=True)
        if lines is None:
            return block.reshape(-1, width)
        height = block.shape[1] - lines.shape[1]
        return block[:, :height].reshape(-1, width), block[:, height:]

    vectors = jnp.stack(
        [b_query, b_value, b_out, gain_one, shift_one, b_down, gain_two, shift_two]
    )
    groups = 128 // share
    spot = grid.me % groups
    at_spot = lax.broadcasted_iota(jnp.int32, (8, 128), 1) // share == spot
    vectors = jnp.where(at_spot, jnp.tile(vectors, (1, groups)), jnp.zeros((), BF16))
    bias_groups = max(1, 128 * devices // hidden)
    bias = jnp.tile(b_up[None, :], (1, bias_groups))
    at_bias = lax.broadcasted_iota(jnp.int32, (1, 128), 1) // b_up.shape[0]
    bias = jnp.where(at_bias == grid.me % bias_groups, bias, jnp.zeros((), BF16))
    bias = jnp.pad(bias, ((0, 7), (0, 0)))
    small = jnp.concatenate([vectors, bias], axis=0)
    early.step1()
    middle.step0()
    to_slots, own_rows = clock.gate(to_slots, rows_in)
    block = contract_rows(to_slots, own_rows.reshape(row_count, width))
    block = block.astype(BF16)
    clock.tick(block)
    (attn,) = early.step2()
    attn.step0()
    middle.step1()
    small = jnp.broadcast_to(small[None], (devices, *small.shape))
    arrived, small_all = swap(clock.gate(block), small)
    attn.step1()
    attn.step2()
    (up,) = middle.step2()
    up.step0()
    late.step0()
    attn.step3()
    arrived, small_all = clock.gate(arrived, small_all)
    inputs = jnp.dot(from_slots, arrived, preferred_element_type=F32)
    lines = jnp.sum(small_all[:, :8].astype(F32).reshape(-1, groups, 8, 128), axis=1)
    bq, bv, bo, g1, s1, bd, g2, s2 = [
        v[None, :] for v in jnp.swapaxes(lines, 0, 1).reshape(8, width)
    ]
    lines = jnp.sum(small_all[:, 8].astype(F32).reshape(-1, bias_groups, 128), axis=1)
    bu = lines.reshape(1, hidden)
    unit_one, scale_one = standardize(inputs)
    normed_one_b = (unit_one * g1 + s1).astype(BF16)
    clock.tick(normed_one_b)
    cot_block = contract_rows(to_slots, clock.gate(cotangent).reshape(row_count, width))
    cot_block = cot_block.astype(BF16)
    clock.tick(cot_block)
    arrived_cot = swap(cot_block)
    late.step1()
    take_both, send_both = clock.gate(take_both, send_both)
    clock.tick(take_both, send_both)
    up.step1()
    up.step2()
    (down,) = late.step2()
    down.step0()
    full_qkv, full_out = attn.done((3 * width,))
    mixed = jnp.dot(clock.gate(normed_one_b), full_qkv, preferred_element_type=F32)
    mixed_b = (mixed + jnp.concatenate([bq, jnp.zeros_like(bq), bv], axis=1)).astype(BF16)
    attended_b = attend(first_len, mixed_b)
    clock.tick(attended_b)
    arrived_cot = clock.gate(arrived_cot)
    grad_m_b = jnp.dot(from_slots, arrived_cot, preferred_element_type=F32)
    grad_m_b = grad_m_b.astype(BF16)
    clock.tick(grad_m_b)
    up.step3()
    attended_b = clock.gate(attended_b)
    hidden_one = inputs + jnp.dot(attended_b, full_out, preferred_element_type=F32) + bo
    unit_two, scale_two = standardize(hidden_one)
    normed_two_b = (unit_two * g2 + s2).astype(BF16)
    clock.tick(normed_two_b)

    (full_up,) = up.done()
    down.step1()
    down.step2()
    pre_act = jnp.dot(clock.gate(normed_two_b), full_up, preferred_element_type=F32) + bu
    half_cdf = 0.5 * (1.0 + lax.erf(pre_act * (0.5**0.5)))
    activation_b = (pre_act * half_cdf).astype(BF16)
    density = jnp.exp(-0.5 * pre_act * pre_act) * ((2.0 * jnp.pi) ** -0.5)
    slope = half_cdf + pre_act * density
    clock.tick(activation_b, slope)

    term_b_down = col_sum(grad_m_b)[None, :]
    for_down = make_scatter(grid, clock, (activation_b, grad_m_b))
    for_down.across()
    down.step3()
    (full_down,) = down.done()
    grad_pre_b, term_b_up = gelu_back(clock.gate(grad_m_b), full_down, slope)
    clock.tick(grad_pre_b)
    for_down.first()
    for_up = make_scatter(grid, clock, (normed_two_b, grad_pre_b))
    for_up.across()

    grad_branch_b, sums_two, grad_hidden = norm_back(
        clock.gate(grad_pre_b), full_up, unit_two, g2, scale_two, grad_m_b, True
    )
    clock.tick(grad_branch_b)
    for_up.first()
    for_down.second()
    grad_att_b = back_dot(clock.gate(grad_branch_b), full_out).astype(BF16)
    clock.tick(grad_att_b)
    grad_mixed_b, term_mixed = attend_back(first_len, mixed_b, clock.gate(grad_att_b))
    clock.tick(grad_mixed_b)
    for_attn = make_scatter(
        grid, clock, (normed_one_b, grad_mixed_b), (attended_b, grad_branch_b)
    )
    for_attn.across()

    grad_inputs_b, sums_one = norm_back(
        clock.gate(grad_mixed_b), full_qkv, unit_one, g1, scale_one, grad_hidden, False
    )
    clock.tick(grad_inputs_b)
    for_attn.first()
    for_up.second()
    for_down.third()
    result = jnp.dot(clock.gate(activation_b), full_down, preferred_element_type=F32)
    result_b = (hidden_one + result + bd).astype(BF16)
    term_mixed, sums_one, sums_two, term_b_down, term_b_up, result_b = clock.gate(
        term_mixed, sums_one, sums_two, term_b_down, term_b_up, result_b
    )
    terms = [term_mixed[:, :width], term_mixed[:, 2 * width :], sums_two[2:3], sums_one[:2]]
    terms = jnp.concatenate([*terms, term_b_down, sums_two[:2]], axis=0).astype(BF16)
    lines = jnp.swapaxes(terms.reshape(8, -1, 128), 0, 1)
    lines = jnp.repeat(lines, groups, axis=0)
    bias = jnp.repeat(term_b_up.astype(BF16).reshape(-1, 1, 128), bias_groups, axis=0)
    lines = jnp.concatenate([lines, jnp.pad(bias, ((0, 0), (0, 7), (0, 0)))], axis=1)
    both = jnp.concatenate([result_b, grad_inputs_b], axis=0)
    block = jnp.dot(send_both, both, preferred_element_type=F32)
    block = block.astype(BF16)
    clock.tick(block)
    returned, small_back = swap(block, lines)

    for_up.third()
    for_attn.second()
    for_down.fourth()
    returned, small_back = clock.gate(returned, small_back)
    clock.tick(returned)
    for_attn.third()
    for_up.fourth()
    for_attn.fourth()
    returned = clock.gate(returned)
    placed = jnp.dot(take_both, returned, preferred_element_type=F32)
    placed = placed.astype(BF16)
    rows_out, grad_rows = placed[:row_count], placed[row_count:]
    sums = jnp.sum(small_back.astype(F32), axis=0)
    clock.tick(placed)
    (grad_w_down,) = for_down.done()
    (grad_w_up,) = for_up.done()
    grad_w_qkv, grad_w_out = for_attn.done()

    mine = lax.dynamic_slice_in_dim(sums[:8], spot * share, share, axis=1)
    grad_bq, grad_bv, grad_bo, grad_g1, grad_s1, grad_bd, grad_g2, grad_s2 = mine
    bias_width = hidden // devices
    grad_bu = lax.dynamic_slice_in_dim(
        sums[8], (grid.me % bias_groups) * bias_width, bias_width, axis=0
    )
    return (
        rows_out.reshape(row_count, 1, width),
        grad_rows.reshape(row_count, 1, width),
        grad_w_qkv,
        grad_bq,
        grad_bv,
        grad_w_out,
        grad_bo,
        grad_g1,
        grad_s1,
        grad_w_up,
        grad_bu,
        grad_w_down,
        grad_bd,
        grad_g2,
        grad_s2,
    )


def solution(mesh):
    n_dp, n_z = mesh.shape["dp"], mesh.shape["fsdp"]
    rows, vec, mat = P(None, AXES, None), P(AXES), P(AXES, None)

    def run(*args):
        return on_device(n_dp, n_z, *args)

    return jax.shard_map(
        run,
        mesh=mesh,
        in_specs=(rows, rows, P(), P())
        + (mat, vec, vec, mat, vec, vec, vec, mat, vec, mat, vec, vec, vec),
        out_specs=(rows, rows, mat, vec, vec, mat, vec, vec, vec, mat, vec, mat, vec, vec, vec),
        check_vma=False,
    )
```

```python
import jax
import jax.numpy as jnp
from jax import lax
from jax.experimental import pallas as pl
from jax.experimental.pallas import tpu as pltpu
from jax.sharding import PartitionSpec as P

HEADS = 16
HEAD_DIM = 64
EPSILON = 1e-05
AXES = ("dp", "fsdp")
BF16 = jnp.bfloat16
F32 = jnp.float32


class Grid:
    def __init__(self, n_dp, n_z):
        self.n_dp, self.n_z = n_dp, n_z
        side = 1
        while side * side * 2 < n_dp:
            side *= 2
        self.nx, self.ny = side, n_dp // (2 * side)
        self.x_masks = [2 * k for k in range(1, self.nx)]
        self.y_masks = [2 * side * k for k in range(1, self.ny)]
        self.z_masks = list(range(1, n_z))
        self.square = self.nx == self.ny == 2 and n_z == 4

    def bind(self):
        self.my_dp = lax.axis_index("dp").astype(jnp.int32)
        self.my_z = lax.axis_index("fsdp").astype(jnp.int32)
        self.me = lax.axis_index(AXES).astype(jnp.int32)

    def over_dp(self, value, mask):
        return lax.ppermute(value, "dp", [(i, i ^ mask) for i in range(self.n_dp)])

    def crossed(self, value, even_mask, odd_mask):
        pairs = [(i, i ^ (odd_mask if i % 2 else even_mask)) for i in range(self.n_dp)]
        return lax.ppermute(value, "dp", pairs)

    def over_z(self, value, mask):
        return lax.ppermute(value, "fsdp", [(i, i ^ mask) for i in range(self.n_z)])


class Clock:
    def __init__(self):
        self.last = ()

    def gate(self, *values):
        held = lax.optimization_barrier(tuple(values) + self.last)[: len(values)]
        return held if len(values) > 1 else held[0]

    def tick(self, *values):
        self.last = values


class Lines:
    def __init__(self, grid, clock, shards):
        self.grid, self.clock = grid, clock
        self.block = shards[0].shape[0]
        self.parts, blocks = [], []
        at = 0
        for shard in shards:
            height, cols = shard.shape
            count = height // self.block
            blocks += [shard[k * self.block : (k + 1) * self.block] for k in range(count)]
            self.parts.append((at, count, cols))
            at += count * cols
        self.shard = jnp.concatenate(blocks, axis=1) if len(blocks) > 1 else blocks[0]

    def step0(self):
        self.held = self.clock.gate(self.shard)
        self.far = [m for m in self.grid.z_masks if m % 2 == 0]
        self.coming = [self.grid.over_z(self.held, m) for m in self.far]

    def step1(self):
        *got, held = self.clock.gate(*self.coming, self.held)
        self.held = jnp.concatenate([held, *got], 0)
        self.clock.tick(self.held)
        self.coming = self.grid.over_z(self.held, 1)

    def step2(self):
        got, held = self.clock.gate(self.coming, self.held)
        z_marks = [0] + self.far
        z_marks += [m ^ 1 for m in z_marks]
        joined = []
        for at, count, cols in self.parts:
            cut = slice(at, at + count * cols)
            joined.append(jnp.concatenate([held[:, cut], got[:, cut]], 0))
        self.clock.tick(*joined)
        return [
            Gather(self.grid, self.clock, rows, z_marks, self.block, count, cols)
            for rows, (_, count, cols) in zip(joined, self.parts)
        ]


class Gather:
    def __init__(self, grid, clock, rows, z_marks, block, count, cols):
        self.grid, self.clock, self.rows = grid, clock, rows
        self.z_marks, self.block, self.count, self.cols = z_marks, block, count, cols
        self.pieces = []

    def take(self, rows, even_mask, odd_mask):
        self.pieces.append((rows, even_mask, odd_mask))
        self.crossing = (self.grid.over_dp(rows, 1), odd_mask ^ 1, even_mask ^ 1)

    def land(self, coming):
        rows, crossed = self.clock.gate(coming, self.crossing[0])
        self.pieces.append((crossed, *self.crossing[1:]))
        self.clock.tick(rows)
        return rows

    def step0(self):
        grid = self.grid
        (x,), (y,) = grid.x_masks, grid.y_masks
        rows = self.clock.gate(self.rows)
        self.first = grid.crossed(rows, x, y)
        self.second = grid.crossed(rows, y, x)
        self.take(rows, 0, 0)

    def step1(self):
        grid = self.grid
        (x,), (y,) = grid.x_masks, grid.y_masks
        first = self.land(self.first)
        self.third = grid.crossed(first, y, x)
        self.take(first, x, y)

    def step2(self):
        (x,), (y,) = self.grid.x_masks, self.grid.y_masks
        self.take(self.land(self.second), y, x)

    def step3(self):
        (x,), (y,) = self.grid.x_masks, self.grid.y_masks
        self.take(self.land(self.third), x ^ y, x ^ y)
        self.pieces.append(self.crossing)

    def done(self, cuts=()):
        grid, block, count = self.grid, self.block, self.count
        pieces, z_marks = self.pieces, self.z_marks
        owners = grid.n_dp * grid.n_z
        edges = [0, *cuts, self.cols]
        spans = list(zip(edges[:-1], edges[1:]))
        copies = owners * count * len(spans)

        def kernel(me_ref, *refs):
            sources = refs[: len(pieces)]
            results = refs[len(pieces) : len(pieces) + len(spans)]
            sems = refs[-1]
            me = me_ref[0]
            odd = (me // grid.n_z) % 2 == 1
            started = []
            for source, (_, even_mask, odd_mask) in zip(sources, pieces):
                mask = jnp.where(odd, jnp.int32(odd_mask), jnp.int32(even_mask))
                for at, z in enumerate(z_marks):
                    owner = lax.bitwise_xor(me, mask * grid.n_z + z)
                    for k in range(count):
                        to = pl.multiple_of((owner * count + k) * block, block)
                        for result, (lo, hi) in zip(results, spans):
                            copy = pltpu.make_async_copy(
                                source.at[
                                    pl.ds(at * block, block), pl.ds(k * self.cols + lo, hi - lo)
                                ],
                                result.at[pl.ds(to, block)],
                                sems.at[len(started)],
                            )
                            copy.start()
                            started.append(copy)
            for copy in started:
                copy.wait()

        arrays = self.clock.gate(*[v for v, _, _ in pieces])
        rows = owners * count * block
        full = pl.pallas_call(
            kernel,
            out_shape=[jax.ShapeDtypeStruct((rows, hi - lo), BF16) for lo, hi in spans],
            grid_spec=pltpu.PrefetchScalarGridSpec(
                num_scalar_prefetch=1,
                grid=(),
                in_specs=[pl.BlockSpec(memory_space=pl.ANY)] * len(pieces),
                out_specs=[pl.BlockSpec(memory_space=pltpu.VMEM)] * len(spans),
                scratch_shapes=[pltpu.SemaphoreType.DMA((copies,))],
            ),
            compiler_params=pltpu.CompilerParams(vmem_limit_bytes=10 << 20),
            cost_estimate=pl.CostEstimate(flops=0, bytes_accessed=0, transcendentals=0),
            name="assemble",
        )(grid.me.reshape(1), *arrays)
        self.clock.tick(*full)
        return full


class PlainLines:
    def __init__(self, grid, clock, shards):
        self.shards = shards

    def step0(self):
        pass

    step1 = step0

    def step2(self):
        return [PlainGather(v) for v in self.shards]


class PlainGather:
    def __init__(self, shard):
        self.full = lax.all_gather(shard, AXES, axis=0, tiled=True)

    def step0(self):
        pass

    step1 = step2 = step3 = step0

    def done(self, cuts=()):
        edges = [0, *cuts, self.full.shape[1]]
        return [self.full[:, lo:hi] for lo, hi in zip(edges[:-1], edges[1:])]


def make_lines(grid, clock, *shards):
    plain = shards[0].shape[0] % 16 or not grid.square
    kind = PlainLines if plain else Lines
    return kind(grid, clock, shards)


def contract_rows(left, right):
    return lax.dot_general(left, right, (((0,), (0,)), ((), ())), preferred_element_type=F32)


def back_dot(grad_rows, weight):
    return lax.dot_general(grad_rows, weight, (((1,), (1,)), ((), ())), preferred_element_type=F32)


def pick(array, index):
    return lax.dynamic_index_in_dim(array, index, 0, keepdims=False)


def total_of(base, parts):
    for part in parts:
        base = base + part.astype(F32)
    return base


class Scatter:
    places = 4

    def __init__(self, grid, clock, lefts, rights):
        self.grid, self.clock, self.lefts, self.rights = grid, clock, lefts, rights
        self.chunk = lefts[0].shape[1] // grid.n_dp
        self.cols = sum(right.shape[1] for right in rights)
        once = pl.Buffered(1)
        self.rows = [
            pl.BlockSpec(right.shape, lambda j, dp: (0, 0), pipeline_mode=once) for right in rights
        ]

    def call(self, other, ins, shapes, targets):
        tokens, count, places = self.lefts[0].shape[0], len(self.lefts), self.places
        added = len(ins)

        def place(j, dp):
            a, b = j // 2, j % 2
            odd = (dp[0] + other) % 2
            mask = jnp.where(odd == 1, 2 * a + 4 * b, 4 * a + 2 * b)
            return 0, lax.bitwise_xor(dp[0], mask + other)

        def kernel(dp_ref, *refs):
            lefts, rights, refs = refs[:count], refs[count : 2 * count], refs[2 * count :]
            gots, outs = refs[:added], refs[added : added + len(shapes)]
            blocks, out_sems, *fetched = refs[added + len(shapes) :]
            step = pl.program_id(0)

            def fetch(k):
                return pltpu.make_async_copy(gots[k], fetched[0].at[k], fetched[1].at[k])

            def put(k):
                return pltpu.make_async_copy(blocks.at[k], targets(outs)[k], out_sems.at[k])

            if added:

                @pl.when(step == 0)
                def _():
                    for k in range(places):
                        fetch(k).start()

            terms = [contract_rows(a[...], b[...]) for a, b in zip(lefts, rights)]
            term = jnp.concatenate(terms, axis=1) if count > 1 else terms[0]
            for k in range(places):

                @pl.when(step == k)
                def _(k=k):
                    whole = term
                    if added:
                        fetch(k).wait()
                        whole = whole + fetched[0][k].astype(F32)
                    blocks[k] = whole.astype(BF16)
                    put(k).start()

            @pl.when(step == places - 1)
            def _():
                for k in range(places):
                    put(k).wait()

        anywhere = pl.BlockSpec(memory_space=pl.ANY)
        scratch = [
            pltpu.VMEM((places, self.chunk, self.cols), BF16),
            pltpu.SemaphoreType.DMA((places,)),
        ]
        ins = self.clock.gate(*self.lefts, *self.rights, *ins)
        return pl.pallas_call(
            kernel,
            out_shape=shapes,
            grid_spec=pltpu.PrefetchScalarGridSpec(
                num_scalar_prefetch=1,
                grid=(places,),
                in_specs=[
                    *[pl.BlockSpec((tokens, self.chunk), place) for _ in self.lefts],
                    *self.rows,
                    *[anywhere] * added,
                ],
                out_specs=[anywhere] * len(shapes),
                scratch_shapes=scratch * (2 if added else 1),
            ),
            compiler_params=pltpu.CompilerParams(vmem_limit_bytes=20 << 20),
            cost_estimate=pl.CostEstimate(flops=0, bytes_accessed=0, transcendentals=0),
            name="outer",
        )(self.grid.my_dp.reshape(1), *ins)

    def across(self):
        shapes = [jax.ShapeDtypeStruct((self.chunk, self.cols), BF16)] * self.places
        sends = self.call(1, (), shapes, lambda outs: outs)
        self.clock.tick(*sends)
        self.got = [self.grid.over_dp(v, 1) for v in sends]

    def first(self):
        grid = self.grid
        (x,), (y,) = grid.x_masks, grid.y_masks
        one = jax.ShapeDtypeStruct((self.chunk, self.cols), BF16)
        pair = jax.ShapeDtypeStruct((2, self.chunk, self.cols), BF16)
        keep, pass_on, far = self.call(
            0,
            self.got,
            [one, one, pair],
            lambda outs: (outs[0], outs[1], outs[2].at[0], outs[2].at[1]),
        )
        self.clock.tick(far)
        self.keep, self.pass_on = keep, pass_on
        self.got = grid.crossed(far, y, x)

    def second(self):
        (x,), (y,) = self.grid.x_masks, self.grid.y_masks
        got, pass_on = self.clock.gate(self.got, self.pass_on)
        send = (pass_on.astype(F32) + got[1].astype(F32)).astype(BF16)
        self.clock.tick(send)
        self.aside = got[0]
        self.got = self.grid.crossed(send, x, y)

    def land(self):
        self.got = self.clock.gate(self.got)
        self.clock.tick(self.got)

    def third(self):
        grid = self.grid
        got, keep = self.clock.gate(self.got, self.keep)
        lines = total_of(keep.astype(F32), [got, self.aside]).reshape(2, 2, -1, self.cols)
        odd = grid.my_z % 2
        send = lax.dynamic_index_in_dim(lines, 1 - odd, 1, keepdims=False).astype(BF16)
        self.keep = lax.dynamic_index_in_dim(lines, odd, 1, keepdims=False)
        self.clock.tick(send)
        self.got = grid.over_z(send, 1)

    def fourth(self):
        grid = self.grid
        got, keep = self.clock.gate(self.got, self.keep)
        held = keep + got.astype(F32)
        pair = grid.my_z // 2
        send = pick(held, 1 - pair).astype(BF16)
        self.keep = pick(held, pair)
        self.clock.tick(send)
        self.got = grid.over_z(send, 2)

    def done(self):
        got, keep = self.clock.gate(self.got, self.keep)
        outs, at = [], 0
        for right in self.rights:
            cut = slice(at, at + right.shape[1])
            outs.append(keep[:, cut] + got[:, cut].astype(F32))
            at += right.shape[1]
        self.clock.tick(*outs)
        return outs


class PlainScatter:
    def __init__(self, lefts, rights):
        self.terms = [contract_rows(a, b) for a, b in zip(lefts, rights)]

    def across(self):
        pass

    first = second = land = third = fourth = across

    def done(self):
        return [lax.psum_scatter(t, AXES, scatter_dimension=0, tiled=True) for t in self.terms]


def make_scatter(grid, clock, *pairs):
    lefts, rights = [a for a, _ in pairs], [b for _, b in pairs]
    if (lefts[0].shape[1] // grid.n_dp) % 128 or not grid.square:
        return PlainScatter(lefts, rights)
    return Scatter(grid, clock, lefts, rights)


def lookup(small_table, index_rows):
    matches = index_rows[:, None] == jnp.arange(small_table.shape[0], dtype=jnp.int32)[None, :]
    return jnp.sum(jnp.where(matches, small_table[None, :], 0), axis=1)


def rank_among(group_label, order_key):
    earlier = (group_label[None, :] == group_label[:, None]) & (
        order_key[None, :] < order_key[:, None]
    )
    return jnp.sum(earlier.astype(jnp.int32), axis=1)


def routing(lengths, deal_order, devices, row_count, device):
    slot_count = deal_order.shape[0]
    slot_ids = jnp.arange(slot_count, dtype=jnp.int32)
    starts = jnp.cumsum(lengths) - lengths
    slot_of = jnp.sum(
        jnp.where(deal_order[None, :] == slot_ids[:, None], slot_ids[None, :], 0), axis=1
    )
    slot_lengths = lookup(lengths, deal_order)
    local_rows = jnp.arange(row_count, dtype=jnp.int32)
    token_index = local_rows * devices + device
    sequence = jnp.sum((starts[None, :] <= token_index[:, None]).astype(jnp.int32), axis=1) - 1
    slot_index = lookup(slot_of, sequence)
    target = slot_index // 2
    send_rank = rank_among(target, local_rows)
    first_len = lax.dynamic_index_in_dim(slot_lengths, 2 * device, 0, False)
    second = local_rows >= first_len
    first_seq = lax.dynamic_index_in_dim(deal_order, 2 * device, 0, False)
    second_seq = lax.dynamic_index_in_dim(deal_order, 2 * device + 1, 0, False)
    sequence_here = jnp.where(second, second_seq, first_seq)
    position = local_rows - jnp.where(second, first_len, 0)
    source_token = lookup(starts, sequence_here) + position
    source = source_token % devices
    take_rank = rank_among(source, source_token)
    return target, send_rank, source, take_rank, first_len.reshape(1)


HEADS_AT_ONCE = 4
LANES = HEADS_AT_ONCE * HEAD_DIM


def head_probs(query, key, first_len):
    scores = back_dot(query, key)
    q_at = lax.broadcasted_iota(jnp.int32, scores.shape, 0)
    k_at = lax.broadcasted_iota(jnp.int32, scores.shape, 1)
    allowed = (k_at <= q_at) & ((q_at < first_len) | (k_at >= first_len))
    masked = jnp.where(allowed, scores, -1000000000.0)
    exps = jnp.exp(masked - jnp.max(masked, axis=-1, keepdims=True))
    return exps * (1.0 / jnp.sum(exps, axis=-1, keepdims=True))


def of_heads(rows, parts):
    head = lax.broadcasted_iota(jnp.int32, (rows, LANES), 1) // HEAD_DIM
    whole = parts[0]
    for k in range(1, len(parts)):
        whole = jnp.where(head == k, parts[k], whole)
    return whole


def one_head(values, k):
    head = lax.broadcasted_iota(jnp.int32, values.shape, 1) // HEAD_DIM
    return jnp.where(head == k, values, jnp.zeros((), BF16))


def attend(first_len, mixed_b):
    rows, width = mixed_b.shape[0], mixed_b.shape[1] // 3
    steps = width // LANES

    def kernel(first_ref, query, key, value, out):
        scaled = query[...] * jnp.asarray(HEAD_DIM**-0.5, BF16)
        probs = [
            head_probs(one_head(scaled, k), key[...], first_ref[0]).astype(BF16)
            for k in range(HEADS_AT_ONCE)
        ]
        found = [jnp.dot(p, value[...], preferred_element_type=F32) for p in probs]
        out[...] = of_heads(rows, found).astype(BF16)

    def part(k):
        return pl.BlockSpec((rows, LANES), lambda h, first: (0, k * steps + h))

    return pl.pallas_call(
        kernel,
        out_shape=jax.ShapeDtypeStruct((rows, width), BF16),
        grid_spec=pltpu.PrefetchScalarGridSpec(
            num_scalar_prefetch=1,
            grid=(steps,),
            in_specs=[part(0), part(1), part(2)],
            out_specs=part(0),
        ),
        compiler_params=pltpu.CompilerParams(vmem_limit_bytes=10 << 20),
        cost_estimate=pl.CostEstimate(flops=0, bytes_accessed=0, transcendentals=0),
        name="attend",
    )(first_len, mixed_b, mixed_b, mixed_b)


def attend_back(first_len, mixed_b, grad_att_b):
    rows, width = grad_att_b.shape
    steps = width // LANES

    def kernel(first_ref, query, key, value, grad, out, sums):
        h = pl.program_id(0)
        scaled = query[...] * jnp.asarray(HEAD_DIM**-0.5, BF16)
        to_query, to_key, to_value = [], [], []
        for k in range(HEADS_AT_ONCE):
            q, g = one_head(scaled, k), one_head(grad[...], k)
            probs = head_probs(q, key[...], first_ref[0])
            grad_probs = back_dot(g, value[...])
            dots = jnp.sum(probs * grad_probs, axis=-1, keepdims=True)
            grad_scores = (probs * (grad_probs - dots)).astype(BF16)
            to_query.append(jnp.dot(grad_scores, key[...], preferred_element_type=F32))
            to_key.append(contract_rows(grad_scores, q))
            to_value.append(contract_rows(probs.astype(BF16), g))
        results = (of_heads(rows, to_query) * HEAD_DIM**-0.5, sum(to_key), sum(to_value))
        for k, block in enumerate(results):
            block = block.astype(BF16)
            at = pl.multiple_of(k * width + h * LANES, LANES)
            out[:, pl.ds(at, LANES)] = block
            sums[:, pl.ds(at, LANES)] = jnp.sum(block.astype(F32), axis=0, keepdims=True)

    def part(k):
        return pl.BlockSpec((rows, LANES), lambda h, first: (0, k * steps + h))

    return pl.pallas_call(
        kernel,
        out_shape=[
            jax.ShapeDtypeStruct((rows, 3 * width), BF16),
            jax.ShapeDtypeStruct((1, 3 * width), F32),
        ],
        grid_spec=pltpu.PrefetchScalarGridSpec(
            num_scalar_prefetch=1,
            grid=(steps,),
            in_specs=[part(0), part(1), part(2), part(0)],
            out_specs=[
                pl.BlockSpec((rows, 3 * width), lambda h, first: (0, 0)),
                pl.BlockSpec((1, 3 * width), lambda h, first: (0, 0)),
            ],
        ),
        compiler_params=pltpu.CompilerParams(vmem_limit_bytes=16 << 20),
        cost_estimate=pl.CostEstimate(flops=0, bytes_accessed=0, transcendentals=0),
        name="attend_back",
    )(first_len, mixed_b, mixed_b, mixed_b, grad_att_b)


def gelu_back(grad_b, weight, slope):
    rows, width = grad_b.shape
    hidden = weight.shape[0]
    tile = min(1024, hidden)

    def kernel(grad, weight, slope, out, sums):
        block = (back_dot(grad[...], weight[...]) * slope[...]).astype(BF16)
        out[...] = block
        sums[...] = jnp.sum(block.astype(F32), axis=0, keepdims=True)

    return pl.pallas_call(
        kernel,
        out_shape=[
            jax.ShapeDtypeStruct((rows, hidden), BF16),
            jax.ShapeDtypeStruct((1, hidden), F32),
        ],
        grid=(hidden // tile,),
        in_specs=[
            pl.BlockSpec((rows, width), lambda j: (0, 0)),
            pl.BlockSpec((tile, width), lambda j: (j, 0)),
            pl.BlockSpec((rows, tile), lambda j: (0, j)),
        ],
        out_specs=[
            pl.BlockSpec((rows, tile), lambda j: (0, j)),
            pl.BlockSpec((1, tile), lambda j: (0, j)),
        ],
        compiler_params=pltpu.CompilerParams(vmem_limit_bytes=14 << 20),
        cost_estimate=pl.CostEstimate(flops=0, bytes_accessed=0, transcendentals=0),
        name="gelu_back",
    )(grad_b, weight, slope)


def in_hbm(array):
    return pltpu.with_memory_space_constraint(array, pltpu.HBM)


def norm_back(grad_b, weight, unit, gain, scale, passed, keep_wide):
    rows, depth = grad_b.shape
    width = weight.shape[0]
    tile = 1024
    steps = depth // tile

    def kernel(grad, weight, unit_at, gain, scale, passed_at, *refs):
        outs, (total, unit, passed, sems) = refs[:-4], refs[-4:]
        step = pl.program_id(0)
        fetches = [
            pltpu.make_async_copy(unit_at, unit, sems.at[0]),
            pltpu.make_async_copy(passed_at, passed, sems.at[1]),
        ]
        part = back_dot(grad[...], weight[...])

        @pl.when(step == 0)
        def _():
            for fetch in fetches:
                fetch.start()
            total[...] = part

        @pl.when(step > 0)
        def _():
            total[...] += part

        @pl.when(step == steps - 1)
        def _():
            for fetch in fetches:
                fetch.wait()
            whole, u = total[...], unit[...]
            normed = whole * gain[...]
            outs[1][0:1] = jnp.sum(whole * u, axis=0, keepdims=True)
            outs[1][1:2] = jnp.sum(whole, axis=0, keepdims=True)
            out = passed[...].astype(F32) + standardize_back(normed, u, scale[...])
            if keep_wide:
                total[...] = out
                store = pltpu.make_async_copy(total, outs[2], sems.at[2])
                store.start()
            out_b = out.astype(BF16)
            outs[0][...] = out_b
            outs[1][2:3] = jnp.sum(out_b.astype(F32), axis=0, keepdims=True)
            if keep_wide:
                store.wait()

    def once(shape):
        return pl.BlockSpec(shape, lambda j: (0, 0), pipeline_mode=pl.Buffered(1))

    anywhere = pl.BlockSpec(memory_space=pl.ANY)
    shapes = [((rows, width), BF16), ((8, width), F32)]
    out_specs = [once(shape) for shape, _ in shapes]
    if keep_wide:
        shapes.append(((rows, width), F32))
        out_specs.append(anywhere)
    return pl.pallas_call(
        kernel,
        out_shape=[jax.ShapeDtypeStruct(*s) for s in shapes],
        grid=(steps,),
        in_specs=[
            pl.BlockSpec((rows, tile), lambda j: (0, j)),
            pl.BlockSpec((width, tile), lambda j: (0, j)),
            anywhere,
            once((1, width)),
            once((rows, 1)),
            anywhere,
        ],
        out_specs=out_specs,
        scratch_shapes=[
            pltpu.VMEM((rows, width), F32),
            pltpu.VMEM((rows, width), unit.dtype),
            pltpu.VMEM((rows, width), passed.dtype),
            pltpu.SemaphoreType.DMA((3,)),
        ],
        compiler_params=pltpu.CompilerParams(vmem_limit_bytes=16 << 20),
        cost_estimate=pl.CostEstimate(flops=0, bytes_accessed=0, transcendentals=0),
        name="norm_back",
    )(grad_b, in_hbm(weight), in_hbm(unit), gain, scale, in_hbm(passed))


def standardize(values):
    centered = values - jnp.mean(values, axis=-1, keepdims=True)
    scale = lax.rsqrt(jnp.mean(centered * centered, axis=-1, keepdims=True) + EPSILON)
    return centered * scale, scale


def standardize_back(grad, unit, scale):
    return scale * (
        grad
        - jnp.mean(grad, axis=-1, keepdims=True)
        - unit * jnp.mean(grad * unit, axis=-1, keepdims=True)
    )


def col_sum(values):
    return jnp.sum(values.astype(F32), axis=0)


def on_device(
    n_dp,
    n_z,
    rows_in,
    cotangent,
    lengths,
    deal_order,
    w_qkv,
    b_query,
    b_value,
    w_out,
    b_out,
    gain_one,
    shift_one,
    w_up,
    b_up,
    w_down,
    b_down,
    gain_two,
    shift_two,
):
    grid = Grid(n_dp, n_z)
    grid.bind()
    clock = Clock()
    devices = n_dp * n_z
    row_count, _, width = rows_in.shape
    hidden = w_up.shape[1]
    share = width // devices

    early = make_lines(grid, clock, jnp.concatenate([w_qkv, w_out], axis=1))
    middle = make_lines(grid, clock, w_up)
    late = make_lines(grid, clock, w_down)
    early.step0()

    target, send_rank, source, take_rank, first_len = routing(
        lengths, deal_order, devices, row_count, grid.me
    )
    slot_rows = row_count // devices + 1
    in_rows = slot_rows
    out_rows = 2 * slot_rows

    def selector(owner, rank, block_rows):
        at = (owner * block_rows + rank)[:, None]
        slot_ids = jnp.arange(devices * block_rows, dtype=jnp.int32)[None, :]
        return (at == slot_ids).astype(BF16)

    to_slots = selector(target, send_rank, in_rows)
    from_slots = selector(source, take_rank, in_rows)

    def both_of(owner, rank):
        at = owner * out_rows + rank
        return jnp.concatenate([at, at + slot_rows])

    out_slot_ids = jnp.arange(devices * out_rows, dtype=jnp.int32)
    take_both = (both_of(target, send_rank)[:, None] == out_slot_ids[None, :]).astype(BF16)
    send_both = (out_slot_ids[:, None] == both_of(source, take_rank)[None, :]).astype(BF16)

    def swap(block, lines=None):
        block = block.reshape(devices, -1, 128)
        if lines is not None:
            block = jnp.concatenate([block, lines], axis=1)
        block = lax.all_to_all(block, AXES, split_axis=0, concat_axis=0, tiled=True)
        if lines is None:
            return block.reshape(-1, width)
        height = block.shape[1] - lines.shape[1]
        return block[:, :height].reshape(-1, width), block[:, height:]

    vectors = jnp.stack(
        [b_query, b_value, b_out, gain_one, shift_one, b_down, gain_two, shift_two]
    )
    groups = 128 // share
    spot = grid.me % groups
    at_spot = lax.broadcasted_iota(jnp.int32, (8, 128), 1) // share == spot
    vectors = jnp.where(at_spot, jnp.tile(vectors, (1, groups)), jnp.zeros((), BF16))
    bias_groups = max(1, 128 * devices // hidden)
    bias = jnp.tile(b_up[None, :], (1, bias_groups))
    at_bias = lax.broadcasted_iota(jnp.int32, (1, 128), 1) // b_up.shape[0]
    bias = jnp.where(at_bias == grid.me % bias_groups, bias, jnp.zeros((), BF16))
    bias = jnp.pad(bias, ((0, 7), (0, 0)))
    small = jnp.concatenate([vectors, bias], axis=0)
    early.step1()
    middle.step0()
    to_slots, own_rows = clock.gate(to_slots, rows_in)
    block = contract_rows(to_slots, own_rows.reshape(row_count, width))
    block = block.astype(BF16)
    clock.tick(block)
    (attn,) = early.step2()
    attn.step0()
    middle.step1()
    small = jnp.broadcast_to(small[None], (devices, *small.shape))
    arrived, small_all = swap(clock.gate(block), small)
    attn.step1()
    attn.step2()
    (up,) = middle.step2()
    up.step0()
    late.step0()
    attn.step3()
    arrived, small_all = clock.gate(arrived, small_all)
    inputs = jnp.dot(from_slots, arrived, preferred_element_type=F32)
    lines = jnp.sum(small_all[:, :8].astype(F32).reshape(-1, groups, 8, 128), axis=1)
    bq, bv, bo, g1, s1, bd, g2, s2 = [
        v[None, :] for v in jnp.swapaxes(lines, 0, 1).reshape(8, width)
    ]
    lines = jnp.sum(small_all[:, 8].astype(F32).reshape(-1, bias_groups, 128), axis=1)
    bu = lines.reshape(1, hidden)
    unit_one, scale_one = standardize(inputs)
    normed_one_b = (unit_one * g1 + s1).astype(BF16)
    clock.tick(normed_one_b)
    cot_block = contract_rows(to_slots, clock.gate(cotangent).reshape(row_count, width))
    cot_block = cot_block.astype(BF16)
    clock.tick(cot_block)
    arrived_cot = swap(cot_block)
    late.step1()
    take_both, send_both = clock.gate(take_both, send_both)
    clock.tick(take_both, send_both)
    up.step1()
    up.step2()
    (down,) = late.step2()
    down.step0()
    full_qkv, full_out = attn.done((3 * width,))
    mixed = jnp.dot(clock.gate(normed_one_b), full_qkv, preferred_element_type=F32)
    mixed_b = (mixed + jnp.concatenate([bq, jnp.zeros_like(bq), bv], axis=1)).astype(BF16)
    attended_b = attend(first_len, mixed_b)
    clock.tick(attended_b)
    arrived_cot = clock.gate(arrived_cot)
    grad_m_b = jnp.dot(from_slots, arrived_cot, preferred_element_type=F32)
    grad_m_b = grad_m_b.astype(BF16)
    clock.tick(grad_m_b)
    up.step3()
    attended_b = clock.gate(attended_b)
    hidden_one = inputs + jnp.dot(attended_b, full_out, preferred_element_type=F32) + bo
    unit_two, scale_two = standardize(hidden_one)
    normed_two_b = (unit_two * g2 + s2).astype(BF16)
    clock.tick(normed_two_b)

    (full_up,) = up.done()
    down.step1()
    down.step2()
    pre_act = jnp.dot(clock.gate(normed_two_b), full_up, preferred_element_type=F32) + bu
    half_cdf = 0.5 * (1.0 + lax.erf(pre_act * (0.5**0.5)))
    activation_b = (pre_act * half_cdf).astype(BF16)
    density = jnp.exp(-0.5 * pre_act * pre_act) * ((2.0 * jnp.pi) ** -0.5)
    slope = half_cdf + pre_act * density
    clock.tick(activation_b, slope)

    term_b_down = col_sum(grad_m_b)[None, :]
    for_down = make_scatter(grid, clock, (activation_b, grad_m_b))
    for_down.across()
    down.step3()
    (full_down,) = down.done()
    grad_pre_b, term_b_up = gelu_back(clock.gate(grad_m_b), full_down, slope)
    clock.tick(grad_pre_b)
    for_down.first()
    for_up = make_scatter(grid, clock, (normed_two_b, grad_pre_b))
    for_up.across()

    grad_branch_b, sums_two, grad_hidden = norm_back(
        clock.gate(grad_pre_b), full_up, unit_two, g2, scale_two, grad_m_b, True
    )
    clock.tick(grad_branch_b)
    for_up.first()
    grad_att_b = back_dot(clock.gate(grad_branch_b), full_out).astype(BF16)
    clock.tick(grad_att_b)
    grad_mixed_b, term_mixed = attend_back(first_len, mixed_b, clock.gate(grad_att_b))
    clock.tick(grad_mixed_b)
    for_attn = make_scatter(
        grid, clock, (normed_one_b, grad_mixed_b), (attended_b, grad_branch_b)
    )
    for_down.land()
    for_attn.across()
    for_down.second()

    grad_inputs_b, sums_one = norm_back(
        clock.gate(grad_mixed_b), full_qkv, unit_one, g1, scale_one, grad_hidden, False
    )
    clock.tick(grad_inputs_b)
    for_attn.first()
    for_up.second()
    for_down.third()
    result = jnp.dot(clock.gate(activation_b), full_down, preferred_element_type=F32)
    result_b = (hidden_one + result + bd).astype(BF16)
    term_mixed, sums_one, sums_two, term_b_down, term_b_up, result_b = clock.gate(
        term_mixed, sums_one, sums_two, term_b_down, term_b_up, result_b
    )
    terms = [term_mixed[:, :width], term_mixed[:, 2 * width :], sums_two[2:3], sums_one[:2]]
    terms = jnp.concatenate([*terms, term_b_down, sums_two[:2]], axis=0).astype(BF16)
    lines = jnp.swapaxes(terms.reshape(8, -1, 128), 0, 1)
    lines = jnp.repeat(lines, groups, axis=0)
    bias = jnp.repeat(term_b_up.astype(BF16).reshape(-1, 1, 128), bias_groups, axis=0)
    lines = jnp.concatenate([lines, jnp.pad(bias, ((0, 0), (0, 7), (0, 0)))], axis=1)
    both = jnp.concatenate([result_b, grad_inputs_b], axis=0)
    block = jnp.dot(send_both, both, preferred_element_type=F32)
    block = block.astype(BF16)
    clock.tick(block)
    returned, small_back = swap(block, lines)

    for_up.third()
    for_attn.second()
    for_down.fourth()
    returned, small_back = clock.gate(returned, small_back)
    clock.tick(returned)
    for_attn.third()
    for_up.fourth()
    for_attn.fourth()
    returned = clock.gate(returned)
    placed = jnp.dot(take_both, returned, preferred_element_type=F32)
    placed = placed.astype(BF16)
    rows_out, grad_rows = placed[:row_count], placed[row_count:]
    sums = jnp.sum(small_back.astype(F32), axis=0)
    clock.tick(placed)
    (grad_w_down,) = for_down.done()
    (grad_w_up,) = for_up.done()
    grad_w_qkv, grad_w_out = for_attn.done()

    mine = lax.dynamic_slice_in_dim(sums[:8], spot * share, share, axis=1)
    grad_bq, grad_bv, grad_bo, grad_g1, grad_s1, grad_bd, grad_g2, grad_s2 = mine
    bias_width = hidden // devices
    grad_bu = lax.dynamic_slice_in_dim(
        sums[8], (grid.me % bias_groups) * bias_width, bias_width, axis=0
    )
    return (
        rows_out.reshape(row_count, 1, width),
        grad_rows.reshape(row_count, 1, width),
        grad_w_qkv,
        grad_bq,
        grad_bv,
        grad_w_out,
        grad_bo,
        grad_g1,
        grad_s1,
        grad_w_up,
        grad_bu,
        grad_w_down,
        grad_bd,
        grad_g2,
        grad_s2,
    )


def solution(mesh):
    n_dp, n_z = mesh.shape["dp"], mesh.shape["fsdp"]
    rows, vec, mat = P(None, AXES, None), P(AXES), P(AXES, None)

    def run(*args):
        return on_device(n_dp, n_z, *args)

    return jax.shard_map(
        run,
        mesh=mesh,
        in_specs=(rows, rows, P(), P())
        + (mat, vec, vec, mat, vec, vec, vec, mat, vec, mat, vec, vec, vec),
        out_specs=(rows, rows, mat, vec, vec, mat, vec, vec, vec, mat, vec, mat, vec, vec, vec),
        check_vma=False,
    )
```

```python
import jax
import jax.numpy as jnp
from jax import lax
from jax.experimental import pallas as pl
from jax.experimental.pallas import tpu as pltpu
from jax.sharding import PartitionSpec as P

HEADS = 16
HEAD_DIM = 64
EPSILON = 1e-05
AXES = ("dp", "fsdp")
BF16 = jnp.bfloat16
F32 = jnp.float32


class Grid:
    def __init__(self, n_dp, n_z):
        self.n_dp, self.n_z = n_dp, n_z
        side = 1
        while side * side * 2 < n_dp:
            side *= 2
        self.nx, self.ny = side, n_dp // (2 * side)
        self.x_masks = [2 * k for k in range(1, self.nx)]
        self.y_masks = [2 * side * k for k in range(1, self.ny)]
        self.z_masks = list(range(1, n_z))
        self.square = self.nx == self.ny == 2 and n_z == 4

    def bind(self):
        self.my_dp = lax.axis_index("dp").astype(jnp.int32)
        self.my_z = lax.axis_index("fsdp").astype(jnp.int32)
        self.me = lax.axis_index(AXES).astype(jnp.int32)

    def over_dp(self, value, mask):
        return lax.ppermute(value, "dp", [(i, i ^ mask) for i in range(self.n_dp)])

    def crossed(self, value, even_mask, odd_mask):
        pairs = [(i, i ^ (odd_mask if i % 2 else even_mask)) for i in range(self.n_dp)]
        return lax.ppermute(value, "dp", pairs)

    def over_z(self, value, mask):
        return lax.ppermute(value, "fsdp", [(i, i ^ mask) for i in range(self.n_z)])


class Clock:
    def __init__(self):
        self.last = ()

    def gate(self, *values):
        held = lax.optimization_barrier(tuple(values) + self.last)[: len(values)]
        return held if len(values) > 1 else held[0]

    def tick(self, *values):
        self.last = values


class Lines:
    def __init__(self, grid, clock, shards):
        self.grid, self.clock = grid, clock
        self.block = shards[0].shape[0]
        self.parts, blocks = [], []
        at = 0
        for shard in shards:
            height, cols = shard.shape
            count = height // self.block
            blocks += [shard[k * self.block : (k + 1) * self.block] for k in range(count)]
            self.parts.append((at, count, cols))
            at += count * cols
        self.shard = jnp.concatenate(blocks, axis=1) if len(blocks) > 1 else blocks[0]

    def step0(self):
        self.held = self.clock.gate(self.shard)
        self.far = [m for m in self.grid.z_masks if m % 2 == 0]
        self.coming = [self.grid.over_z(self.held, m) for m in self.far]

    def step1(self):
        *got, held = self.clock.gate(*self.coming, self.held)
        self.held = jnp.concatenate([held, *got], 0)
        self.clock.tick(self.held)
        self.coming = self.grid.over_z(self.held, 1)

    def step2(self):
        got, held = self.clock.gate(self.coming, self.held)
        z_marks = [0] + self.far
        z_marks += [m ^ 1 for m in z_marks]
        joined = []
        for at, count, cols in self.parts:
            cut = slice(at, at + count * cols)
            joined.append(jnp.concatenate([held[:, cut], got[:, cut]], 0))
        self.clock.tick(*joined)
        return [
            Gather(self.grid, self.clock, rows, z_marks, self.block, count, cols)
            for rows, (_, count, cols) in zip(joined, self.parts)
        ]


class Gather:
    def __init__(self, grid, clock, rows, z_marks, block, count, cols):
        self.grid, self.clock, self.rows = grid, clock, rows
        self.z_marks, self.block, self.count, self.cols = z_marks, block, count, cols
        self.pieces = []

    def take(self, rows, even_mask, odd_mask):
        self.pieces.append((rows, even_mask, odd_mask))
        self.crossing = (self.grid.over_dp(rows, 1), odd_mask ^ 1, even_mask ^ 1)

    def land(self, coming):
        rows, crossed = self.clock.gate(coming, self.crossing[0])
        self.pieces.append((crossed, *self.crossing[1:]))
        self.clock.tick(rows)
        return rows

    def step0(self):
        grid = self.grid
        (x,), (y,) = grid.x_masks, grid.y_masks
        rows = self.clock.gate(self.rows)
        self.first = grid.crossed(rows, x, y)
        self.second = grid.crossed(rows, y, x)
        self.take(rows, 0, 0)

    def step1(self):
        grid = self.grid
        (x,), (y,) = grid.x_masks, grid.y_masks
        first = self.land(self.first)
        self.third = grid.crossed(first, y, x)
        self.take(first, x, y)

    def step2(self):
        (x,), (y,) = self.grid.x_masks, self.grid.y_masks
        self.take(self.land(self.second), y, x)

    def step3(self):
        (x,), (y,) = self.grid.x_masks, self.grid.y_masks
        self.take(self.land(self.third), x ^ y, x ^ y)
        self.pieces.append(self.crossing)

    def done(self, cuts=()):
        grid, block, count = self.grid, self.block, self.count
        pieces, z_marks = self.pieces, self.z_marks
        owners = grid.n_dp * grid.n_z
        edges = [0, *cuts, self.cols]
        spans = list(zip(edges[:-1], edges[1:]))

        def kernel(me_ref, *refs):
            sources = refs[: len(pieces)]
            results = refs[len(pieces) : len(pieces) + len(spans)]
            sems = refs[-1]
            me = me_ref[0]
            odd = (me // grid.n_z) % 2 == 1
            for source, (_, even_mask, odd_mask) in zip(sources, pieces):
                mask = jnp.where(odd, jnp.int32(odd_mask), jnp.int32(even_mask))
                for at, z in enumerate(z_marks):
                    owner = lax.bitwise_xor(me, mask * grid.n_z + z)
                    for k in range(count):
                        to = pl.multiple_of((owner * count + k) * block, block)
                        for n, (result, (lo, hi)) in enumerate(zip(results, spans)):
                            pltpu.make_async_copy(
                                source.at[
                                    pl.ds(at * block, block), pl.ds(k * self.cols + lo, hi - lo)
                                ],
                                result.at[pl.ds(to, block)],
                                sems.at[n],
                            ).start()
            for n, result in enumerate(results):
                pltpu.make_async_copy(result, result, sems.at[n]).wait()

        arrays = self.clock.gate(*[v for v, _, _ in pieces])
        rows = owners * count * block
        full = pl.pallas_call(
            kernel,
            out_shape=[jax.ShapeDtypeStruct((rows, hi - lo), BF16) for lo, hi in spans],
            grid_spec=pltpu.PrefetchScalarGridSpec(
                num_scalar_prefetch=1,
                grid=(),
                in_specs=[pl.BlockSpec(memory_space=pl.ANY)] * len(pieces),
                out_specs=[pl.BlockSpec(memory_space=pltpu.VMEM)] * len(spans),
                scratch_shapes=[pltpu.SemaphoreType.DMA((len(spans),))],
            ),
            compiler_params=pltpu.CompilerParams(vmem_limit_bytes=10 << 20),
            cost_estimate=pl.CostEstimate(flops=0, bytes_accessed=0, transcendentals=0),
            name="assemble",
        )(grid.me.reshape(1), *arrays)
        self.clock.tick(*full)
        return full


class PlainLines:
    def __init__(self, grid, clock, shards):
        self.shards = shards

    def step0(self):
        pass

    step1 = step0

    def step2(self):
        return [PlainGather(v) for v in self.shards]


class PlainGather:
    def __init__(self, shard):
        self.full = lax.all_gather(shard, AXES, axis=0, tiled=True)

    def step0(self):
        pass

    step1 = step2 = step3 = step0

    def done(self, cuts=()):
        edges = [0, *cuts, self.full.shape[1]]
        return [self.full[:, lo:hi] for lo, hi in zip(edges[:-1], edges[1:])]


def make_lines(grid, clock, *shards):
    plain = shards[0].shape[0] % 16 or not grid.square
    kind = PlainLines if plain else Lines
    return kind(grid, clock, shards)


def contract_rows(left, right):
    return lax.dot_general(left, right, (((0,), (0,)), ((), ())), preferred_element_type=F32)


def back_dot(grad_rows, weight):
    return lax.dot_general(grad_rows, weight, (((1,), (1,)), ((), ())), preferred_element_type=F32)


def pick(array, index):
    return lax.dynamic_index_in_dim(array, index, 0, keepdims=False)


def total_of(base, parts):
    for part in parts:
        base = base + part.astype(F32)
    return base


class Scatter:
    places = 4

    def __init__(self, grid, clock, lefts, rights):
        self.grid, self.clock, self.lefts, self.rights = grid, clock, lefts, rights
        self.chunk = lefts[0].shape[1] // grid.n_dp
        self.cols = sum(right.shape[1] for right in rights)
        once = pl.Buffered(1)
        self.rows = [
            pl.BlockSpec(right.shape, lambda j, dp: (0, 0), pipeline_mode=once) for right in rights
        ]

    def call(self, other, ins, shapes, targets):
        tokens, count, places = self.lefts[0].shape[0], len(self.lefts), self.places
        added = len(ins)

        def place(j, dp):
            a, b = j // 2, j % 2
            odd = (dp[0] + other) % 2
            mask = jnp.where(odd == 1, 2 * a + 4 * b, 4 * a + 2 * b)
            return 0, lax.bitwise_xor(dp[0], mask + other)

        def kernel(dp_ref, *refs):
            lefts, rights, refs = refs[:count], refs[count : 2 * count], refs[2 * count :]
            gots, outs = refs[:added], refs[added : added + len(shapes)]
            blocks, out_sems, *fetched = refs[added + len(shapes) :]
            step = pl.program_id(0)

            def fetch(k):
                return pltpu.make_async_copy(gots[k], fetched[0].at[k], fetched[1].at[k])

            def put(k):
                return pltpu.make_async_copy(blocks.at[k], targets(outs)[k], out_sems.at[k])

            if added:

                @pl.when(step == 0)
                def _():
                    for k in range(places):
                        fetch(k).start()

            terms = [contract_rows(a[...], b[...]) for a, b in zip(lefts, rights)]
            term = jnp.concatenate(terms, axis=1) if count > 1 else terms[0]
            whole = term
            if added:
                for k in range(places):

                    @pl.when(step == k)
                    def _(k=k):
                        fetch(k).wait()

                whole = term + fetched[0][step].astype(F32)
            blocks[step] = whole.astype(BF16)
            for k in range(places):

                @pl.when(step == k)
                def _(k=k):
                    put(k).start()

            @pl.when(step == places - 1)
            def _():
                for k in range(places):
                    put(k).wait()

        anywhere = pl.BlockSpec(memory_space=pl.ANY)
        scratch = [
            pltpu.VMEM((places, self.chunk, self.cols), BF16),
            pltpu.SemaphoreType.DMA((places,)),
        ]
        ins = self.clock.gate(*self.lefts, *self.rights, *ins)
        return pl.pallas_call(
            kernel,
            out_shape=shapes,
            grid_spec=pltpu.PrefetchScalarGridSpec(
                num_scalar_prefetch=1,
                grid=(places,),
                in_specs=[
                    *[pl.BlockSpec((tokens, self.chunk), place) for _ in self.lefts],
                    *self.rows,
                    *[anywhere] * added,
                ],
                out_specs=[anywhere] * len(shapes),
                scratch_shapes=scratch * (2 if added else 1),
            ),
            compiler_params=pltpu.CompilerParams(vmem_limit_bytes=20 << 20),
            cost_estimate=pl.CostEstimate(flops=0, bytes_accessed=0, transcendentals=0),
            name="outer",
        )(self.grid.my_dp.reshape(1), *ins)

    def across(self):
        shapes = [jax.ShapeDtypeStruct((self.chunk, self.cols), BF16)] * self.places
        sends = self.call(1, (), shapes, lambda outs: outs)
        self.clock.tick(*sends)
        self.got = [self.grid.over_dp(v, 1) for v in sends]

    def first(self):
        grid = self.grid
        (x,), (y,) = grid.x_masks, grid.y_masks
        one = jax.ShapeDtypeStruct((self.chunk, self.cols), BF16)
        pair = jax.ShapeDtypeStruct((2, self.chunk, self.cols), BF16)
        keep, pass_on, far = self.call(
            0,
            self.got,
            [one, one, pair],
            lambda outs: (outs[0], outs[1], outs[2].at[0], outs[2].at[1]),
        )
        self.clock.tick(far)
        self.keep, self.pass_on = keep, pass_on
        self.got = grid.crossed(far, y, x)

    def second(self):
        (x,), (y,) = self.grid.x_masks, self.grid.y_masks
        got, pass_on = self.clock.gate(self.got, self.pass_on)
        send = (pass_on.astype(F32) + got[1].astype(F32)).astype(BF16)
        self.clock.tick(send)
        self.aside = got[0]
        self.got = self.grid.crossed(send, x, y)

    def land(self):
        self.got = self.clock.gate(self.got)
        self.clock.tick(self.got)

    def third(self):
        grid = self.grid
        got, keep = self.clock.gate(self.got, self.keep)
        lines = total_of(keep.astype(F32), [got, self.aside]).reshape(2, 2, -1, self.cols)
        odd = grid.my_z % 2
        send = lax.dynamic_index_in_dim(lines, 1 - odd, 1, keepdims=False).astype(BF16)
        self.keep = lax.dynamic_index_in_dim(lines, odd, 1, keepdims=False)
        self.clock.tick(send)
        self.got = grid.over_z(send, 1)

    def fourth(self):
        grid = self.grid
        got, keep = self.clock.gate(self.got, self.keep)
        held = keep + got.astype(F32)
        pair = grid.my_z // 2
        send = pick(held, 1 - pair).astype(BF16)
        self.keep = pick(held, pair)
        self.clock.tick(send)
        self.got = grid.over_z(send, 2)

    def done(self):
        got, keep = self.clock.gate(self.got, self.keep)
        outs, at = [], 0
        for right in self.rights:
            cut = slice(at, at + right.shape[1])
            outs.append(keep[:, cut] + got[:, cut].astype(F32))
            at += right.shape[1]
        self.clock.tick(*outs)
        return outs


class PlainScatter:
    def __init__(self, lefts, rights):
        self.terms = [contract_rows(a, b) for a, b in zip(lefts, rights)]

    def across(self):
        pass

    first = second = land = third = fourth = across

    def done(self):
        return [lax.psum_scatter(t, AXES, scatter_dimension=0, tiled=True) for t in self.terms]


def make_scatter(grid, clock, *pairs):
    lefts, rights = [a for a, _ in pairs], [b for _, b in pairs]
    if (lefts[0].shape[1] // grid.n_dp) % 128 or not grid.square:
        return PlainScatter(lefts, rights)
    return Scatter(grid, clock, lefts, rights)


def lookup(small_table, index_rows):
    matches = index_rows[:, None] == jnp.arange(small_table.shape[0], dtype=jnp.int32)[None, :]
    return jnp.sum(jnp.where(matches, small_table[None, :], 0), axis=1)


def rank_among(group_label, order_key):
    earlier = (group_label[None, :] == group_label[:, None]) & (
        order_key[None, :] < order_key[:, None]
    )
    return jnp.sum(earlier.astype(jnp.int32), axis=1)


def routing(lengths, deal_order, devices, row_count, device):
    slot_count = deal_order.shape[0]
    slot_ids = jnp.arange(slot_count, dtype=jnp.int32)
    starts = jnp.cumsum(lengths) - lengths
    slot_of = jnp.sum(
        jnp.where(deal_order[None, :] == slot_ids[:, None], slot_ids[None, :], 0), axis=1
    )
    slot_lengths = lookup(lengths, deal_order)
    local_rows = jnp.arange(row_count, dtype=jnp.int32)
    token_index = local_rows * devices + device
    sequence = jnp.sum((starts[None, :] <= token_index[:, None]).astype(jnp.int32), axis=1) - 1
    slot_index = lookup(slot_of, sequence)
    target = slot_index // 2
    send_rank = rank_among(target, local_rows)
    first_len = lax.dynamic_index_in_dim(slot_lengths, 2 * device, 0, False)
    second = local_rows >= first_len
    first_seq = lax.dynamic_index_in_dim(deal_order, 2 * device, 0, False)
    second_seq = lax.dynamic_index_in_dim(deal_order, 2 * device + 1, 0, False)
    sequence_here = jnp.where(second, second_seq, first_seq)
    position = local_rows - jnp.where(second, first_len, 0)
    source_token = lookup(starts, sequence_here) + position
    source = source_token % devices
    take_rank = rank_among(source, source_token)
    return target, send_rank, source, take_rank, first_len.reshape(1)


HEADS_AT_ONCE = 4
LANES = HEADS_AT_ONCE * HEAD_DIM


def head_probs(query, key, first_len):
    scores = back_dot(query, key)
    q_at = lax.broadcasted_iota(jnp.int32, scores.shape, 0)
    k_at = lax.broadcasted_iota(jnp.int32, scores.shape, 1)
    allowed = (k_at <= q_at) & ((q_at < first_len) | (k_at >= first_len))
    masked = jnp.where(allowed, scores, -1000000000.0)
    exps = jnp.exp(masked - jnp.max(masked, axis=-1, keepdims=True))
    return exps * (1.0 / jnp.sum(exps, axis=-1, keepdims=True))


def of_heads(rows, parts):
    head = lax.broadcasted_iota(jnp.int32, (rows, LANES), 1) // HEAD_DIM
    whole = parts[0]
    for k in range(1, len(parts)):
        whole = jnp.where(head == k, parts[k], whole)
    return whole


def one_head(values, k):
    head = lax.broadcasted_iota(jnp.int32, values.shape, 1) // HEAD_DIM
    return jnp.where(head == k, values, jnp.zeros((), BF16))


def attend(first_len, mixed_b):
    rows, width = mixed_b.shape[0], mixed_b.shape[1] // 3
    steps = width // LANES

    def kernel(first_ref, query, key, value, out):
        scaled = query[...] * jnp.asarray(HEAD_DIM**-0.5, BF16)
        probs = [
            head_probs(one_head(scaled, k), key[...], first_ref[0]).astype(BF16)
            for k in range(HEADS_AT_ONCE)
        ]
        found = [jnp.dot(p, value[...], preferred_element_type=F32) for p in probs]
        out[...] = of_heads(rows, found).astype(BF16)

    def part(k):
        return pl.BlockSpec((rows, LANES), lambda h, first: (0, k * steps + h))

    return pl.pallas_call(
        kernel,
        out_shape=jax.ShapeDtypeStruct((rows, width), BF16),
        grid_spec=pltpu.PrefetchScalarGridSpec(
            num_scalar_prefetch=1,
            grid=(steps,),
            in_specs=[part(0), part(1), part(2)],
            out_specs=part(0),
        ),
        compiler_params=pltpu.CompilerParams(vmem_limit_bytes=10 << 20),
        cost_estimate=pl.CostEstimate(flops=0, bytes_accessed=0, transcendentals=0),
        name="attend",
    )(first_len, mixed_b, mixed_b, mixed_b)


def attend_back(first_len, mixed_b, grad_att_b):
    rows, width = grad_att_b.shape
    steps = width // LANES

    def kernel(first_ref, query, key, value, grad, out, sums):
        h = pl.program_id(0)
        scaled = query[...] * jnp.asarray(HEAD_DIM**-0.5, BF16)
        to_query, to_key, to_value = [], [], []
        for k in range(HEADS_AT_ONCE):
            q, g = one_head(scaled, k), one_head(grad[...], k)
            probs = head_probs(q, key[...], first_ref[0])
            grad_probs = back_dot(g, value[...])
            dots = jnp.sum(probs * grad_probs, axis=-1, keepdims=True)
            grad_scores = (probs * (grad_probs - dots)).astype(BF16)
            to_query.append(jnp.dot(grad_scores, key[...], preferred_element_type=F32))
            to_key.append(contract_rows(grad_scores, q))
            to_value.append(contract_rows(probs.astype(BF16), g))
        results = (of_heads(rows, to_query) * HEAD_DIM**-0.5, sum(to_key), sum(to_value))
        for k, block in enumerate(results):
            block = block.astype(BF16)
            at = pl.multiple_of(k * width + h * LANES, LANES)
            out[:, pl.ds(at, LANES)] = block
            sums[:, pl.ds(at, LANES)] = jnp.sum(block.astype(F32), axis=0, keepdims=True)

    def part(k):
        return pl.BlockSpec((rows, LANES), lambda h, first: (0, k * steps + h))

    return pl.pallas_call(
        kernel,
        out_shape=[
            jax.ShapeDtypeStruct((rows, 3 * width), BF16),
            jax.ShapeDtypeStruct((1, 3 * width), F32),
        ],
        grid_spec=pltpu.PrefetchScalarGridSpec(
            num_scalar_prefetch=1,
            grid=(steps,),
            in_specs=[part(0), part(1), part(2), part(0)],
            out_specs=[
                pl.BlockSpec((rows, 3 * width), lambda h, first: (0, 0)),
                pl.BlockSpec((1, 3 * width), lambda h, first: (0, 0)),
            ],
        ),
        compiler_params=pltpu.CompilerParams(vmem_limit_bytes=16 << 20),
        cost_estimate=pl.CostEstimate(flops=0, bytes_accessed=0, transcendentals=0),
        name="attend_back",
    )(first_len, mixed_b, mixed_b, mixed_b, grad_att_b)


def gelu_back(grad_b, weight, slope):
    rows, width = grad_b.shape
    hidden = weight.shape[0]
    tile = min(1024, hidden)

    def kernel(grad, weight, slope, out, sums):
        block = (back_dot(grad[...], weight[...]) * slope[...]).astype(BF16)
        out[...] = block
        sums[...] = jnp.sum(block.astype(F32), axis=0, keepdims=True)

    return pl.pallas_call(
        kernel,
        out_shape=[
            jax.ShapeDtypeStruct((rows, hidden), BF16),
            jax.ShapeDtypeStruct((1, hidden), F32),
        ],
        grid=(hidden // tile,),
        in_specs=[
            pl.BlockSpec((rows, width), lambda j: (0, 0)),
            pl.BlockSpec((tile, width), lambda j: (j, 0)),
            pl.BlockSpec((rows, tile), lambda j: (0, j)),
        ],
        out_specs=[
            pl.BlockSpec((rows, tile), lambda j: (0, j)),
            pl.BlockSpec((1, tile), lambda j: (0, j)),
        ],
        compiler_params=pltpu.CompilerParams(vmem_limit_bytes=14 << 20),
        cost_estimate=pl.CostEstimate(flops=0, bytes_accessed=0, transcendentals=0),
        name="gelu_back",
    )(grad_b, weight, slope)


def in_hbm(array):
    return pltpu.with_memory_space_constraint(array, pltpu.HBM)


def norm_back(grad_b, weight, unit, gain, scale, passed, keep_wide):
    rows, depth = grad_b.shape
    width = weight.shape[0]
    tile = 1024
    steps = depth // tile

    def kernel(grad, weight, unit_at, gain, scale, passed_at, *refs):
        outs, (total, unit, passed, sems) = refs[:-4], refs[-4:]
        step = pl.program_id(0)
        fetches = [
            pltpu.make_async_copy(unit_at, unit, sems.at[0]),
            pltpu.make_async_copy(passed_at, passed, sems.at[1]),
        ]
        part = back_dot(grad[...], weight[...])

        @pl.when(step == 0)
        def _():
            for fetch in fetches:
                fetch.start()
            total[...] = part

        @pl.when(step > 0)
        def _():
            total[...] += part

        @pl.when(step == steps - 1)
        def _():
            for fetch in fetches:
                fetch.wait()
            whole, u = total[...], unit[...]
            normed = whole * gain[...]
            outs[1][0:1] = jnp.sum(whole * u, axis=0, keepdims=True)
            outs[1][1:2] = jnp.sum(whole, axis=0, keepdims=True)
            out = passed[...].astype(F32) + standardize_back(normed, u, scale[...])
            if keep_wide:
                total[...] = out
                store = pltpu.make_async_copy(total, outs[2], sems.at[2])
                store.start()
            out_b = out.astype(BF16)
            outs[0][...] = out_b
            outs[1][2:3] = jnp.sum(out_b.astype(F32), axis=0, keepdims=True)
            if keep_wide:
                store.wait()

    def once(shape):
        return pl.BlockSpec(shape, lambda j: (0, 0), pipeline_mode=pl.Buffered(1))

    anywhere = pl.BlockSpec(memory_space=pl.ANY)
    shapes = [((rows, width), BF16), ((8, width), F32)]
    out_specs = [once(shape) for shape, _ in shapes]
    if keep_wide:
        shapes.append(((rows, width), F32))
        out_specs.append(anywhere)
    return pl.pallas_call(
        kernel,
        out_shape=[jax.ShapeDtypeStruct(*s) for s in shapes],
        grid=(steps,),
        in_specs=[
            pl.BlockSpec((rows, tile), lambda j: (0, j)),
            pl.BlockSpec((width, tile), lambda j: (0, j)),
            anywhere,
            once((1, width)),
            once((rows, 1)),
            anywhere,
        ],
        out_specs=out_specs,
        scratch_shapes=[
            pltpu.VMEM((rows, width), F32),
            pltpu.VMEM((rows, width), unit.dtype),
            pltpu.VMEM((rows, width), passed.dtype),
            pltpu.SemaphoreType.DMA((3,)),
        ],
        compiler_params=pltpu.CompilerParams(vmem_limit_bytes=16 << 20),
        cost_estimate=pl.CostEstimate(flops=0, bytes_accessed=0, transcendentals=0),
        name="norm_back",
    )(grad_b, in_hbm(weight), in_hbm(unit), gain, scale, in_hbm(passed))


def standardize(values):
    centered = values - jnp.mean(values, axis=-1, keepdims=True)
    scale = lax.rsqrt(jnp.mean(centered * centered, axis=-1, keepdims=True) + EPSILON)
    return centered * scale, scale


def standardize_back(grad, unit, scale):
    return scale * (
        grad
        - jnp.mean(grad, axis=-1, keepdims=True)
        - unit * jnp.mean(grad * unit, axis=-1, keepdims=True)
    )


def col_sum(values):
    return jnp.sum(values.astype(F32), axis=0)


def on_device(
    n_dp,
    n_z,
    rows_in,
    cotangent,
    lengths,
    deal_order,
    w_qkv,
    b_query,
    b_value,
    w_out,
    b_out,
    gain_one,
    shift_one,
    w_up,
    b_up,
    w_down,
    b_down,
    gain_two,
    shift_two,
):
    grid = Grid(n_dp, n_z)
    grid.bind()
    clock = Clock()
    devices = n_dp * n_z
    row_count, _, width = rows_in.shape
    hidden = w_up.shape[1]
    share = width // devices

    early = make_lines(grid, clock, jnp.concatenate([w_qkv, w_out], axis=1))
    middle = make_lines(grid, clock, w_up)
    late = make_lines(grid, clock, w_down)
    early.step0()

    target, send_rank, source, take_rank, first_len = routing(
        lengths, deal_order, devices, row_count, grid.me
    )
    slot_rows = row_count // devices + 1
    in_rows = slot_rows
    out_rows = 2 * slot_rows

    def selector(owner, rank, block_rows):
        at = (owner * block_rows + rank)[:, None]
        slot_ids = jnp.arange(devices * block_rows, dtype=jnp.int32)[None, :]
        return (at == slot_ids).astype(BF16)

    to_slots = selector(target, send_rank, in_rows)
    from_slots = selector(source, take_rank, in_rows)

    def both_of(owner, rank):
        at = owner * out_rows + rank
        return jnp.concatenate([at, at + slot_rows])

    out_slot_ids = jnp.arange(devices * out_rows, dtype=jnp.int32)
    take_both = (both_of(target, send_rank)[:, None] == out_slot_ids[None, :]).astype(BF16)
    send_both = (out_slot_ids[:, None] == both_of(source, take_rank)[None, :]).astype(BF16)

    def swap(block, lines=None):
        block = block.reshape(devices, -1, 128)
        if lines is not None:
            block = jnp.concatenate([block, lines], axis=1)
        block = lax.all_to_all(block, AXES, split_axis=0, concat_axis=0, tiled=True)
        if lines is None:
            return block.reshape(-1, width)
        height = block.shape[1] - lines.shape[1]
        return block[:, :height].reshape(-1, width), block[:, height:]

    vectors = jnp.stack(
        [b_query, b_value, b_out, gain_one, shift_one, b_down, gain_two, shift_two]
    )
    groups = 128 // share
    spot = grid.me % groups
    at_spot = lax.broadcasted_iota(jnp.int32, (8, 128), 1) // share == spot
    vectors = jnp.where(at_spot, jnp.tile(vectors, (1, groups)), jnp.zeros((), BF16))
    bias_groups = max(1, 128 * devices // hidden)
    bias = jnp.tile(b_up[None, :], (1, bias_groups))
    at_bias = lax.broadcasted_iota(jnp.int32, (1, 128), 1) // b_up.shape[0]
    bias = jnp.where(at_bias == grid.me % bias_groups, bias, jnp.zeros((), BF16))
    bias = jnp.pad(bias, ((0, 7), (0, 0)))
    small = jnp.concatenate([vectors, bias], axis=0)
    early.step1()
    middle.step0()
    to_slots, own_rows = clock.gate(to_slots, rows_in)
    block = contract_rows(to_slots, own_rows.reshape(row_count, width))
    block = block.astype(BF16)
    clock.tick(block)
    (attn,) = early.step2()
    attn.step0()
    middle.step1()
    small = jnp.broadcast_to(small[None], (devices, *small.shape))
    arrived, small_all = swap(clock.gate(block), small)
    attn.step1()
    attn.step2()
    (up,) = middle.step2()
    up.step0()
    late.step0()
    attn.step3()
    arrived, small_all = clock.gate(arrived, small_all)
    inputs = jnp.dot(from_slots, arrived, preferred_element_type=F32)
    lines = jnp.sum(small_all[:, :8].astype(F32).reshape(-1, groups, 8, 128), axis=1)
    bq, bv, bo, g1, s1, bd, g2, s2 = [
        v[None, :] for v in jnp.swapaxes(lines, 0, 1).reshape(8, width)
    ]
    lines = jnp.sum(small_all[:, 8].astype(F32).reshape(-1, bias_groups, 128), axis=1)
    bu = lines.reshape(1, hidden)
    unit_one, scale_one = standardize(inputs)
    normed_one_b = (unit_one * g1 + s1).astype(BF16)
    clock.tick(normed_one_b)
    cot_block = contract_rows(to_slots, clock.gate(cotangent).reshape(row_count, width))
    cot_block = cot_block.astype(BF16)
    clock.tick(cot_block)
    arrived_cot = swap(cot_block)
    late.step1()
    take_both, send_both = clock.gate(take_both, send_both)
    clock.tick(take_both, send_both)
    up.step1()
    up.step2()
    (down,) = late.step2()
    down.step0()
    full_qkv, full_out = attn.done((3 * width,))
    mixed = jnp.dot(clock.gate(normed_one_b), full_qkv, preferred_element_type=F32)
    mixed_b = (mixed + jnp.concatenate([bq, jnp.zeros_like(bq), bv], axis=1)).astype(BF16)
    attended_b = attend(first_len, mixed_b)
    clock.tick(attended_b)
    arrived_cot = clock.gate(arrived_cot)
    grad_m_b = jnp.dot(from_slots, arrived_cot, preferred_element_type=F32)
    grad_m_b = grad_m_b.astype(BF16)
    clock.tick(grad_m_b)
    up.step3()
    attended_b = clock.gate(attended_b)
    hidden_one = inputs + jnp.dot(attended_b, full_out, preferred_element_type=F32) + bo
    unit_two, scale_two = standardize(hidden_one)
    normed_two_b = (unit_two * g2 + s2).astype(BF16)
    clock.tick(normed_two_b)

    (full_up,) = up.done()
    down.step1()
    down.step2()
    pre_act = jnp.dot(clock.gate(normed_two_b), full_up, preferred_element_type=F32) + bu
    half_cdf = 0.5 * (1.0 + lax.erf(pre_act * (0.5**0.5)))
    activation_b = (pre_act * half_cdf).astype(BF16)
    density = jnp.exp(-0.5 * pre_act * pre_act) * ((2.0 * jnp.pi) ** -0.5)
    slope = half_cdf + pre_act * density
    clock.tick(activation_b, slope)

    term_b_down = col_sum(grad_m_b)[None, :]
    for_down = make_scatter(grid, clock, (activation_b, grad_m_b))
    for_down.across()
    down.step3()
    (full_down,) = down.done()
    grad_pre_b, term_b_up = gelu_back(clock.gate(grad_m_b), full_down, slope)
    clock.tick(grad_pre_b)
    for_down.first()
    for_up = make_scatter(grid, clock, (normed_two_b, grad_pre_b))
    for_up.across()

    grad_branch_b, sums_two, grad_hidden = norm_back(
        clock.gate(grad_pre_b), full_up, unit_two, g2, scale_two, grad_m_b, True
    )
    clock.tick(grad_branch_b)
    for_up.first()
    grad_att_b = back_dot(clock.gate(grad_branch_b), full_out).astype(BF16)
    clock.tick(grad_att_b)
    grad_mixed_b, term_mixed = attend_back(first_len, mixed_b, clock.gate(grad_att_b))
    clock.tick(grad_mixed_b)
    for_attn = make_scatter(
        grid, clock, (normed_one_b, grad_mixed_b), (attended_b, grad_branch_b)
    )
    for_down.land()
    for_attn.across()
    for_down.second()

    grad_inputs_b, sums_one = norm_back(
        clock.gate(grad_mixed_b), full_qkv, unit_one, g1, scale_one, grad_hidden, False
    )
    clock.tick(grad_inputs_b)
    for_attn.first()
    for_up.second()
    for_down.third()
    result = jnp.dot(clock.gate(activation_b), full_down, preferred_element_type=F32)
    result_b = (hidden_one + result + bd).astype(BF16)
    term_mixed, sums_one, sums_two, term_b_down, term_b_up, result_b = clock.gate(
        term_mixed, sums_one, sums_two, term_b_down, term_b_up, result_b
    )
    terms = [term_mixed[:, :width], term_mixed[:, 2 * width :], sums_two[2:3], sums_one[:2]]
    terms = jnp.concatenate([*terms, term_b_down, sums_two[:2]], axis=0).astype(BF16)
    lines = jnp.swapaxes(terms.reshape(8, -1, 128), 0, 1)
    lines = jnp.repeat(lines, groups, axis=0)
    bias = jnp.repeat(term_b_up.astype(BF16).reshape(-1, 1, 128), bias_groups, axis=0)
    lines = jnp.concatenate([lines, jnp.pad(bias, ((0, 0), (0, 7), (0, 0)))], axis=1)
    both = jnp.concatenate([result_b, grad_inputs_b], axis=0)
    block = jnp.dot(send_both, both, preferred_element_type=F32)
    block = block.astype(BF16)
    clock.tick(block)
    returned, small_back = swap(block, lines)

    for_up.third()
    for_attn.second()
    for_down.fourth()
    returned, small_back = clock.gate(returned, small_back)
    clock.tick(returned)
    for_attn.third()
    for_up.fourth()
    for_attn.fourth()
    returned = clock.gate(returned)
    placed = jnp.dot(take_both, returned, preferred_element_type=F32)
    placed = placed.astype(BF16)
    rows_out, grad_rows = placed[:row_count], placed[row_count:]
    sums = jnp.sum(small_back.astype(F32), axis=0)
    clock.tick(placed)
    (grad_w_down,) = for_down.done()
    (grad_w_up,) = for_up.done()
    grad_w_qkv, grad_w_out = for_attn.done()

    mine = lax.dynamic_slice_in_dim(sums[:8], spot * share, share, axis=1)
    grad_bq, grad_bv, grad_bo, grad_g1, grad_s1, grad_bd, grad_g2, grad_s2 = mine
    bias_width = hidden // devices
    grad_bu = lax.dynamic_slice_in_dim(
        sums[8], (grid.me % bias_groups) * bias_width, bias_width, axis=0
    )
    return (
        rows_out.reshape(row_count, 1, width),
        grad_rows.reshape(row_count, 1, width),
        grad_w_qkv,
        grad_bq,
        grad_bv,
        grad_w_out,
        grad_bo,
        grad_g1,
        grad_s1,
        grad_w_up,
        grad_bu,
        grad_w_down,
        grad_bd,
        grad_g2,
        grad_s2,
    )


def solution(mesh):
    n_dp, n_z = mesh.shape["dp"], mesh.shape["fsdp"]
    rows, vec, mat = P(None, AXES, None), P(AXES), P(AXES, None)

    def run(*args):
        return on_device(n_dp, n_z, *args)

    return jax.shard_map(
        run,
        mesh=mesh,
        in_specs=(rows, rows, P(), P())
        + (mat, vec, vec, mat, vec, vec, vec, mat, vec, mat, vec, vec, vec),
        out_specs=(rows, rows, mat, vec, vec, mat, vec, vec, vec, mat, vec, mat, vec, vec, vec),
        check_vma=False,
    )
```

```python
import jax
import jax.numpy as jnp
from jax import lax
from jax.experimental import pallas as pl
from jax.experimental.pallas import tpu as pltpu
from jax.sharding import PartitionSpec as P

HEADS = 16
HEAD_DIM = 64
EPSILON = 1e-05
AXES = ("dp", "fsdp")
BF16 = jnp.bfloat16
F32 = jnp.float32


class Grid:
    def __init__(self, n_dp, n_z):
        self.n_dp, self.n_z = n_dp, n_z
        side = 1
        while side * side * 2 < n_dp:
            side *= 2
        self.nx, self.ny = side, n_dp // (2 * side)
        self.x_masks = [2 * k for k in range(1, self.nx)]
        self.y_masks = [2 * side * k for k in range(1, self.ny)]
        self.z_masks = list(range(1, n_z))
        self.square = self.nx == self.ny == 2 and n_z == 4

    def bind(self):
        self.my_dp = lax.axis_index("dp").astype(jnp.int32)
        self.my_z = lax.axis_index("fsdp").astype(jnp.int32)
        self.me = lax.axis_index(AXES).astype(jnp.int32)

    def over_dp(self, value, mask):
        return lax.ppermute(value, "dp", [(i, i ^ mask) for i in range(self.n_dp)])

    def crossed(self, value, even_mask, odd_mask):
        pairs = [(i, i ^ (odd_mask if i % 2 else even_mask)) for i in range(self.n_dp)]
        return lax.ppermute(value, "dp", pairs)

    def over_z(self, value, mask):
        return lax.ppermute(value, "fsdp", [(i, i ^ mask) for i in range(self.n_z)])


class Clock:
    def __init__(self):
        self.last = ()

    def gate(self, *values):
        held = lax.optimization_barrier(tuple(values) + self.last)[: len(values)]
        return held if len(values) > 1 else held[0]

    def tick(self, *values):
        self.last = values


class Lines:
    def __init__(self, grid, clock, shards):
        self.grid, self.clock = grid, clock
        self.block = shards[0].shape[0]
        self.parts, blocks = [], []
        at = 0
        for shard in shards:
            height, cols = shard.shape
            count = height // self.block
            blocks += [shard[k * self.block : (k + 1) * self.block] for k in range(count)]
            self.parts.append((at, count, cols))
            at += count * cols
        self.shard = jnp.concatenate(blocks, axis=1) if len(blocks) > 1 else blocks[0]

    def step0(self):
        self.held = self.clock.gate(self.shard)
        self.far = [m for m in self.grid.z_masks if m % 2 == 0]
        self.coming = [self.grid.over_z(self.held, m) for m in self.far]

    def step1(self):
        *got, held = self.clock.gate(*self.coming, self.held)
        self.held = jnp.concatenate([held, *got], 0)
        self.clock.tick(self.held)
        self.coming = self.grid.over_z(self.held, 1)

    def step2(self):
        got, held = self.clock.gate(self.coming, self.held)
        z_marks = [0] + self.far
        z_marks += [m ^ 1 for m in z_marks]
        joined = []
        for at, count, cols in self.parts:
            cut = slice(at, at + count * cols)
            joined.append(jnp.concatenate([held[:, cut], got[:, cut]], 0))
        self.clock.tick(*joined)
        return [
            Gather(self.grid, self.clock, rows, z_marks, self.block, count, cols)
            for rows, (_, count, cols) in zip(joined, self.parts)
        ]


class Gather:
    def __init__(self, grid, clock, rows, z_marks, block, count, cols):
        self.grid, self.clock, self.rows = grid, clock, rows
        self.z_marks, self.block, self.count, self.cols = z_marks, block, count, cols
        self.pieces = []

    def take(self, rows, even_mask, odd_mask):
        self.pieces.append((rows, even_mask, odd_mask))
        self.crossing = (self.grid.over_dp(rows, 1), odd_mask ^ 1, even_mask ^ 1)

    def land(self, coming):
        rows, crossed = self.clock.gate(coming, self.crossing[0])
        self.pieces.append((crossed, *self.crossing[1:]))
        self.clock.tick(rows)
        return rows

    def step0(self):
        grid = self.grid
        (x,), (y,) = grid.x_masks, grid.y_masks
        rows = self.clock.gate(self.rows)
        self.first = grid.crossed(rows, x, y)
        self.second = grid.crossed(rows, y, x)
        self.take(rows, 0, 0)

    def step1(self):
        grid = self.grid
        (x,), (y,) = grid.x_masks, grid.y_masks
        first = self.land(self.first)
        self.third = grid.crossed(first, y, x)
        self.take(first, x, y)

    def step2(self):
        (x,), (y,) = self.grid.x_masks, self.grid.y_masks
        self.take(self.land(self.second), y, x)

    def step3(self):
        (x,), (y,) = self.grid.x_masks, self.grid.y_masks
        self.take(self.land(self.third), x ^ y, x ^ y)
        self.pieces.append(self.crossing)

    def done(self, cuts=()):
        grid, block, count = self.grid, self.block, self.count
        pieces, z_marks = self.pieces, self.z_marks
        owners = grid.n_dp * grid.n_z
        edges = [0, *cuts, self.cols]
        spans = list(zip(edges[:-1], edges[1:]))

        def kernel(me_ref, *refs):
            sources = refs[: len(pieces)]
            results = refs[len(pieces) : len(pieces) + len(spans)]
            sems = refs[-1]
            me = me_ref[0]
            odd = (me // grid.n_z) % 2 == 1
            for source, (_, even_mask, odd_mask) in zip(sources, pieces):
                mask = jnp.where(odd, jnp.int32(odd_mask), jnp.int32(even_mask))
                for at, z in enumerate(z_marks):
                    owner = lax.bitwise_xor(me, mask * grid.n_z + z)
                    for k in range(count):
                        to = pl.multiple_of((owner * count + k) * block, block)
                        for n, (result, (lo, hi)) in enumerate(zip(results, spans)):
                            pltpu.make_async_copy(
                                source.at[
                                    pl.ds(at * block, block), pl.ds(k * self.cols + lo, hi - lo)
                                ],
                                result.at[pl.ds(to, block)],
                                sems.at[n],
                            ).start()
            for n, result in enumerate(results):
                pltpu.make_async_copy(result, result, sems.at[n]).wait()

        arrays = self.clock.gate(*[v for v, _, _ in pieces])
        rows = owners * count * block
        full = pl.pallas_call(
            kernel,
            out_shape=[jax.ShapeDtypeStruct((rows, hi - lo), BF16) for lo, hi in spans],
            grid_spec=pltpu.PrefetchScalarGridSpec(
                num_scalar_prefetch=1,
                grid=(),
                in_specs=[pl.BlockSpec(memory_space=pl.ANY)] * len(pieces),
                out_specs=[pl.BlockSpec(memory_space=pltpu.VMEM)] * len(spans),
                scratch_shapes=[pltpu.SemaphoreType.DMA((len(spans),))],
            ),
            compiler_params=pltpu.CompilerParams(vmem_limit_bytes=10 << 20),
            cost_estimate=pl.CostEstimate(flops=0, bytes_accessed=0, transcendentals=0),
            name="assemble",
        )(grid.me.reshape(1), *arrays)
        self.clock.tick(*full)
        return full


class PlainLines:
    def __init__(self, grid, clock, shards):
        self.shards = shards

    def step0(self):
        pass

    step1 = step0

    def step2(self):
        return [PlainGather(v) for v in self.shards]


class PlainGather:
    def __init__(self, shard):
        self.full = lax.all_gather(shard, AXES, axis=0, tiled=True)

    def step0(self):
        pass

    step1 = step2 = step3 = step0

    def done(self, cuts=()):
        edges = [0, *cuts, self.full.shape[1]]
        return [self.full[:, lo:hi] for lo, hi in zip(edges[:-1], edges[1:])]


def make_lines(grid, clock, *shards):
    plain = shards[0].shape[0] % 16 or not grid.square
    kind = PlainLines if plain else Lines
    return kind(grid, clock, shards)


def contract_rows(left, right):
    return lax.dot_general(left, right, (((0,), (0,)), ((), ())), preferred_element_type=F32)


def back_dot(grad_rows, weight):
    return lax.dot_general(grad_rows, weight, (((1,), (1,)), ((), ())), preferred_element_type=F32)


def pick(array, index):
    return lax.dynamic_index_in_dim(array, index, 0, keepdims=False)


def total_of(base, parts):
    for part in parts:
        base = base + part.astype(F32)
    return base


class Scatter:
    places = 4

    def __init__(self, grid, clock, lefts, rights):
        self.grid, self.clock, self.lefts, self.rights = grid, clock, lefts, rights
        self.chunk = lefts[0].shape[1] // grid.n_dp
        self.cols = sum(right.shape[1] for right in rights)
        once = pl.Buffered(1)
        self.rows = [
            pl.BlockSpec(right.shape, lambda j, dp: (0, 0), pipeline_mode=once) for right in rights
        ]

    def call(self, other, ins, shapes, targets):
        tokens, count, places = self.lefts[0].shape[0], len(self.lefts), self.places
        added = len(ins)

        def place(j, dp):
            a, b = j // 2, j % 2
            odd = (dp[0] + other) % 2
            mask = jnp.where(odd == 1, 2 * a + 4 * b, 4 * a + 2 * b)
            return 0, lax.bitwise_xor(dp[0], mask + other)

        def kernel(dp_ref, *refs):
            lefts, rights, refs = refs[:count], refs[count : 2 * count], refs[2 * count :]
            gots, outs = refs[:added], refs[added : added + len(shapes)]
            blocks, out_sems, *fetched = refs[added + len(shapes) :]
            step = pl.program_id(0)

            def fetch(k):
                return pltpu.make_async_copy(gots[k], fetched[0].at[k], fetched[1].at[k])

            def put(k):
                return pltpu.make_async_copy(blocks.at[k], targets(outs)[k], out_sems.at[k])

            if added:

                @pl.when(step == 0)
                def _():
                    for k in range(places):
                        fetch(k).start()

            terms = [contract_rows(a[...], b[...]) for a, b in zip(lefts, rights)]
            term = jnp.concatenate(terms, axis=1) if count > 1 else terms[0]
            whole = term
            if added:
                for k in range(places):

                    @pl.when(step == k)
                    def _(k=k):
                        fetch(k).wait()

                whole = term + fetched[0][step].astype(F32)
            blocks[step] = whole.astype(BF16)
            for k in range(places):

                @pl.when(step == k)
                def _(k=k):
                    put(k).start()

            @pl.when(step == places - 1)
            def _():
                for k in range(places):
                    put(k).wait()

        anywhere = pl.BlockSpec(memory_space=pl.ANY)
        scratch = [
            pltpu.VMEM((places, self.chunk, self.cols), BF16),
            pltpu.SemaphoreType.DMA((places,)),
        ]
        ins = self.clock.gate(*self.lefts, *self.rights, *ins)
        return pl.pallas_call(
            kernel,
            out_shape=shapes,
            grid_spec=pltpu.PrefetchScalarGridSpec(
                num_scalar_prefetch=1,
                grid=(places,),
                in_specs=[
                    *[pl.BlockSpec((tokens, self.chunk), place) for _ in self.lefts],
                    *self.rows,
                    *[anywhere] * added,
                ],
                out_specs=[anywhere] * len(shapes),
                scratch_shapes=scratch * (2 if added else 1),
            ),
            compiler_params=pltpu.CompilerParams(vmem_limit_bytes=20 << 20),
            cost_estimate=pl.CostEstimate(flops=0, bytes_accessed=0, transcendentals=0),
            name="outer",
        )(self.grid.my_dp.reshape(1), *ins)

    def across(self):
        shapes = [jax.ShapeDtypeStruct((self.chunk, self.cols), BF16)] * self.places
        sends = self.call(1, (), shapes, lambda outs: outs)
        self.clock.tick(*sends)
        self.got = [self.grid.over_dp(v, 1) for v in sends]

    def first(self):
        grid = self.grid
        (x,), (y,) = grid.x_masks, grid.y_masks
        one = jax.ShapeDtypeStruct((self.chunk, self.cols), BF16)
        pair = jax.ShapeDtypeStruct((2, self.chunk, self.cols), BF16)
        keep, pass_on, far = self.call(
            0,
            self.got,
            [one, one, pair],
            lambda outs: (outs[0], outs[1], outs[2].at[0], outs[2].at[1]),
        )
        self.clock.tick(far)
        self.keep, self.pass_on = keep, pass_on
        self.got = grid.crossed(far, y, x)

    def second(self):
        (x,), (y,) = self.grid.x_masks, self.grid.y_masks
        got, pass_on = self.clock.gate(self.got, self.pass_on)
        send = (pass_on.astype(F32) + got[1].astype(F32)).astype(BF16)
        self.clock.tick(send)
        self.aside = got[0]
        self.got = self.grid.crossed(send, x, y)

    def land(self):
        self.got = self.clock.gate(self.got)
        self.clock.tick(self.got)

    def third(self):
        grid = self.grid
        got, keep = self.clock.gate(self.got, self.keep)
        lines = total_of(keep.astype(F32), [got, self.aside]).reshape(2, 2, -1, self.cols)
        odd = grid.my_z % 2
        send = lax.dynamic_index_in_dim(lines, 1 - odd, 1, keepdims=False).astype(BF16)
        self.keep = lax.dynamic_index_in_dim(lines, odd, 1, keepdims=False)
        self.clock.tick(send)
        self.got = grid.over_z(send, 1)

    def fourth(self):
        grid = self.grid
        got, keep = self.clock.gate(self.got, self.keep)
        held = keep + got.astype(F32)
        pair = grid.my_z // 2
        send = pick(held, 1 - pair).astype(BF16)
        self.keep = pick(held, pair)
        self.clock.tick(send)
        self.got = grid.over_z(send, 2)

    def done(self):
        got, keep = self.clock.gate(self.got, self.keep)
        outs, at = [], 0
        for right in self.rights:
            cut = slice(at, at + right.shape[1])
            outs.append(keep[:, cut] + got[:, cut].astype(F32))
            at += right.shape[1]
        self.clock.tick(*outs)
        return outs


class PlainScatter:
    def __init__(self, lefts, rights):
        self.terms = [contract_rows(a, b) for a, b in zip(lefts, rights)]

    def across(self):
        pass

    first = second = land = third = fourth = across

    def done(self):
        return [lax.psum_scatter(t, AXES, scatter_dimension=0, tiled=True) for t in self.terms]


def make_scatter(grid, clock, *pairs):
    lefts, rights = [a for a, _ in pairs], [b for _, b in pairs]
    if (lefts[0].shape[1] // grid.n_dp) % 128 or not grid.square:
        return PlainScatter(lefts, rights)
    return Scatter(grid, clock, lefts, rights)


def lookup(small_table, index_rows):
    matches = index_rows[:, None] == jnp.arange(small_table.shape[0], dtype=jnp.int32)[None, :]
    return jnp.sum(jnp.where(matches, small_table[None, :], 0), axis=1)


def rank_among(group_label, order_key):
    earlier = (group_label[None, :] == group_label[:, None]) & (
        order_key[None, :] < order_key[:, None]
    )
    return jnp.sum(earlier.astype(jnp.int32), axis=1)


def routing(lengths, deal_order, devices, row_count, device):
    slot_count = deal_order.shape[0]
    slot_ids = jnp.arange(slot_count, dtype=jnp.int32)
    starts = jnp.cumsum(lengths) - lengths
    slot_of = jnp.sum(
        jnp.where(deal_order[None, :] == slot_ids[:, None], slot_ids[None, :], 0), axis=1
    )
    slot_lengths = lookup(lengths, deal_order)
    local_rows = jnp.arange(row_count, dtype=jnp.int32)
    token_index = local_rows * devices + device
    sequence = jnp.sum((starts[None, :] <= token_index[:, None]).astype(jnp.int32), axis=1) - 1
    slot_index = lookup(slot_of, sequence)
    target = slot_index // 2
    send_rank = rank_among(target, local_rows)
    first_len = lax.dynamic_index_in_dim(slot_lengths, 2 * device, 0, False)
    second = local_rows >= first_len
    first_seq = lax.dynamic_index_in_dim(deal_order, 2 * device, 0, False)
    second_seq = lax.dynamic_index_in_dim(deal_order, 2 * device + 1, 0, False)
    sequence_here = jnp.where(second, second_seq, first_seq)
    position = local_rows - jnp.where(second, first_len, 0)
    source_token = lookup(starts, sequence_here) + position
    source = source_token % devices
    take_rank = rank_among(source, source_token)
    return target, send_rank, source, take_rank, first_len.reshape(1)


HEADS_AT_ONCE = 4
LANES = HEADS_AT_ONCE * HEAD_DIM


def head_probs(query, key, first_len):
    scores = back_dot(query, key)
    q_at = lax.broadcasted_iota(jnp.int32, scores.shape, 0)
    k_at = lax.broadcasted_iota(jnp.int32, scores.shape, 1)
    allowed = (k_at <= q_at) & ((q_at < first_len) | (k_at >= first_len))
    masked = jnp.where(allowed, scores, -1000000000.0)
    exps = jnp.exp(masked - jnp.max(masked, axis=-1, keepdims=True))
    return exps * (1.0 / jnp.sum(exps, axis=-1, keepdims=True))


def of_heads(rows, parts):
    head = lax.broadcasted_iota(jnp.int32, (rows, LANES), 1) // HEAD_DIM
    whole = parts[0]
    for k in range(1, len(parts)):
        whole = jnp.where(head == k, parts[k], whole)
    return whole


def one_head(values, k):
    head = lax.broadcasted_iota(jnp.int32, values.shape, 1) // HEAD_DIM
    return jnp.where(head == k, values, jnp.zeros((), BF16))


def attend(first_len, mixed_b):
    rows, width = mixed_b.shape[0], mixed_b.shape[1] // 3
    steps = width // LANES

    def kernel(first_ref, query, key, value, out):
        scaled = query[...] * jnp.asarray(HEAD_DIM**-0.5, BF16)
        probs = [
            head_probs(one_head(scaled, k), key[...], first_ref[0]).astype(BF16)
            for k in range(HEADS_AT_ONCE)
        ]
        found = [jnp.dot(p, value[...], preferred_element_type=F32) for p in probs]
        out[...] = of_heads(rows, found).astype(BF16)

    def part(k):
        return pl.BlockSpec((rows, LANES), lambda h, first: (0, k * steps + h))

    return pl.pallas_call(
        kernel,
        out_shape=jax.ShapeDtypeStruct((rows, width), BF16),
        grid_spec=pltpu.PrefetchScalarGridSpec(
            num_scalar_prefetch=1,
            grid=(steps,),
            in_specs=[part(0), part(1), part(2)],
            out_specs=part(0),
        ),
        compiler_params=pltpu.CompilerParams(vmem_limit_bytes=10 << 20),
        cost_estimate=pl.CostEstimate(flops=0, bytes_accessed=0, transcendentals=0),
        name="attend",
    )(first_len, mixed_b, mixed_b, mixed_b)


def attend_back(first_len, mixed_b, grad_att_b):
    rows, width = grad_att_b.shape
    steps = width // LANES

    def kernel(first_ref, query, key, value, grad, out, sums):
        h = pl.program_id(0)
        scaled = query[...] * jnp.asarray(HEAD_DIM**-0.5, BF16)
        to_query, to_key, to_value = [], [], []
        for k in range(HEADS_AT_ONCE):
            q, g = one_head(scaled, k), one_head(grad[...], k)
            probs = head_probs(q, key[...], first_ref[0])
            grad_probs = back_dot(g, value[...])
            dots = jnp.sum(probs * grad_probs, axis=-1, keepdims=True)
            grad_scores = (probs * (grad_probs - dots)).astype(BF16)
            to_query.append(jnp.dot(grad_scores, key[...], preferred_element_type=F32))
            to_key.append(contract_rows(grad_scores, q))
            to_value.append(contract_rows(probs.astype(BF16), g))
        results = (of_heads(rows, to_query) * HEAD_DIM**-0.5, sum(to_key), sum(to_value))
        for k, block in enumerate(results):
            block = block.astype(BF16)
            at = pl.multiple_of(k * width + h * LANES, LANES)
            out[:, pl.ds(at, LANES)] = block
            sums[:, pl.ds(at, LANES)] = jnp.sum(block.astype(F32), axis=0, keepdims=True)

    def part(k):
        return pl.BlockSpec((rows, LANES), lambda h, first: (0, k * steps + h))

    return pl.pallas_call(
        kernel,
        out_shape=[
            jax.ShapeDtypeStruct((rows, 3 * width), BF16),
            jax.ShapeDtypeStruct((1, 3 * width), F32),
        ],
        grid_spec=pltpu.PrefetchScalarGridSpec(
            num_scalar_prefetch=1,
            grid=(steps,),
            in_specs=[part(0), part(1), part(2), part(0)],
            out_specs=[
                pl.BlockSpec((rows, 3 * width), lambda h, first: (0, 0)),
                pl.BlockSpec((1, 3 * width), lambda h, first: (0, 0)),
            ],
        ),
        compiler_params=pltpu.CompilerParams(vmem_limit_bytes=16 << 20),
        cost_estimate=pl.CostEstimate(flops=0, bytes_accessed=0, transcendentals=0),
        name="attend_back",
    )(first_len, mixed_b, mixed_b, mixed_b, grad_att_b)


def gelu_back(grad_b, weight, slope):
    rows, width = grad_b.shape
    hidden = weight.shape[0]
    tile = min(1024, hidden)

    def kernel(grad, weight, slope, out, sums):
        block = (back_dot(grad[...], weight[...]) * slope[...]).astype(BF16)
        out[...] = block
        sums[...] = jnp.sum(block.astype(F32), axis=0, keepdims=True)

    return pl.pallas_call(
        kernel,
        out_shape=[
            jax.ShapeDtypeStruct((rows, hidden), BF16),
            jax.ShapeDtypeStruct((1, hidden), F32),
        ],
        grid=(hidden // tile,),
        in_specs=[
            pl.BlockSpec((rows, width), lambda j: (0, 0)),
            pl.BlockSpec((tile, width), lambda j: (j, 0)),
            pl.BlockSpec((rows, tile), lambda j: (0, j)),
        ],
        out_specs=[
            pl.BlockSpec((rows, tile), lambda j: (0, j)),
            pl.BlockSpec((1, tile), lambda j: (0, j)),
        ],
        compiler_params=pltpu.CompilerParams(vmem_limit_bytes=14 << 20),
        cost_estimate=pl.CostEstimate(flops=0, bytes_accessed=0, transcendentals=0),
        name="gelu_back",
    )(grad_b, weight, slope)


def in_hbm(array):
    return pltpu.with_memory_space_constraint(array, pltpu.HBM)


def norm_back(grad_b, weight, unit, gain, scale, passed, keep_wide):
    rows, depth = grad_b.shape
    width = weight.shape[0]
    tile = 1024
    steps = depth // tile

    def kernel(grad, weight, unit_at, gain, scale, passed_at, *refs):
        outs, (total, unit, passed, sems) = refs[:-4], refs[-4:]
        step = pl.program_id(0)
        fetches = [
            pltpu.make_async_copy(unit_at, unit, sems.at[0]),
            pltpu.make_async_copy(passed_at, passed, sems.at[1]),
        ]
        part = back_dot(grad[...], weight[...])

        @pl.when(step == 0)
        def _():
            for fetch in fetches:
                fetch.start()
            total[...] = part

        @pl.when(step > 0)
        def _():
            total[...] += part

        @pl.when(step == steps - 1)
        def _():
            for fetch in fetches:
                fetch.wait()
            whole, u = total[...], unit[...]
            normed = whole * gain[...]
            outs[1][0:1] = jnp.sum(whole * u, axis=0, keepdims=True)
            outs[1][1:2] = jnp.sum(whole, axis=0, keepdims=True)
            out = passed[...].astype(F32) + standardize_back(normed, u, scale[...])
            if keep_wide:
                total[...] = out
                store = pltpu.make_async_copy(total, outs[2], sems.at[2])
                store.start()
            out_b = out.astype(BF16)
            outs[0][...] = out_b
            outs[1][2:3] = jnp.sum(out_b.astype(F32), axis=0, keepdims=True)
            if keep_wide:
                store.wait()

    def once(shape):
        return pl.BlockSpec(shape, lambda j: (0, 0), pipeline_mode=pl.Buffered(1))

    anywhere = pl.BlockSpec(memory_space=pl.ANY)
    shapes = [((rows, width), BF16), ((8, width), F32)]
    out_specs = [once(shape) for shape, _ in shapes]
    if keep_wide:
        shapes.append(((rows, width), F32))
        out_specs.append(anywhere)
    return pl.pallas_call(
        kernel,
        out_shape=[jax.ShapeDtypeStruct(*s) for s in shapes],
        grid=(steps,),
        in_specs=[
            pl.BlockSpec((rows, tile), lambda j: (0, j)),
            pl.BlockSpec((width, tile), lambda j: (0, j)),
            anywhere,
            once((1, width)),
            once((rows, 1)),
            anywhere,
        ],
        out_specs=out_specs,
        scratch_shapes=[
            pltpu.VMEM((rows, width), F32),
            pltpu.VMEM((rows, width), unit.dtype),
            pltpu.VMEM((rows, width), passed.dtype),
            pltpu.SemaphoreType.DMA((3,)),
        ],
        compiler_params=pltpu.CompilerParams(vmem_limit_bytes=16 << 20),
        cost_estimate=pl.CostEstimate(flops=0, bytes_accessed=0, transcendentals=0),
        name="norm_back",
    )(grad_b, in_hbm(weight), in_hbm(unit), gain, scale, in_hbm(passed))


def standardize(values):
    centered = values - jnp.mean(values, axis=-1, keepdims=True)
    scale = lax.rsqrt(jnp.mean(centered * centered, axis=-1, keepdims=True) + EPSILON)
    return centered * scale, scale


def standardize_back(grad, unit, scale):
    return scale * (
        grad
        - jnp.mean(grad, axis=-1, keepdims=True)
        - unit * jnp.mean(grad * unit, axis=-1, keepdims=True)
    )


def col_sum(values):
    return jnp.sum(values.astype(F32), axis=0)


def on_device(
    n_dp,
    n_z,
    rows_in,
    cotangent,
    lengths,
    deal_order,
    w_qkv,
    b_query,
    b_value,
    w_out,
    b_out,
    gain_one,
    shift_one,
    w_up,
    b_up,
    w_down,
    b_down,
    gain_two,
    shift_two,
):
    grid = Grid(n_dp, n_z)
    grid.bind()
    clock = Clock()
    devices = n_dp * n_z
    row_count, _, width = rows_in.shape
    hidden = w_up.shape[1]
    share = width // devices

    early = make_lines(grid, clock, jnp.concatenate([w_qkv, w_out], axis=1))
    middle = make_lines(grid, clock, w_up)
    late = make_lines(grid, clock, w_down)
    early.step0()

    target, send_rank, source, take_rank, first_len = routing(
        lengths, deal_order, devices, row_count, grid.me
    )
    slot_rows = row_count // devices + 1
    in_rows = slot_rows
    out_rows = 2 * slot_rows

    def selector(owner, rank, block_rows):
        at = (owner * block_rows + rank)[:, None]
        slot_ids = jnp.arange(devices * block_rows, dtype=jnp.int32)[None, :]
        return (at == slot_ids).astype(BF16)

    to_slots = selector(target, send_rank, in_rows)
    from_slots = selector(source, take_rank, in_rows)

    def both_of(owner, rank):
        at = owner * out_rows + rank
        return jnp.concatenate([at, at + slot_rows])

    out_slot_ids = jnp.arange(devices * out_rows, dtype=jnp.int32)
    take_both = (both_of(target, send_rank)[:, None] == out_slot_ids[None, :]).astype(BF16)
    send_both = (out_slot_ids[:, None] == both_of(source, take_rank)[None, :]).astype(BF16)

    def swap(block, lines=None):
        block = block.reshape(devices, -1, 128)
        if lines is not None:
            block = jnp.concatenate([block, lines], axis=1)
        block = lax.all_to_all(block, AXES, split_axis=0, concat_axis=0, tiled=True)
        if lines is None:
            return block.reshape(-1, width)
        height = block.shape[1] - lines.shape[1]
        return block[:, :height].reshape(-1, width), block[:, height:]

    vectors = jnp.stack(
        [b_query, b_value, b_out, gain_one, shift_one, b_down, gain_two, shift_two]
    )
    groups = 128 // share
    spot = grid.me % groups
    at_spot = lax.broadcasted_iota(jnp.int32, (8, 128), 1) // share == spot
    vectors = jnp.where(at_spot, jnp.tile(vectors, (1, groups)), jnp.zeros((), BF16))
    bias_groups = max(1, 128 * devices // hidden)
    bias = jnp.tile(b_up[None, :], (1, bias_groups))
    at_bias = lax.broadcasted_iota(jnp.int32, (1, 128), 1) // b_up.shape[0]
    bias = jnp.where(at_bias == grid.me % bias_groups, bias, jnp.zeros((), BF16))
    bias = jnp.pad(bias, ((0, 7), (0, 0)))
    small = jnp.concatenate([vectors, bias], axis=0)
    early.step1()
    middle.step0()
    to_slots, own_rows = clock.gate(to_slots, rows_in)
    block = contract_rows(to_slots, own_rows.reshape(row_count, width))
    block = block.astype(BF16)
    clock.tick(block)
    (attn,) = early.step2()
    attn.step0()
    middle.step1()
    small = jnp.broadcast_to(small[None], (devices, *small.shape))
    arrived, small_all = swap(clock.gate(block), small)
    attn.step1()
    attn.step2()
    (up,) = middle.step2()
    up.step0()
    late.step0()
    attn.step3()
    arrived, small_all = clock.gate(arrived, small_all)
    inputs = jnp.dot(from_slots, arrived, preferred_element_type=F32)
    lines = jnp.sum(small_all[:, :8].astype(F32).reshape(-1, groups, 8, 128), axis=1)
    bq, bv, bo, g1, s1, bd, g2, s2 = [
        v[None, :] for v in jnp.swapaxes(lines, 0, 1).reshape(8, width)
    ]
    lines = jnp.sum(small_all[:, 8].astype(F32).reshape(-1, bias_groups, 128), axis=1)
    bu = lines.reshape(1, hidden)
    unit_one, scale_one = standardize(inputs)
    normed_one_b = (unit_one * g1 + s1).astype(BF16)
    clock.tick(normed_one_b)
    cot_block = contract_rows(to_slots, clock.gate(cotangent).reshape(row_count, width))
    cot_block = cot_block.astype(BF16)
    clock.tick(cot_block)
    arrived_cot = swap(cot_block)
    late.step1()
    take_both, send_both = clock.gate(take_both, send_both)
    clock.tick(take_both, send_both)
    up.step1()
    up.step2()
    (down,) = late.step2()
    down.step0()
    full_qkv, full_out = attn.done((3 * width,))
    mixed = jnp.dot(clock.gate(normed_one_b), full_qkv, preferred_element_type=F32)
    mixed_b = (mixed + jnp.concatenate([bq, jnp.zeros_like(bq), bv], axis=1)).astype(BF16)
    attended_b = attend(first_len, mixed_b)
    clock.tick(attended_b)
    arrived_cot = clock.gate(arrived_cot)
    grad_m_b = jnp.dot(from_slots, arrived_cot, preferred_element_type=F32)
    grad_m_b = grad_m_b.astype(BF16)
    clock.tick(grad_m_b)
    up.step3()
    attended_b = clock.gate(attended_b)
    hidden_one = inputs + jnp.dot(attended_b, full_out, preferred_element_type=F32) + bo
    unit_two, scale_two = standardize(hidden_one)
    normed_two_b = (unit_two * g2 + s2).astype(BF16)
    clock.tick(normed_two_b)

    (full_up,) = up.done()
    down.step1()
    down.step2()
    pre_act = jnp.dot(clock.gate(normed_two_b), full_up, preferred_element_type=F32) + bu
    half_cdf = 0.5 * (1.0 + lax.erf(pre_act * (0.5**0.5)))
    activation_b = (pre_act * half_cdf).astype(BF16)
    density = jnp.exp(-0.5 * pre_act * pre_act) * ((2.0 * jnp.pi) ** -0.5)
    slope = half_cdf + pre_act * density
    clock.tick(activation_b, slope)

    term_b_down = col_sum(grad_m_b)[None, :]
    for_down = make_scatter(grid, clock, (activation_b, grad_m_b))
    for_down.across()
    down.step3()
    (full_down,) = down.done()
    grad_pre_b, term_b_up = gelu_back(clock.gate(grad_m_b), full_down, slope)
    clock.tick(grad_pre_b)
    for_down.first()
    for_up = make_scatter(grid, clock, (normed_two_b, grad_pre_b))
    for_up.across()

    grad_branch_b, sums_two, grad_hidden = norm_back(
        clock.gate(grad_pre_b), full_up, unit_two, g2, scale_two, grad_m_b, True
    )
    clock.tick(grad_branch_b)
    for_up.first()
    grad_att_b = back_dot(clock.gate(grad_branch_b), full_out).astype(BF16)
    clock.tick(grad_att_b)
    grad_mixed_b, term_mixed = attend_back(first_len, mixed_b, clock.gate(grad_att_b))
    clock.tick(grad_mixed_b)
    for_attn = make_scatter(
        grid, clock, (normed_one_b, grad_mixed_b), (attended_b, grad_branch_b)
    )
    for_down.land()
    for_attn.across()
    for_down.second()

    grad_inputs_b, sums_one = norm_back(
        clock.gate(grad_mixed_b), full_qkv, unit_one, g1, scale_one, grad_hidden, False
    )
    clock.tick(grad_inputs_b)
    for_attn.first()
    for_up.second()
    for_down.third()
    result = jnp.dot(clock.gate(activation_b), full_down, preferred_element_type=F32)
    result_b = (hidden_one + result + bd).astype(BF16)
    term_mixed, sums_one, sums_two, term_b_down, term_b_up, result_b = clock.gate(
        term_mixed, sums_one, sums_two, term_b_down, term_b_up, result_b
    )
    terms = [term_mixed[:, :width], term_mixed[:, 2 * width :], sums_two[2:3], sums_one[:2]]
    terms = jnp.concatenate([*terms, term_b_down, sums_two[:2]], axis=0).astype(BF16)
    lines = jnp.swapaxes(terms.reshape(8, -1, 128), 0, 1)
    lines = jnp.repeat(lines, groups, axis=0)
    bias = jnp.repeat(term_b_up.astype(BF16).reshape(-1, 1, 128), bias_groups, axis=0)
    lines = jnp.concatenate([lines, jnp.pad(bias, ((0, 0), (0, 7), (0, 0)))], axis=1)
    both = jnp.concatenate([result_b, grad_inputs_b], axis=0)
    block = jnp.dot(send_both, both, preferred_element_type=F32)
    block = block.astype(BF16)
    clock.tick(block)
    returned, small_back = swap(block, lines)

    for_up.third()
    for_attn.second()
    returned, small_back = clock.gate(returned, small_back)
    clock.tick(returned)
    for_attn.third()
    for_down.fourth()
    for_up.fourth()
    for_attn.fourth()
    returned = clock.gate(returned)
    placed = jnp.dot(take_both, returned, preferred_element_type=F32)
    placed = placed.astype(BF16)
    rows_out, grad_rows = placed[:row_count], placed[row_count:]
    sums = jnp.sum(small_back.astype(F32), axis=0)
    clock.tick(placed)
    (grad_w_down,) = for_down.done()
    (grad_w_up,) = for_up.done()
    grad_w_qkv, grad_w_out = for_attn.done()

    mine = lax.dynamic_slice_in_dim(sums[:8], spot * share, share, axis=1)
    grad_bq, grad_bv, grad_bo, grad_g1, grad_s1, grad_bd, grad_g2, grad_s2 = mine
    bias_width = hidden // devices
    grad_bu = lax.dynamic_slice_in_dim(
        sums[8], (grid.me % bias_groups) * bias_width, bias_width, axis=0
    )
    return (
        rows_out.reshape(row_count, 1, width),
        grad_rows.reshape(row_count, 1, width),
        grad_w_qkv,
        grad_bq,
        grad_bv,
        grad_w_out,
        grad_bo,
        grad_g1,
        grad_s1,
        grad_w_up,
        grad_bu,
        grad_w_down,
        grad_bd,
        grad_g2,
        grad_s2,
    )


def solution(mesh):
    n_dp, n_z = mesh.shape["dp"], mesh.shape["fsdp"]
    rows, vec, mat = P(None, AXES, None), P(AXES), P(AXES, None)

    def run(*args):
        return on_device(n_dp, n_z, *args)

    return jax.shard_map(
        run,
        mesh=mesh,
        in_specs=(rows, rows, P(), P())
        + (mat, vec, vec, mat, vec, vec, vec, mat, vec, mat, vec, vec, vec),
        out_specs=(rows, rows, mat, vec, vec, mat, vec, vec, vec, mat, vec, mat, vec, vec, vec),
        check_vma=False,
    )
```
